32 devices in a mesh: groups: 2 (over x), ep: 16 (over z, y, core).
Axes of the slice: x: 2, y: 2, z: 4, core: 2. Of those that a mesh axis runs over, the one named last changes fastest.
Arguments:
- states: float32 [2, 256, 2048], P(None, ('groups', 'ep')), parts along dimension 1, may hold values from -6 to 6
- attn_gain: float32 [2048], replicated, may hold values from 0.1 to 1.9
- moe_gain: float32 [2048], replicated, may hold values from 0.1 to 1.9
- w_query: bfloat16 [2048, 2048], P(None, 'ep'), may hold values from -11 to 11
- w_key: bfloat16 [2048, 256], P(None, 'ep'), may hold values from -0.125 to 0.125
- w_value: bfloat16 [2048, 256], P(None, 'ep'), may hold values from -0.125 to 0.125
- w_output: bfloat16 [2048, 2048], P('ep'), may hold values from -0.125 to 0.125
- w_gate_up: bfloat16 [16, 2048, 1536], P('ep'), may hold values from -0.125 to 0.125
- w_down: bfloat16 [16, 768, 2048], P('ep'), may hold values from -0.21875 to 0.21875
- key_cache: bfloat16 [64, 1024, 256], P(('groups', 'ep')), parts along dimension 0, may hold values from -60 to 60
- value_cache: bfloat16 [64, 1024, 256], P(('groups', 'ep')), parts along dimension 0, may hold values from -24 to 24
- cache_lengths: int32 [64], P(('groups', 'ep')), parts along dimension 0, may hold values from 1 to 1024, as said below
- prefix_slot: int32 [256], P(('groups', 'ep')), parts along dimension 0, may hold values from 0 to 1
- routes: int32 [256, 2, 8], P(('groups', 'ep')), parts along dimension 0, may hold values from 0 to 15, all different within a row; in each aligned block of 16 rows (0 to 15, 16 to 31, ..., all dimensions but the last counted through in order) at most 16 rows name the same one
- gate_weights: float32 [2, 256, 8], P(None, ('groups', 'ep')), parts along dimension 1, may hold values from 0.05 to 0.5
Outputs:
- layer_out: float32 [2, 256, 2048], P(None, ('groups', 'ep')), parts along dimension 1
- appended_kv: bfloat16 [2, 256, 512], P(None, ('groups', 'ep')), parts along dimension 1
The draws below stay inside these ranges and needn't reach their ends.
There are 2 independent parts, one for each index of `groups`. The reference program is written for one: setup_inputs(seed, part) draws one part's arguments, and reference() takes and returns one part's arrays. A program takes and returns all parts, laid end to end along the dimension named above; an argument that names none is the same for every part. Nothing has to cross between parts.
Inputs may be any that keep to these rules, and one draw needn't show every extreme that they name: `cache_lengths`: positions beyond a prefix's length are unused; some prefix is full at 1024. `routes`: over both steps together, the 8 branches of one ep device choose any one expert at most 16 times; a branch's 8 experts at one step differ.
All inputs are finite; a program needn't handle non-finite values.
Results may differ from the reference program's by a relative error of at most 0.0024.
The reference program's roundings to bfloat16 on the way count: a program that leaves them out, or rounds other values in their place, can miss the bound.
Values may be sent and summed in bfloat16 or wider, within the bound.
A program may use at most 128 MiB of HBM per device.

```python
import math
import jax
import jax.numpy as jnp
import numpy as np
from jax import lax

D = 2048
HQ = 16
KVH = 2
HD = 128
FF = 768
TOPK = 8
BR_DEV = 8
PREF_DEV = 2
CACHE = 1024
EXPERTS = 16
B = 128
PREFIXES = 32
CAP = 16
N_EP = 16


def draw_cache_lengths(key, part):
    lengths = jax.random.randint(key, (PREFIXES,), 1, CACHE + 1, dtype=jnp.int32)
    return lengths.at[0].set(CACHE)


def draw_w_query(key, part):
    base = jax.random.truncated_normal(key, -6.0, 6.0, (D, HQ * HD), jnp.float32) * D ** (-0.5)
    return base.astype(jnp.bfloat16)


def draw_key_cache(key, part):
    base = jax.random.truncated_normal(key, -6.0, 6.0, (PREFIXES, CACHE, KVH * HD), jnp.float32) * 1.5
    return base.astype(jnp.bfloat16)


def set_ends(drawn, own_key, least, high):
    longest = drawn.shape.index(max(drawn.shape))
    spots = []
    for shift in (0, 1):
        where = [jax.random.randint(jax.random.fold_in(own_key, axis), (), 0, length) for axis, length in enumerate(drawn.shape)]
        where[longest] = (where[longest] + shift) % drawn.shape[longest]
        spots.append(tuple(where))
    return drawn.at[spots[0]].set(least).at[spots[1]].set(high)


def block_levels(key, shape, cuts, low, high):
    factor_of, own = 1.0, jax.random.fold_in(key, 6)
    for axis_at, shards_of in cuts:
        heights = jnp.exp(jax.random.uniform(jax.random.fold_in(own, axis_at), (shards_of,), jnp.float32, low / len(cuts), high / len(cuts)))
        factor_of = factor_of * jnp.repeat(heights, shape[axis_at] // shards_of).reshape([-1 if axis == axis_at else 1 for axis in range(len(shape))])
    return factor_of


def assign_block(own_key, own, number, rows, number_of, top, most, slope):
    ranking = jax.random.permutation(own_key, number_of)
    heavy_load, ordinary = portions_of(number_of, rows * top, most, slope, True), portions_of(number_of, rows * top, most, slope, False)
    places = jnp.arange(number_of)

    def named(sizes, offset_by):
        used = int((sizes > 0).sum())
        fixed = max(1, used // 4)
        passed = fixed + (places - fixed + offset_by * (used - fixed)) % max(1, number_of - fixed)
        return jnp.zeros((number_of,), jnp.int32).at[ranking[jnp.where(places < fixed, places, passed)]].set(jnp.asarray(sizes, jnp.int32))

    sizes = jnp.where(number % 4 == 0, named(heavy_load, number // 4), named(ordinary, number - number // 4 - 1))
    mixed = jax.random.permutation(jax.random.fold_in(own, 3), number_of)
    giver, receiver = mixed[0:number_of // 2 * 2:2], mixed[1:number_of // 2 * 2:2]
    margin = jnp.minimum(sizes[giver] - 1, most - sizes[receiver]) // 2
    margin = jnp.where((giver == ranking[0]) | (receiver == ranking[0]) | (sizes[receiver] == 0), 0, jnp.maximum(margin, 0))
    passed = jax.random.randint(jax.random.fold_in(own, 4), (number_of // 2,), 0, 1 << 20) % (margin + 1)
    sizes = sizes.at[giver].add(-passed).at[receiver].add(passed)
    items = jnp.searchsorted(jnp.cumsum(sizes), jnp.arange(rows * top), side="right").astype(jnp.int32)
    listing = items.reshape(top, rows).T
    listing = listing[jax.random.permutation(jax.random.fold_in(own, 1), rows)]
    offset_by = jax.random.randint(jax.random.fold_in(own, 2), (rows, 1), 0, top)
    return jnp.take_along_axis(listing, (jnp.arange(top)[None, :] + offset_by) % top, axis=1)


def portions_of(amount, total, bound, slope, full):
    weights = [(1 << 20) // math.isqrt(rank ** slope) + 1 for rank in range(1, amount + 1)]
    largest = bound if full else min(bound, max(-(-total // amount), total * weights[0] // sum(weights)))
    least = 1 if total - largest >= amount - 1 else 0
    given, surplus = [largest] + [least] * (amount - 1), total - largest - least * (amount - 1)
    while surplus > 0:
        movable = [i for i in range(1, amount) if given[i] < largest] or [i for i in range(1, amount) if given[i] < bound]
        mass, left = sum([weights[i] for i in movable]), surplus
        for i in movable:
            addition = min(bound - given[i], max(1, left * weights[i] // mass), surplus)
            given[i] = given[i] + addition
            surplus = surplus - addition
    return np.array(given)


def scatter_about(own_key, dims, width, limit, cuts=(), kind=jnp.bfloat16):
    values = width * jax.random.normal(own_key, dims, jnp.float32)
    if cuts:
        values = values * block_levels(own_key, dims, cuts, -0.22, 0.18)
    return jnp.clip(values, -limit, limit).astype(kind)


def setup_inputs(seed: int = 0, part: int = 0) -> dict:
    key_list = jax.random.split(jax.random.key(seed), 16)
    own_keys = jax.random.split(jax.random.fold_in(key_list[15], part), 16)
    states = scatter_about(own_keys[0], (2, B, D), 1.0, 6.0, ((1, 16),), jnp.float32)
    attn_gain = jnp.clip(1.0 + 0.18 * jax.random.normal(key_list[1], (D,), jnp.float32), 0.1, 1.9)
    moe_gain = jnp.clip(1.0 + 0.18 * jax.random.normal(key_list[2], (D,), jnp.float32), 0.1, 1.9)
    w_query = draw_w_query(jax.random.fold_in(key_list[15], 71), part)
    w_key = scatter_about(key_list[4], (D, KVH * HD), D ** -0.5, 0.125, ((1, 16),))
    w_value = scatter_about(key_list[5], (D, KVH * HD), D ** -0.5, 0.125, ((1, 16),))
    w_output = scatter_about(key_list[6], (HQ * HD, D), (HQ * HD) ** -0.5, 0.125, ((0, 16),))
    w_gate_up = scatter_about(key_list[7], (EXPERTS, D, 2 * FF), D ** -0.5, 0.125, ((0, 16),))
    w_down = scatter_about(key_list[8], (EXPERTS, FF, D), FF ** -0.5, 0.21875, ((0, 16),))
    key_cache = draw_key_cache(jax.random.fold_in(jax.random.fold_in(key_list[15], part), 71), part)
    value_cache = scatter_about(own_keys[10], (PREFIXES, CACHE, KVH * HD), 4.0, 24.0, ((0, 16),))
    cache_lengths = draw_cache_lengths(jax.random.fold_in(jax.random.fold_in(key_list[15], part), 71), part)
    prefix_slot = set_ends(jax.random.randint(own_keys[12], (B,), 0, PREF_DEV), jax.random.fold_in(own_keys[12], 1), 0, PREF_DEV - 1).astype(jnp.int32)
    routes_keys = jax.random.split(jax.random.fold_in(own_keys[13], 1), B * 2 // (2 * BR_DEV))
    routes_turns = jax.random.permutation(jax.random.fold_in(own_keys[13], 3), B * 2 // (2 * BR_DEV))
    routes = jax.vmap(lambda own, number: assign_block(jax.random.fold_in(own_keys[13], 2), own, number, 2 * BR_DEV, EXPERTS, TOPK, CAP, 2))(routes_keys, routes_turns).reshape((B, 2, TOPK))
    gate_weights = jnp.clip(jnp.exp(math.log(0.5) - 2.3025851 * jax.random.uniform(own_keys[14], (2, B, TOPK), jnp.float32) ** block_levels(own_keys[14], (2, B, TOPK), ((1, 16),), -0.2, 0.2)), 0.05, 0.5)
    return {"states": states, "attn_gain": attn_gain, "moe_gain": moe_gain, "w_query": w_query, "w_key": w_key, "w_value": w_value, "w_output": w_output, "w_gate_up": w_gate_up, "w_down": w_down, "key_cache": key_cache, "value_cache": value_cache, "cache_lengths": cache_lengths, "prefix_slot": prefix_slot, "routes": routes, "gate_weights": gate_weights}


EPS = 1e-06
THETA = 1000000.0

def rms_scale(values, gain):
    squares = lax.optimization_barrier(jnp.mean(values * values, axis=-1, keepdims=True))
    return values * lax.rsqrt(squares + EPS) * gain

def rotate(vectors, positions):
    head_size = vectors.shape[-1]
    half_size = head_size // 2
    inverse_rate = THETA ** (-(jnp.arange(half_size).astype(jnp.float32) * 2.0 / head_size))
    phases = positions[..., None, None] * inverse_rate
    cosine = jnp.cos(phases)
    sine_part = jnp.sin(phases)
    first_half = vectors[..., :half_size]
    second_half = vectors[..., half_size:]
    return jnp.concatenate([first_half * cosine - second_half * sine_part, second_half * cosine + first_half * sine_part], axis=-1)

def attend_block(packed):
    queries, new_keys, new_values, key_block, value_block, lengths, slots = packed
    step_count, row_count, head_count, head_size = queries.shape
    prefix_count, cache_span, kv_heads, _ = key_block.shape
    group_size = head_count // kv_heads
    grouped = queries.reshape(step_count, row_count, kv_heads, group_size, head_size).astype(jnp.float32)
    inv_root = 1.0 / math.sqrt(head_size)
    far_scores = jnp.einsum('srkgd,pckd->srkgpc', grouped, key_block.astype(jnp.float32)) * inv_root
    visible = (jnp.arange(cache_span)[None, None, :] < lengths[None, :, None]) & (slots[:, None, None] == jnp.arange(prefix_count)[None, :, None])
    far_scores = jnp.where(visible[None, :, None, None], far_scores, -1e+30)
    own_scores = jnp.einsum('srkgd,trkd->srkgt', grouped, new_keys.astype(jnp.float32)) * inv_root
    causal = jnp.arange(step_count)[None, :] <= jnp.arange(step_count)[:, None]
    own_scores = jnp.where(causal[:, None, None, None, :], own_scores, -1e+30)
    peak = jnp.maximum(lax.optimization_barrier(jnp.max(far_scores, axis=(-2, -1))), lax.optimization_barrier(jnp.max(own_scores, axis=-1)))
    far_weights = jnp.exp(far_scores - peak[..., None, None])
    own_weights = jnp.exp(own_scores - peak[..., None])
    normalizer = lax.optimization_barrier(jnp.sum(far_weights, axis=(-2, -1))) + lax.optimization_barrier(jnp.sum(own_weights, axis=-1))
    far_probs = (far_weights / normalizer[..., None, None]).astype(jnp.bfloat16)
    own_probs = (own_weights / normalizer[..., None]).astype(jnp.bfloat16)
    attended = jnp.einsum('srkgpc,pckd->srkgd', far_probs.astype(jnp.float32), value_block.astype(jnp.float32))
    attended = attended + jnp.einsum('srkgt,trkd->srkgd', own_probs.astype(jnp.float32), new_values.astype(jnp.float32))
    return attended.reshape(step_count, row_count, head_count * head_size).astype(jnp.bfloat16)

def reference(states, attn_gain, moe_gain, w_query, w_key, w_value, w_output, w_gate_up, w_down, key_cache, value_cache, cache_lengths, prefix_slot, routes, gate_weights):
    normed = rms_scale(states, attn_gain).astype(jnp.bfloat16)
    flat_normed = normed.reshape(2 * B, D).astype(jnp.float32)
    queries = jnp.dot(flat_normed, w_query.astype(jnp.float32)).reshape(2, B, HQ, HD)
    new_keys = jnp.dot(flat_normed, w_key.astype(jnp.float32)).reshape(2, B, KVH, HD)
    new_values = jnp.dot(flat_normed, w_value.astype(jnp.float32)).reshape(2, B, KVH, HD).astype(jnp.bfloat16)
    prefix_id = (jnp.arange(B) // BR_DEV * PREF_DEV + prefix_slot).astype(jnp.int32)
    positions = cache_lengths[prefix_id].astype(jnp.float32)[None, :] + jnp.arange(2).astype(jnp.float32)[:, None]
    queries = rotate(queries, positions).astype(jnp.bfloat16)
    new_keys = rotate(new_keys, positions).astype(jnp.bfloat16)

    def by_block(array):
        return jnp.swapaxes(array.reshape((2, N_EP, BR_DEV) + array.shape[2:]), 0, 1)
    attended = lax.map(attend_block, (by_block(queries), by_block(new_keys), by_block(new_values), key_cache.reshape(N_EP, PREF_DEV, CACHE, KVH, HD), value_cache.reshape(N_EP, PREF_DEV, CACHE, KVH, HD), cache_lengths.reshape(N_EP, PREF_DEV), prefix_slot.reshape(N_EP, BR_DEV)))
    attended = jnp.swapaxes(attended, 0, 1).reshape(2 * B, HQ * HD)
    projected = jnp.dot(attended.astype(jnp.float32), w_output.astype(jnp.float32)).reshape(2, B, D)
    hidden = states + projected
    moe_input = rms_scale(hidden, moe_gain).astype(jnp.bfloat16).reshape(2 * B, D)
    flat_routes = jnp.swapaxes(routes, 0, 1).reshape(-1).astype(jnp.int32)
    total_count = flat_routes.shape[0]
    sorted_ids = jnp.argsort(flat_routes, stable=True).astype(jnp.int32)
    counts = lax.optimization_barrier(jnp.sum((flat_routes[:, None] == jnp.arange(EXPERTS)[None, :]).astype(jnp.int32), axis=0))
    starts = (jnp.cumsum(counts) - counts).astype(jnp.int32)
    row_limit = N_EP * CAP
    padded_ids = jnp.concatenate([sorted_ids, jnp.zeros((row_limit,), jnp.int32)])

    def run_expert(expert_id):
        chosen = lax.dynamic_slice_in_dim(padded_ids, starts[expert_id], row_limit)
        inputs = moe_input[chosen // TOPK].astype(jnp.float32)
        both = jnp.dot(inputs, w_gate_up[expert_id].astype(jnp.float32))
        activation = (jax.nn.silu(both[:, :FF]) * both[:, FF:]).astype(jnp.bfloat16)
        return jnp.dot(activation.astype(jnp.float32), w_down[expert_id].astype(jnp.float32)).astype(jnp.bfloat16)
    outputs = lax.map(run_expert, jnp.arange(EXPERTS).astype(jnp.int32))
    within = jnp.zeros((total_count,), jnp.int32).at[sorted_ids].set(jnp.arange(total_count).astype(jnp.int32) - starts[flat_routes[sorted_ids]])
    picked = outputs[flat_routes, within].astype(jnp.float32).reshape(2, B, TOPK, D)
    mixture = lax.optimization_barrier(jnp.sum(gate_weights[..., None] * picked, axis=2))
    appended = jnp.concatenate([new_keys.reshape(2, B, KVH * HD), new_values.reshape(2, B, KVH * HD)], axis=-1)
    return (hidden + mixture, appended)
```

```python
import math

import jax
import jax.numpy as jnp
import numpy as np
from jax import lax
from jax.experimental import pallas as pl
from jax.experimental.pallas import tpu as pltpu
from jax.sharding import PartitionSpec as P

HQ = 16
KVH = 2
HD = 128
TOPK = 8


EPS = 1e-06
THETA = 1000000.0


def rms_scale(values, gain):
    squares = jnp.mean(values * values, axis=-1, keepdims=True)
    return values * lax.rsqrt(squares + EPS) * gain


def rotate(vectors, positions):
    head_size = vectors.shape[-1]
    half_size = head_size // 2
    inverse_rate = THETA ** (-(jnp.arange(half_size).astype(jnp.float32) * 2.0 / head_size))
    phases = positions[..., None, None] * inverse_rate
    cosine = jnp.cos(phases)
    sine_part = jnp.sin(phases)
    first_half = vectors[..., :half_size]
    second_half = vectors[..., half_size:]
    return jnp.concatenate(
        [
            first_half * cosine - second_half * sine_part,
            second_half * cosine + first_half * sine_part,
        ],
        axis=-1,
    )


def attend_block(queries, new_keys, new_values, key_block, value_block, lengths, slots):
    step_count, row_count, head_count, head_size = queries.shape
    prefix_count, cache_span, kv_heads, _ = key_block.shape
    group_size = head_count // kv_heads
    grouped = queries.reshape(step_count, row_count, kv_heads, group_size, head_size)
    inv_root = 1.0 / math.sqrt(head_size)
    far_scores = (
        jnp.einsum("srkgd,pckd->srkgpc", grouped, key_block, preferred_element_type=jnp.float32)
        * inv_root
    )
    visible = (jnp.arange(cache_span)[None, None, :] < lengths[None, :, None]) & (
        slots[:, None, None] == jnp.arange(prefix_count)[None, :, None]
    )
    far_scores = jnp.where(visible[None, :, None, None], far_scores, -1e30)
    own_scores = (
        jnp.einsum("srkgd,trkd->srkgt", grouped, new_keys, preferred_element_type=jnp.float32)
        * inv_root
    )
    causal = jnp.arange(step_count)[None, :] <= jnp.arange(step_count)[:, None]
    own_scores = jnp.where(causal[:, None, None, None, :], own_scores, -1e30)
    peak = jnp.maximum(jnp.max(far_scores, axis=(-2, -1)), jnp.max(own_scores, axis=-1))
    far_weights = jnp.exp(far_scores - peak[..., None, None])
    own_weights = jnp.exp(own_scores - peak[..., None])
    normalizer = jnp.sum(far_weights, axis=(-2, -1)) + jnp.sum(own_weights, axis=-1)
    far_probs = (far_weights / normalizer[..., None, None]).astype(jnp.bfloat16)
    own_probs = (own_weights / normalizer[..., None]).astype(jnp.bfloat16)
    attended = jnp.einsum(
        "srkgpc,pckd->srkgd", far_probs, value_block, preferred_element_type=jnp.float32
    )
    attended = attended + jnp.einsum(
        "srkgt,trkd->srkgd", own_probs, new_values, preferred_element_type=jnp.float32
    )
    return attended.reshape(step_count, row_count, head_count * head_size).astype(jnp.bfloat16)


def shards(
    states,
    attn_gain,
    moe_gain,
    w_query,
    w_key,
    w_value,
    w_output,
    w_gate_up,
    w_down,
    key_cache,
    value_cache,
    cache_lengths,
    prefix_slot,
    routes,
    gate_weights,
):
    devices = lax.axis_size("ep")
    step_count, row_count, model_width = states.shape
    query_cols = w_query.shape[1]
    kv_cols = w_key.shape[1]
    normed = rms_scale(states, attn_gain).astype(jnp.bfloat16)
    joined = jnp.concatenate([w_query, w_key, w_value], axis=1)
    head_parts = jnp.einsum(
        "srd,dc->src",
        lax.all_gather(normed, "ep", axis=1, tiled=True),
        joined,
        preferred_element_type=jnp.float32,
    )
    own_cols = lax.all_to_all(head_parts, "ep", split_axis=1, concat_axis=2, tiled=True)
    own_cols = own_cols.reshape(step_count, row_count, devices, query_cols + 2 * kv_cols)
    queries = own_cols[..., :query_cols].reshape(step_count, row_count, HQ, HD)
    new_keys = own_cols[..., query_cols : query_cols + kv_cols].reshape(
        step_count, row_count, KVH, HD
    )
    new_values = (
        own_cols[..., query_cols + kv_cols :]
        .reshape(step_count, row_count, KVH, HD)
        .astype(jnp.bfloat16)
    )
    prefix_count, cache_span, _ = key_cache.shape
    lengths_here = jnp.sum(
        jnp.where(
            prefix_slot[:, None] == jnp.arange(prefix_count)[None, :], cache_lengths[None, :], 0
        ),
        axis=1,
    )
    positions = (
        lengths_here.astype(jnp.float32)[None, :]
        + jnp.arange(step_count).astype(jnp.float32)[:, None]
    )
    queries = rotate(queries, positions).astype(jnp.bfloat16)
    new_keys = rotate(new_keys, positions).astype(jnp.bfloat16)
    attended = attend_block(
        queries,
        new_keys,
        new_values,
        key_cache.reshape(prefix_count, cache_span, KVH, HD),
        value_cache.reshape(prefix_count, cache_span, KVH, HD),
        cache_lengths,
        prefix_slot,
    )
    w_columns = lax.all_to_all(w_output, "ep", split_axis=1, concat_axis=0, tiled=True)
    column_part = jnp.einsum(
        "srf,fc->src",
        lax.all_gather(attended, "ep", axis=1, tiled=True),
        w_columns,
        preferred_element_type=jnp.float32,
    )
    projected = lax.all_to_all(column_part, "ep", split_axis=1, concat_axis=2, tiled=True)
    hidden = states + projected
    moe_input = (
        rms_scale(hidden, moe_gain)
        .astype(jnp.bfloat16)
        .reshape(step_count * row_count, model_width)
    )
    expert_count = w_gate_up.shape[0] * devices
    capacity = max(2, 4 * row_count * TOPK // expert_count)
    flat_routes = jnp.swapaxes(routes, 0, 1).reshape(-1)
    order = jnp.arange(flat_routes.shape[0])
    earlier = (flat_routes[:, None] == flat_routes[None, :]) & (order[None, :] < order[:, None])
    within = jnp.sum(earlier.astype(jnp.int32), axis=1)
    slot_index = flat_routes * capacity + within
    dispatch = (jnp.arange(expert_count * capacity)[:, None] == slot_index[None, :]).astype(
        jnp.bfloat16
    )
    repeated = jnp.repeat(moe_input, TOPK, axis=0)
    outgoing = jnp.dot(dispatch, repeated, preferred_element_type=jnp.float32).astype(jnp.bfloat16)
    outgoing = outgoing.reshape(expert_count, capacity, model_width)
    both = jnp.einsum(
        "nsd,df->nsf",
        lax.all_to_all(outgoing, "ep", split_axis=0, concat_axis=0, tiled=True),
        w_gate_up[0],
        preferred_element_type=jnp.float32,
    )
    half_cols = both.shape[-1] // 2
    activation = (jax.nn.silu(both[..., :half_cols]) * both[..., half_cols:]).astype(jnp.bfloat16)
    expert_done = jnp.einsum(
        "nsf,fd->nsd", activation, w_down[0], preferred_element_type=jnp.float32
    ).astype(jnp.bfloat16)
    returned = lax.all_to_all(expert_done, "ep", split_axis=0, concat_axis=0, tiled=True)
    picked = returned.reshape(expert_count * capacity, model_width)[slot_index]
    picked = picked.astype(jnp.float32).reshape(step_count, row_count, TOPK, model_width)
    mixture = jnp.sum(gate_weights[..., None] * picked, axis=2)
    appended = jnp.concatenate(
        [
            new_keys.reshape(step_count, row_count, KVH * HD),
            new_values.reshape(step_count, row_count, KVH * HD),
        ],
        axis=-1,
    )
    return (hidden + mixture, appended)


TUNED_DEVICES = 16
ROWS = 16
NODES = 8
QUADS = 4
CODE_TOP = 14.99
CODE_STEPS = 256.0


def norm_rows(values, gain):
    squares = jnp.mean(values * values, axis=-1, keepdims=True)
    return values * lax.rsqrt(squares + EPS) * gain


def layer_kernel(
    states,
    attn_gain,
    moe_gain,
    rates,
    lengths,
    slots,
    routes,
    gate_weights,
    w_query,
    w_key,
    w_value,
    w_output,
    w_gate_up,
    w_down,
    key_cache,
    value_cache,
    out,
    appended,
    w_query_v,
    w_kv_v,
    gates_all,
    gather_q,
    gather_o,
    gather_m,
    attended_v,
    parts,
    own_parts,
    w_cols,
    cols,
    own_cols,
    hidden,
    act,
    mix,
    coded,
    near_in,
    relay_in,
    mirror_out,
    mirror_in,
    fresh_k,
    fresh_v,
    queries,
    gate_up_v,
    down_v,
    keys_v,
    values_v,
    load_sem,
    twin_send,
    twin_recv,
    ag_send,
    ag_recv,
    a2a_send,
    a2a_recv,
):
    me = lax.axis_index("ep")
    c = me % 2
    node = me // 2
    half = node // QUADS
    quad = node % QUADS
    twin = me + 1 - 2 * c
    width = states.shape[1]
    wide = width // QUADS
    deep = width // 2
    ff = down_v.shape[1]

    def device(m):
        return m * 2 + c

    mates = [half * QUADS + (quad + i) % QUADS for i in range(1, QUADS)]
    mirror = (node + QUADS) % NODES
    across = [(1 - half) * QUADS + (quad + i) % QUADS for i in range(QUADS)]

    def block(ref, m):
        return ref.at[pl.ds(pl.multiple_of(m * ROWS, ROWS), ROWS), :]

    def rdma(src, dst, send, recv, target):
        return pltpu.make_async_remote_copy(
            src_ref=src,
            dst_ref=dst,
            send_sem=send,
            recv_sem=recv,
            device_id={"ep": target},
            device_id_type=pl.DeviceIdType.MESH,
        )

    barrier = pltpu.get_barrier_semaphore()
    for target in [twin] + [device((node + i) % NODES) for i in range(1, NODES)]:
        pl.semaphore_signal(
            barrier,
            inc=1,
            device_id={"ep": target},
            device_id_type=pl.DeviceIdType.MESH,
        )

    def lanes_of(index, size):
        return pl.ds(pl.multiple_of(index * size, size), size)

    def twin_pairs():
        return [
            (w_query, w_query_v.at[:, lanes_of(c, 128)]),
            (w_key, w_kv_v.at[pl.ds(pl.multiple_of(c * 16, 16), 16), :]),
            (w_value, w_kv_v.at[pl.ds(pl.multiple_of(32 + c * 16, 16), 16), :]),
            (w_gate_up, gate_up_v.at[c]),
            (w_down, down_v.at[c]),
        ]

    local = [pltpu.make_async_copy(s, d, load_sem.at[i]) for i, (s, d) in enumerate(twin_pairs())]
    shared = [
        rdma(s, d, twin_send.at[i], twin_recv.at[i], twin) for i, (s, d) in enumerate(twin_pairs())
    ]
    w_rows = pl.ds(pl.multiple_of((2 * quad + c) * 128, 128), 128)
    local += [
        pltpu.make_async_copy(key_cache, keys_v, load_sem.at[5]),
        pltpu.make_async_copy(value_cache, values_v, load_sem.at[6]),
        pltpu.make_async_copy(
            w_output.at[:, lanes_of(quad, wide)], w_cols.at[w_rows, :], load_sem.at[7]
        ),
    ]
    for i in (0, 1, 2, 5, 6, 7, 3, 4):
        local[i].start()

    class Gather:
        def __init__(self, buf, phase, chunks):
            self.buf, self.phase, self.sends = buf, phase, []
            self.size = buf.shape[1] // chunks
            self.chunks = chunks

        def piece(self, m, chunk):
            rows = pl.ds(pl.multiple_of(m * ROWS, ROWS), ROWS)
            return self.buf.at[rows, chunk * self.size : (chunk + 1) * self.size]

        def push(self, src, dst, m, chunk, target):
            k = len(self.sends)
            copy = rdma(
                src,
                dst,
                ag_send.at[self.phase, k],
                ag_recv.at[self.phase, m + NODES * chunk],
                device(target),
            )
            copy.start()
            self.sends.append(copy)

        def arrived(self, ref, m, chunk):
            rdma(
                ref,
                ref,
                ag_send.at[self.phase, 0],
                ag_recv.at[self.phase, m + NODES * chunk],
                device(mates[0]),
            ).wait_recv()

        def cross(self, source):
            for chunk in range(self.chunks):
                piece = source.at[:, chunk * self.size : (chunk + 1) * self.size]
                self.push(piece, self.piece(node, chunk), node, chunk, mirror)

        def begin(self, source):
            for m in mates:
                self.push(source, block(self.buf, node), node, 0, m)

        def forward(self):
            for chunk in range(self.chunks):
                piece = self.piece(mirror, chunk)
                self.arrived(piece, mirror, chunk)
                for m in mates:
                    self.push(piece, piece, mirror, chunk, m)

        def near_ready(self):
            for m in mates:
                self.arrived(block(self.buf, m), m, 0)

        def far_ready(self):
            for chunk in range(self.chunks):
                for m in mates:
                    far = (m + QUADS) % NODES
                    self.arrived(self.piece(far, chunk), far, chunk)

        def finish(self):
            for copy in self.sends:
                copy.wait_send()

    class Scatter:
        def __init__(self, src, dst, phase, view):
            self.src, self.dst, self.phase, self.view = src, dst, phase, view

        def copy(self, to, source):
            return rdma(
                self.view(self.src, to),
                self.view(self.dst, source),
                a2a_send.at[self.phase, to],
                a2a_recv.at[self.phase, source],
                device(to),
            )

        def start(self, targets):
            for m in targets:
                self.copy(m, node).start()

        def arrived(self, sources):
            for m in sources:
                self.copy(m, m).wait_recv()

        def sent(self, targets):
            for m in targets:
                self.copy(m, m).wait_send()

    def whole(ref, m):
        return ref.at[m]

    others = mates + across

    block(gather_q, node)[...] = norm_rows(states[...], attn_gain[...]).astype(jnp.bfloat16)
    pl.semaphore_wait(barrier, NODES)

    first = Gather(gather_q, 0, 2)
    first.cross(block(gather_q, node))
    first.begin(block(gather_q, node))
    for i in (0, 1, 2):
        shared[i].start()

    row_id = lax.broadcasted_iota(jnp.int32, (ROWS, 128), 0)
    lane_id = lax.broadcasted_iota(jnp.int32, (ROWS, 128), 1)
    chosen = jnp.concatenate([routes[:, 0, :], routes[:, 1, :]], axis=0)
    shares = jnp.concatenate([gate_weights[0], gate_weights[1]], axis=0)
    weighed = jnp.zeros((ROWS, 128), jnp.float32)
    for k in range(TOPK):
        weighed = jnp.where(lane_id == chosen[:, k : k + 1], shares[:, k : k + 1], weighed)
    block(gates_all, node)[...] = weighed
    slot_of = jnp.zeros((ROWS, 128), jnp.int32)
    for b in range(8):
        slot_of = jnp.where(row_id % 8 == b, slots[b], slot_of)
    limits = [jnp.where(slot_of == p, lengths[p], 0) for p in range(2)]
    phases = (limits[0] + limits[1] + row_id // 8).astype(jnp.float32) * rates[...]
    cosine = jnp.cos(phases)
    sine = jnp.sin(phases)
    sine = jnp.where(lane_id < 64, -sine, sine)

    def group_rows(group):
        return pl.ds(pl.multiple_of(group * 64, 64), 64)

    def project(group):
        inputs = gather_q[group_rows(group), :]
        q = jnp.dot(inputs, w_query_v[...], preferred_element_type=jnp.float32)
        kv = lax.dot_general(
            inputs, w_kv_v[...], (((1,), (1,)), ((), ())), preferred_element_type=jnp.float32
        )
        kv = kv.reshape(QUADS, ROWS, 64)
        kv = jnp.concatenate([kv[:, 0:8, :], kv[:, 8:16, :]], axis=-1)
        at = pl.ds(group * QUADS, QUADS)
        parts[at, 0:ROWS, :] = q[:, 0:128].reshape(QUADS, ROWS, 128)
        parts[at, ROWS : 2 * ROWS, :] = q[:, 128:256].reshape(QUADS, ROWS, 128)
        parts[at, 2 * ROWS : 2 * ROWS + 8, :] = kv

    gates_sent = Scatter(gates_all, gates_all, 3, block)

    def gates_copy(to, source):
        return rdma(
            block(gates_all, source),
            block(gates_all, source),
            a2a_send.at[3, to],
            a2a_recv.at[3, source],
            device(to),
        )

    w_out = Scatter(w_output, w_cols, 2, None)

    def w_copy(to, source):
        return rdma(
            w_output.at[:, lanes_of(to % QUADS, wide)],
            w_cols.at[pl.ds(pl.multiple_of((2 * (source % QUADS) + c) * 128, 128), 128), :],
            a2a_send.at[2, to],
            a2a_recv.at[2, source],
            device(to),
        )

    w_out.copy = w_copy

    first.forward()
    for i in (0, 1, 2):
        local[i].wait()
        shared[i].wait_recv()
    first.near_ready()
    project(half)
    heads = Scatter(parts, own_parts, 0, whole)
    heads.start(mates)
    own_parts[node] = parts[node]
    first.far_ready()
    project(1 - half)
    heads.start(across)
    w_out.start(mates)
    shared[3].start()
    shared[4].start()
    first.finish()
    heads.arrived(others)

    def turned(vectors):
        return vectors * cosine + pltpu.roll(vectors, 64, 1) * sine

    for j in range(NODES):
        for cc in range(2):
            h = 2 * j + cc
            queries[h * ROWS : (h + 1) * ROWS, :] = turned(
                own_parts[j, cc * ROWS : (cc + 1) * ROWS, :]
            ).astype(jnp.bfloat16)
        packed = own_parts[j, 2 * ROWS : 2 * ROWS + 8, :]
        unpacked = jnp.concatenate([packed[:, 0:64], packed[:, 64:128]], axis=0)
        fresh_k[:, j * 32 : (j + 1) * 32] = unpacked[:, 0:32]
        fresh_v[:, j * 32 : (j + 1) * 32] = unpacked[:, 32:64]
    local[5].wait()
    local[6].wait()
    inv_root = 1.0 / math.sqrt(HD)
    group_size = HQ // KVH
    q_rows = group_size * ROWS
    span = keys_v.shape[1]
    far_pos = lax.broadcasted_iota(jnp.int32, (q_rows, span), 1)
    row_at = lax.broadcasted_iota(jnp.int32, (q_rows, ROWS), 0) % ROWS
    col_at = lax.broadcasted_iota(jnp.int32, (q_rows, ROWS), 1)
    own_seen = (row_at % 8 == col_at % 8) & (col_at // 8 <= row_at // 8)
    limits = [jnp.concatenate([m[:, 0:1]] * group_size, axis=0) for m in limits]

    def attend(k):
        lanes = lanes_of(k, HD)
        new_keys = turned(fresh_k[:, lanes]).astype(jnp.bfloat16)
        new_values = fresh_v[:, lanes].astype(jnp.bfloat16)
        appended[:, lanes] = new_keys
        appended[:, lanes_of(KVH + k, HD)] = new_values
        q = queries[pl.ds(pl.multiple_of(k * q_rows, q_rows), q_rows), :]

        def against(rows):
            return (
                lax.dot_general(
                    q, rows, (((1,), (1,)), ((), ())), preferred_element_type=jnp.float32
                )
                * inv_root
            )

        scores = [
            jnp.where(far_pos < limits[p], against(keys_v[p, :, lanes]), -1e30) for p in range(2)
        ]
        own_scores = jnp.where(own_seen, against(new_keys), -1e30)
        peak = jnp.maximum(
            jnp.maximum(
                jnp.max(scores[0], axis=1, keepdims=True), jnp.max(scores[1], axis=1, keepdims=True)
            ),
            jnp.max(own_scores, axis=1, keepdims=True),
        )
        weights = [jnp.exp(s - peak) for s in scores]
        own_weights = jnp.exp(own_scores - peak)
        total = (
            jnp.sum(weights[0], axis=1, keepdims=True)
            + jnp.sum(weights[1], axis=1, keepdims=True)
            + jnp.sum(own_weights, axis=1, keepdims=True)
        )
        scale = 1.0 / total
        attended = jnp.dot(
            (own_weights * scale).astype(jnp.bfloat16),
            new_values,
            preferred_element_type=jnp.float32,
        )
        for p in range(2):
            attended = attended + jnp.dot(
                (weights[p] * scale).astype(jnp.bfloat16),
                values_v[p, :, lanes],
                preferred_element_type=jnp.float32,
            )
        attended = attended.astype(jnp.bfloat16)
        for g in range(group_size):
            attended_v[k, :, g * HD : (g + 1) * HD] = attended[g * ROWS : (g + 1) * ROWS, :]

    second = Gather(gather_o, 1, 1)
    attend(1 - half)
    second.cross(attended_v.at[1 - half])
    attend(half)
    second.begin(attended_v.at[half])
    block(gather_o, node)[...] = attended_v[half]
    for m in others:
        gates_copy(m, node).start()
    heads.sent(others)

    def w_pass(q, core):
        rows = w_cols.at[pl.ds(pl.multiple_of((2 * q + core) * 128, 128), 128), :]
        return rdma(rows, rows, twin_send.at[8 + q], twin_recv.at[8 + q], twin)

    local[7].wait()
    w_pass(quad, c).start()
    w_out.arrived(mates)
    for m in mates:
        w_pass(m % QUADS, c).start()
    second.forward()
    for m in [node] + mates:
        w_pass(m % QUADS, 1 - c).wait_recv()

    def out_project(group):
        cols[group_rows(group), :] = jnp.dot(
            gather_o[group_rows(group), :], w_cols[...], preferred_element_type=jnp.float32
        )

    second.near_ready()
    out_project(half)
    columns = Scatter(cols, own_cols, 1, block)
    columns.start(mates)
    block(own_cols, node)[...] = block(cols, node)[...]
    second.far_ready()
    out_project(1 - half)
    columns.start(across)
    second.finish()
    w_out.sent(mates)
    for m in [node] + mates:
        w_pass(m % QUADS, c).wait_send()
    columns.arrived(others)
    for q in range(QUADS):
        lanes = slice(q * wide, (q + 1) * wide)
        hidden[:, lanes] = states[:, lanes] + (
            own_cols[q * ROWS : (q + 1) * ROWS, :]
            + own_cols[(q + QUADS) * ROWS : (q + QUADS + 1) * ROWS, :]
        )
    block(gather_m, node)[...] = norm_rows(hidden[...], moe_gain[...]).astype(jnp.bfloat16)

    third = Gather(gather_m, 2, 2)
    third.cross(block(gather_m, node))
    third.begin(block(gather_m, node))
    columns.sent(others)
    for m in others:
        gates_copy(m, m).wait_recv()
    for i in (3, 4):
        local[i].wait()
        shared[i].wait_recv()

    def code_of(largest):
        return jnp.ceil(jnp.log2(jnp.maximum(largest, 1e-30)) * CODE_STEPS)

    def encode(values, code, ref_rows, lanes, ref):
        factor = jnp.exp2(CODE_TOP - code * (1.0 / CODE_STEPS))
        ref[ref_rows, lanes] = (
            jnp.round(values * factor).astype(jnp.int32).astype(jnp.int16)
        )

    def decode(ref):
        values = ref[...]
        code = values[:, width : width + 1].astype(jnp.int32).astype(jnp.float32)
        factor = jnp.exp2(code * (1.0 / CODE_STEPS) - CODE_TOP)
        return values[:, :width].astype(jnp.int32).astype(jnp.float32) * factor

    group_lane = lax.broadcasted_iota(jnp.int32, (64, 128), 1)

    def experts(group):
        rows = group_rows(group)

        for e in range(2):

            @pl.loop(0, ff // 256)
            def _(t):
                at = pl.multiple_of(t * 256, 256)
                inputs = gather_m[rows, :]
                g = jnp.dot(
                    inputs, gate_up_v[e, :, pl.ds(at, 256)], preferred_element_type=jnp.float32
                )
                u = jnp.dot(
                    inputs,
                    gate_up_v[e, :, pl.ds(pl.multiple_of(ff + t * 256, 256), 256)],
                    preferred_element_type=jnp.float32,
                )
                act[e, :, pl.ds(at, 256)] = (g / (1.0 + jnp.exp(-g)) * u).astype(jnp.bfloat16)

        gates = gates_all[rows, :]
        share = [
            jnp.sum(jnp.where(group_lane == 2 * node + e, gates, 0.0), axis=1, keepdims=True)
            for e in range(2)
        ]

        def tile(t, largest):
            at = pl.multiple_of(t * 512, 512)
            total = jnp.zeros((64, 512), jnp.float32)
            for e in range(2):
                got = jnp.dot(
                    act[e], down_v[e, :, pl.ds(at, 512)], preferred_element_type=jnp.float32
                )
                got = got.astype(jnp.bfloat16).astype(jnp.float32)
                total = total + jnp.where(share[e] > 0.0, share[e] * got, 0.0)
            mix[rows, pl.ds(at, 512)] = total
            return jnp.maximum(largest, jnp.max(jnp.abs(total), axis=1, keepdims=True))

        largest = lax.fori_loop(0, width // 512, tile, jnp.zeros((64, 1), jnp.float32))
        code = code_of(largest)

        @pl.loop(0, width // 512)
        def _(t):
            lanes = pl.ds(pl.multiple_of(t * 512, 512), 512)
            encode(mix[rows, lanes], code, rows, lanes, coded)

        coded[rows, pl.ds(width, 128)] = jnp.broadcast_to(
            code.astype(jnp.int32), (64, 128)
        ).astype(jnp.int16)

    def by_quad(ref, m):
        return ref.at[m % QUADS]

    class Return(Scatter):
        def copy(self, to, source):
            block_of = to if self.phase == 4 else (to + QUADS) % NODES
            return rdma(
                block(coded, block_of),
                self.dst.at[source % QUADS],
                a2a_send.at[self.phase, to],
                a2a_recv.at[self.phase, source],
                device(to),
            )

    third.forward()
    third.near_ready()
    experts(half)
    home = Return(coded, near_in, 4, None)
    home.start(mates)
    third.far_ready()
    experts(1 - half)
    relay = Return(coded, relay_in, 5, None)
    relay.start(mates)
    third.finish()
    total = hidden[...] + block(mix, node)[...]
    home.arrived(mates)
    for m in mates:
        total = total + decode(near_in.at[m % QUADS])
    hidden[...] = total
    total = block(mix, mirror)[...]
    relay.arrived(mates)
    for m in mates:
        total = total + decode(relay_in.at[m % QUADS])
    code = code_of(jnp.max(jnp.abs(total), axis=1, keepdims=True))
    encode(total, code, slice(None), slice(0, width), mirror_out)
    mirror_out[:, width : width + 128] = jnp.broadcast_to(
        code.astype(jnp.int32), (ROWS, 128)
    ).astype(jnp.int16)
    last = rdma(mirror_out, mirror_in, a2a_send.at[6, 0], a2a_recv.at[6, 0], device(mirror))
    last.start()
    home.sent(mates)
    relay.sent(mates)
    for m in others:
        gates_copy(m, node).wait_send()
    for copy in shared:
        copy.wait_send()
    last.wait()
    out[...] = hidden[...] + decode(mirror_in)


def tuned(
    states,
    attn_gain,
    moe_gain,
    w_query,
    w_key,
    w_value,
    w_output,
    w_gate_up,
    w_down,
    key_cache,
    value_cache,
    cache_lengths,
    prefix_slot,
    routes,
    gate_weights,
):
    step_count, row_count, width = states.shape
    rows = step_count * row_count
    prefix_count, span, kv_width = key_cache.shape
    ff = w_down.shape[1]
    rates = np.tile(THETA ** (-(np.arange(HD // 2) * 2.0 / HD)), 2)
    rates = jnp.asarray(rates.astype(np.float32).reshape(1, HD))
    in_vmem = pl.BlockSpec(memory_space=pltpu.VMEM)
    in_smem = pl.BlockSpec(memory_space=pltpu.SMEM)
    in_hbm = pl.BlockSpec(memory_space=pl.ANY)
    everyone = NODES * rows
    coded_width = width + 128
    bf16, f32, i16 = jnp.bfloat16, jnp.float32, jnp.int16
    out, appended = pl.pallas_call(
        layer_kernel,
        out_shape=(
            jax.ShapeDtypeStruct((rows, width), f32),
            jax.ShapeDtypeStruct((rows, 2 * kv_width), bf16),
        ),
        in_specs=[in_vmem] * 4 + [in_smem] * 2 + [in_vmem] * 2 + [in_hbm] * 8,
        out_specs=(in_vmem, in_vmem),
        scratch_shapes=[
            pltpu.VMEM((width, 256), bf16),
            pltpu.VMEM((64, width), bf16),
            pltpu.VMEM((everyone, 128), f32),
            pltpu.VMEM((everyone, width), bf16),
            pltpu.VMEM((everyone, width // 2), bf16),
            pltpu.VMEM((everyone, width), bf16),
            pltpu.VMEM((2, rows, width // 2), bf16),
            pltpu.VMEM((NODES, 2 * rows + 8, 128), f32),
            pltpu.VMEM((NODES, 2 * rows + 8, 128), f32),
            pltpu.VMEM((width // 2, width // QUADS), bf16),
            pltpu.VMEM((everyone, width // QUADS), f32),
            pltpu.VMEM((everyone, width // QUADS), f32),
            pltpu.VMEM((rows, width), f32),
            pltpu.VMEM((2, everyone // 2, ff), bf16),
            pltpu.VMEM((everyone, width), f32),
            pltpu.VMEM((everyone, coded_width), i16),
            pltpu.VMEM((QUADS, rows, coded_width), i16),
            pltpu.VMEM((QUADS, rows, coded_width), i16),
            pltpu.VMEM((rows, coded_width), i16),
            pltpu.VMEM((rows, coded_width), i16),
            pltpu.VMEM((rows, kv_width), f32),
            pltpu.VMEM((rows, kv_width), f32),
            pltpu.VMEM((HQ * rows, HD), bf16),
            pltpu.VMEM((2, width, 2 * ff), bf16),
            pltpu.VMEM((2, ff, width), bf16),
            pltpu.VMEM((prefix_count, span, kv_width), bf16),
            pltpu.VMEM((prefix_count, span, kv_width), bf16),
            pltpu.SemaphoreType.DMA((8,)),
            pltpu.SemaphoreType.DMA((12,)),
            pltpu.SemaphoreType.DMA((12,)),
            pltpu.SemaphoreType.DMA((3, 16)),
            pltpu.SemaphoreType.DMA((3, 16)),
            pltpu.SemaphoreType.DMA((7, 8)),
            pltpu.SemaphoreType.DMA((7, 8)),
        ],
        compiler_params=pltpu.CompilerParams(
            collective_id=0, has_side_effects=True, vmem_limit_bytes=56 * 1024 * 1024
        ),
    )(
        states.reshape(rows, width),
        attn_gain.reshape(1, width),
        moe_gain.reshape(1, width),
        rates,
        cache_lengths,
        prefix_slot,
        routes,
        gate_weights,
        w_query,
        w_key.T,
        w_value.T,
        w_output,
        w_gate_up[0],
        w_down[0],
        key_cache,
        value_cache,
    )
    return (
        out.reshape(step_count, row_count, width),
        appended.reshape(step_count, row_count, 2 * kv_width),
    )


def solution(mesh):
    return jax.shard_map(
        tuned if mesh.shape["ep"] == TUNED_DEVICES else shards,
        mesh=mesh,
        in_specs=(
            P(None, ("groups", "ep"), None),
            P(),
            P(),
            P(None, "ep"),
            P(None, "ep"),
            P(None, "ep"),
            P("ep", None),
            P("ep", None, None),
            P("ep", None, None),
            P(("groups", "ep"), None, None),
            P(("groups", "ep"), None, None),
            P(("groups", "ep")),
            P(("groups", "ep")),
            P(("groups", "ep"), None, None),
            P(None, ("groups", "ep"), None),
        ),
        out_specs=(P(None, ("groups", "ep"), None), P(None, ("groups", "ep"), None)),
        check_vma=False,
    )
```

```python
import math

import jax
import jax.numpy as jnp
import numpy as np
from jax import lax
from jax.experimental import pallas as pl
from jax.experimental.pallas import tpu as pltpu
from jax.sharding import PartitionSpec as P

HQ = 16
KVH = 2
HD = 128
TOPK = 8


EPS = 1e-06
THETA = 1000000.0


def rms_scale(values, gain):
    squares = jnp.mean(values * values, axis=-1, keepdims=True)
    return values * lax.rsqrt(squares + EPS) * gain


def rotate(vectors, positions):
    head_size = vectors.shape[-1]
    half_size = head_size // 2
    inverse_rate = THETA ** (-(jnp.arange(half_size).astype(jnp.float32) * 2.0 / head_size))
    phases = positions[..., None, None] * inverse_rate
    cosine = jnp.cos(phases)
    sine_part = jnp.sin(phases)
    first_half = vectors[..., :half_size]
    second_half = vectors[..., half_size:]
    return jnp.concatenate(
        [
            first_half * cosine - second_half * sine_part,
            second_half * cosine + first_half * sine_part,
        ],
        axis=-1,
    )


def attend_block(queries, new_keys, new_values, key_block, value_block, lengths, slots):
    step_count, row_count, head_count, head_size = queries.shape
    prefix_count, cache_span, kv_heads, _ = key_block.shape
    group_size = head_count // kv_heads
    grouped = queries.reshape(step_count, row_count, kv_heads, group_size, head_size)
    inv_root = 1.0 / math.sqrt(head_size)
    far_scores = (
        jnp.einsum("srkgd,pckd->srkgpc", grouped, key_block, preferred_element_type=jnp.float32)
        * inv_root
    )
    visible = (jnp.arange(cache_span)[None, None, :] < lengths[None, :, None]) & (
        slots[:, None, None] == jnp.arange(prefix_count)[None, :, None]
    )
    far_scores = jnp.where(visible[None, :, None, None], far_scores, -1e30)
    own_scores = (
        jnp.einsum("srkgd,trkd->srkgt", grouped, new_keys, preferred_element_type=jnp.float32)
        * inv_root
    )
    causal = jnp.arange(step_count)[None, :] <= jnp.arange(step_count)[:, None]
    own_scores = jnp.where(causal[:, None, None, None, :], own_scores, -1e30)
    peak = jnp.maximum(jnp.max(far_scores, axis=(-2, -1)), jnp.max(own_scores, axis=-1))
    far_weights = jnp.exp(far_scores - peak[..., None, None])
    own_weights = jnp.exp(own_scores - peak[..., None])
    normalizer = jnp.sum(far_weights, axis=(-2, -1)) + jnp.sum(own_weights, axis=-1)
    far_probs = (far_weights / normalizer[..., None, None]).astype(jnp.bfloat16)
    own_probs = (own_weights / normalizer[..., None]).astype(jnp.bfloat16)
    attended = jnp.einsum(
        "srkgpc,pckd->srkgd", far_probs, value_block, preferred_element_type=jnp.float32
    )
    attended = attended + jnp.einsum(
        "srkgt,trkd->srkgd", own_probs, new_values, preferred_element_type=jnp.float32
    )
    return attended.reshape(step_count, row_count, head_count * head_size).astype(jnp.bfloat16)


def shards(
    states,
    attn_gain,
    moe_gain,
    w_query,
    w_key,
    w_value,
    w_output,
    w_gate_up,
    w_down,
    key_cache,
    value_cache,
    cache_lengths,
    prefix_slot,
    routes,
    gate_weights,
):
    devices = lax.axis_size("ep")
    step_count, row_count, model_width = states.shape
    query_cols = w_query.shape[1]
    kv_cols = w_key.shape[1]
    normed = rms_scale(states, attn_gain).astype(jnp.bfloat16)
    joined = jnp.concatenate([w_query, w_key, w_value], axis=1)
    head_parts = jnp.einsum(
        "srd,dc->src",
        lax.all_gather(normed, "ep", axis=1, tiled=True),
        joined,
        preferred_element_type=jnp.float32,
    )
    own_cols = lax.all_to_all(head_parts, "ep", split_axis=1, concat_axis=2, tiled=True)
    own_cols = own_cols.reshape(step_count, row_count, devices, query_cols + 2 * kv_cols)
    queries = own_cols[..., :query_cols].reshape(step_count, row_count, HQ, HD)
    new_keys = own_cols[..., query_cols : query_cols + kv_cols].reshape(
        step_count, row_count, KVH, HD
    )
    new_values = (
        own_cols[..., query_cols + kv_cols :]
        .reshape(step_count, row_count, KVH, HD)
        .astype(jnp.bfloat16)
    )
    prefix_count, cache_span, _ = key_cache.shape
    lengths_here = jnp.sum(
        jnp.where(
            prefix_slot[:, None] == jnp.arange(prefix_count)[None, :], cache_lengths[None, :], 0
        ),
        axis=1,
    )
    positions = (
        lengths_here.astype(jnp.float32)[None, :]
        + jnp.arange(step_count).astype(jnp.float32)[:, None]
    )
    queries = rotate(queries, positions).astype(jnp.bfloat16)
    new_keys = rotate(new_keys, positions).astype(jnp.bfloat16)
    attended = attend_block(
        queries,
        new_keys,
        new_values,
        key_cache.reshape(prefix_count, cache_span, KVH, HD),
        value_cache.reshape(prefix_count, cache_span, KVH, HD),
        cache_lengths,
        prefix_slot,
    )
    w_columns = lax.all_to_all(w_output, "ep", split_axis=1, concat_axis=0, tiled=True)
    column_part = jnp.einsum(
        "srf,fc->src",
        lax.all_gather(attended, "ep", axis=1, tiled=True),
        w_columns,
        preferred_element_type=jnp.float32,
    )
    projected = lax.all_to_all(column_part, "ep", split_axis=1, concat_axis=2, tiled=True)
    hidden = states + projected
    moe_input = (
        rms_scale(hidden, moe_gain)
        .astype(jnp.bfloat16)
        .reshape(step_count * row_count, model_width)
    )
    expert_count = w_gate_up.shape[0] * devices
    capacity = max(2, 4 * row_count * TOPK // expert_count)
    flat_routes = jnp.swapaxes(routes, 0, 1).reshape(-1)
    order = jnp.arange(flat_routes.shape[0])
    earlier = (flat_routes[:, None] == flat_routes[None, :]) & (order[None, :] < order[:, None])
    within = jnp.sum(earlier.astype(jnp.int32), axis=1)
    slot_index = flat_routes * capacity + within
    dispatch = (jnp.arange(expert_count * capacity)[:, None] == slot_index[None, :]).astype(
        jnp.bfloat16
    )
    repeated = jnp.repeat(moe_input, TOPK, axis=0)
    outgoing = jnp.dot(dispatch, repeated, preferred_element_type=jnp.float32).astype(jnp.bfloat16)
    outgoing = outgoing.reshape(expert_count, capacity, model_width)
    both = jnp.einsum(
        "nsd,df->nsf",
        lax.all_to_all(outgoing, "ep", split_axis=0, concat_axis=0, tiled=True),
        w_gate_up[0],
        preferred_element_type=jnp.float32,
    )
    half_cols = both.shape[-1] // 2
    activation = (jax.nn.silu(both[..., :half_cols]) * both[..., half_cols:]).astype(jnp.bfloat16)
    expert_done = jnp.einsum(
        "nsf,fd->nsd", activation, w_down[0], preferred_element_type=jnp.float32
    ).astype(jnp.bfloat16)
    returned = lax.all_to_all(expert_done, "ep", split_axis=0, concat_axis=0, tiled=True)
    picked = returned.reshape(expert_count * capacity, model_width)[slot_index]
    picked = picked.astype(jnp.float32).reshape(step_count, row_count, TOPK, model_width)
    mixture = jnp.sum(gate_weights[..., None] * picked, axis=2)
    appended = jnp.concatenate(
        [
            new_keys.reshape(step_count, row_count, KVH * HD),
            new_values.reshape(step_count, row_count, KVH * HD),
        ],
        axis=-1,
    )
    return (hidden + mixture, appended)


TUNED_DEVICES = 16
ROWS = 16
NODES = 8
QUADS = 4
CODE_TOP = 14.99
CODE_STEPS = 256.0


def norm_rows(values, gain):
    squares = jnp.mean(values * values, axis=-1, keepdims=True)
    return values * lax.rsqrt(squares + EPS) * gain


def layer_kernel(
    states_in,
    attn_gain_in,
    moe_gain_in,
    rates_in,
    lengths_in,
    slots_in,
    routes_in,
    gate_weights_in,
    w_query,
    w_key,
    w_value,
    w_output,
    w_gate_up,
    w_down,
    key_cache,
    value_cache,
    out,
    appended,
    states,
    attn_gain,
    moe_gain,
    rates,
    lengths,
    slots,
    routes,
    gate_weights,
    w_query_v,
    w_kv_v,
    gates_all,
    gather_q,
    gather_o,
    gather_m,
    attended_v,
    parts,
    own_parts,
    w_cols,
    cols,
    own_cols,
    hidden,
    act,
    mix,
    coded,
    near_in,
    relay_in,
    mirror_out,
    mirror_in,
    fresh_k,
    fresh_v,
    queries,
    gate_up_v,
    down_v,
    keys_v,
    values_v,
    small_sem,
    load_sem,
    twin_send,
    twin_recv,
    ag_sem,
    a2a_sem,
    ret_sem,
):
    me = lax.axis_index("ep")
    c = me % 2
    node = me // 2
    half = node // QUADS
    quad = node % QUADS
    twin = me + 1 - 2 * c
    width = states.shape[1]
    wide = width // QUADS
    deep = width // 2
    ff = down_v.shape[1]

    def device(m):
        return m * 2 + c

    mates = [half * QUADS + (quad + i) % QUADS for i in range(1, QUADS)]
    mirror = (node + QUADS) % NODES
    across = [(1 - half) * QUADS + (quad + i) % QUADS for i in range(QUADS)]

    def block(ref, m):
        return ref.at[pl.ds(pl.multiple_of(m * ROWS, ROWS), ROWS), :]

    def rdma(src, dst, send, recv, target):
        return pltpu.make_async_remote_copy(
            src_ref=src,
            dst_ref=dst,
            send_sem=send,
            recv_sem=recv,
            device_id={"ep": target},
            device_id_type=pl.DeviceIdType.MESH,
        )

    barrier = pltpu.get_barrier_semaphore()
    for target in [twin] + [device((node + i) % NODES) for i in range(1, NODES)]:
        pl.semaphore_signal(
            barrier,
            inc=1,
            device_id={"ep": target},
            device_id_type=pl.DeviceIdType.MESH,
        )

    small = [
        pltpu.make_async_copy(s, d, small_sem.at[i])
        for i, (s, d) in enumerate(
            (
                (states_in, states),
                (attn_gain_in, attn_gain),
                (lengths_in, lengths),
                (slots_in, slots),
                (rates_in, rates),
                (routes_in, routes),
                (gate_weights_in, gate_weights),
                (moe_gain_in, moe_gain),
            )
        )
    ]
    for copy in small:
        copy.start()

    def lanes_of(index, size):
        return pl.ds(pl.multiple_of(index * size, size), size)

    def twin_pairs():
        return [
            (w_query, w_query_v.at[:, lanes_of(c, 128)]),
            (w_key, w_kv_v.at[pl.ds(pl.multiple_of(c * 16, 16), 16), :]),
            (w_value, w_kv_v.at[pl.ds(pl.multiple_of(32 + c * 16, 16), 16), :]),
            (w_gate_up, gate_up_v.at[c]),
            (w_down, down_v.at[c]),
        ]

    local = [pltpu.make_async_copy(s, d, load_sem.at[i]) for i, (s, d) in enumerate(twin_pairs())]
    shared = [
        rdma(s, d, twin_send.at[i], twin_recv.at[i], twin) for i, (s, d) in enumerate(twin_pairs())
    ]
    w_rows = pl.ds(pl.multiple_of((2 * quad + c) * 128, 128), 128)
    local += [
        pltpu.make_async_copy(key_cache, keys_v, load_sem.at[5]),
        pltpu.make_async_copy(value_cache, values_v, load_sem.at[6]),
        pltpu.make_async_copy(
            w_output.at[:, lanes_of(quad, wide)], w_cols.at[w_rows, :], load_sem.at[7]
        ),
    ]
    for i in (0, 1, 2, 5, 6, 7, 3, 4):
        local[i].start()

    class Gather:
        def __init__(self, buf, phase, chunks):
            self.buf, self.phase, self.chunks = buf, phase, chunks
            self.size = buf.shape[1] // chunks
            self.send = ag_sem.at[6 * phase]

        def lanes(self, part):
            if part == 0:
                return slice(None)
            return slice((part - 1) % 2 * self.size, ((part - 1) % 2 + 1) * self.size)

        def piece(self, m, part):
            return self.buf.at[pl.ds(pl.multiple_of(m * ROWS, ROWS), ROWS), self.lanes(part)]

        def push(self, src, m, part, target):
            landed = ag_sem.at[6 * self.phase + 1 + part]
            rdma(src, self.piece(m, part), self.send, landed, device(target)).start()

        def arrived(self, part, count):
            ref = self.buf.at[0 : count * ROWS, self.lanes(part)]
            landed = ag_sem.at[6 * self.phase + 1 + part]
            rdma(ref, ref, self.send, landed, device(mirror)).wait_recv()

        def cross(self, source):
            for part in range(1, 1 + self.chunks):
                self.push(source.at[:, self.lanes(part)], node, part, mirror)

        def begin(self, source):
            for m in mates:
                self.push(source, node, 0, m)

        def forward(self):
            for part in range(1, 1 + self.chunks):
                self.arrived(part, 1)
                for m in mates:
                    self.push(self.piece(mirror, part), mirror, part + 2, m)

        def near_ready(self):
            self.arrived(0, QUADS - 1)

        def far_ready(self):
            for part in range(3, 3 + self.chunks):
                self.arrived(part, QUADS - 1)

        def finish(self):
            ref = self.buf.at[0 : 7 * ROWS, :]
            rdma(ref, ref, self.send, self.send, device(mirror)).wait_send()

    class Scatter:
        def __init__(self, src, dst, phase):
            self.src, self.dst = src, dst
            self.send, self.recv = a2a_sem.at[2 * phase], a2a_sem.at[2 * phase + 1]

        def pick(self, ref, m):
            return ref.at[m] if len(ref.shape) == 3 else block(ref, m)

        def start(self, targets):
            for m in targets:
                rdma(
                    self.pick(self.src, m),
                    self.pick(self.dst, node),
                    self.send,
                    self.recv,
                    device(m),
                ).start()

        def all(self, ref):
            count = 7 if len(ref.shape) == 3 else 7 * ROWS
            return ref.at[0:count]

        def arrived(self):
            dst = self.all(self.dst)
            rdma(dst, dst, self.send, self.recv, device(mirror)).wait_recv()

        def sent(self):
            src = self.all(self.src)
            rdma(src, src, self.send, self.recv, device(mirror)).wait_send()

    others = mates + across

    small[0].wait()
    small[1].wait()
    block(gather_q, node)[...] = norm_rows(states[...], attn_gain[...]).astype(jnp.bfloat16)
    pl.semaphore_wait(barrier, NODES)

    first = Gather(gather_q, 0, 2)
    first.cross(block(gather_q, node))
    first.begin(block(gather_q, node))
    for i in (0, 1, 2):
        shared[i].start()

    def group_rows(group):
        return pl.ds(pl.multiple_of(group * 64, 64), 64)

    def project(group):
        inputs = gather_q[group_rows(group), :]
        q = jnp.dot(inputs, w_query_v[...], preferred_element_type=jnp.float32)
        kv = lax.dot_general(
            inputs, w_kv_v[...], (((1,), (1,)), ((), ())), preferred_element_type=jnp.float32
        )
        kv = kv.reshape(QUADS, ROWS, 64)
        kv = jnp.concatenate([kv[:, 0:8, :], kv[:, 8:16, :]], axis=-1)
        at = pl.ds(group * QUADS, QUADS)
        parts[at, 0:ROWS, :] = q[:, 0:128].reshape(QUADS, ROWS, 128)
        parts[at, ROWS : 2 * ROWS, :] = q[:, 128:256].reshape(QUADS, ROWS, 128)
        parts[at, 2 * ROWS : 2 * ROWS + 8, :] = kv

    def w_start():
        for m in mates:
            rdma(
                w_output.at[:, lanes_of(m % QUADS, wide)],
                w_cols.at[w_rows, :],
                a2a_sem.at[4],
                a2a_sem.at[5],
                device(m),
            ).start()

    def w_all():
        ref = w_cols.at[0:384, :]
        return rdma(ref, ref, a2a_sem.at[4], a2a_sem.at[5], device(mirror))

    def gates_start():
        mine = block(gates_all, node)
        for m in others:
            rdma(mine, mine, a2a_sem.at[6], a2a_sem.at[7], device(m)).start()

    def gates_wait():
        ref = gates_all.at[0 : 7 * ROWS, :]
        rdma(ref, ref, a2a_sem.at[6], a2a_sem.at[7], device(mirror)).wait()

    first.forward()
    for i in (0, 1, 2):
        local[i].wait()
        shared[i].wait_recv()
    first.near_ready()
    project(half)
    heads = Scatter(parts, own_parts, 0)
    heads.start(mates)
    own_parts[node] = parts[node]

    for copy in small[2:]:
        copy.wait()
    row_id = lax.broadcasted_iota(jnp.int32, (ROWS, 128), 0)
    lane_id = lax.broadcasted_iota(jnp.int32, (ROWS, 128), 1)
    chosen = jnp.concatenate([routes[:, 0, :], routes[:, 1, :]], axis=0)
    shares = jnp.concatenate([gate_weights[0], gate_weights[1]], axis=0)
    weighed = jnp.zeros((ROWS, 128), jnp.float32)
    for k in range(TOPK):
        weighed = jnp.where(lane_id == chosen[:, k : k + 1], shares[:, k : k + 1], weighed)
    block(gates_all, node)[...] = weighed
    slot_of = jnp.zeros((ROWS, 128), jnp.int32)
    for b in range(8):
        slot_of = jnp.where(row_id % 8 == b, slots[b], slot_of)
    limits = [jnp.where(slot_of == p, lengths[p], 0) for p in range(2)]
    phases = (limits[0] + limits[1] + row_id // 8).astype(jnp.float32) * rates[...]
    cosine = jnp.cos(phases)
    sine = jnp.sin(phases)
    sine = jnp.where(lane_id < 64, -sine, sine)

    first.far_ready()
    project(1 - half)
    heads.start(across)
    w_start()
    shared[3].start()
    shared[4].start()
    first.finish()
    heads.arrived()

    def turned(vectors):
        return vectors * cosine + pltpu.roll(vectors, 64, 1) * sine

    for j in range(NODES):
        for cc in range(2):
            h = 2 * j + cc
            queries[h * ROWS : (h + 1) * ROWS, :] = turned(
                own_parts[j, cc * ROWS : (cc + 1) * ROWS, :]
            ).astype(jnp.bfloat16)
        packed = own_parts[j, 2 * ROWS : 2 * ROWS + 8, :]
        unpacked = jnp.concatenate([packed[:, 0:64], packed[:, 64:128]], axis=0)
        fresh_k[:, j * 32 : (j + 1) * 32] = unpacked[:, 0:32]
        fresh_v[:, j * 32 : (j + 1) * 32] = unpacked[:, 32:64]
    local[5].wait()
    local[6].wait()
    inv_root = 1.0 / math.sqrt(HD)
    group_size = HQ // KVH
    q_rows = group_size * ROWS
    span = keys_v.shape[1]
    far_pos = lax.broadcasted_iota(jnp.int32, (q_rows, span), 1)
    row_at = lax.broadcasted_iota(jnp.int32, (q_rows, ROWS), 0) % ROWS
    col_at = lax.broadcasted_iota(jnp.int32, (q_rows, ROWS), 1)
    own_seen = (row_at % 8 == col_at % 8) & (col_at // 8 <= row_at // 8)
    limits = [jnp.concatenate([m[:, 0:1]] * group_size, axis=0) for m in limits]

    def attend(k):
        lanes = lanes_of(k, HD)
        new_keys = turned(fresh_k[:, lanes]).astype(jnp.bfloat16)
        new_values = fresh_v[:, lanes].astype(jnp.bfloat16)
        appended[:, lanes] = new_keys
        appended[:, lanes_of(KVH + k, HD)] = new_values
        q = queries[pl.ds(pl.multiple_of(k * q_rows, q_rows), q_rows), :]

        def against(rows):
            return (
                lax.dot_general(
                    q, rows, (((1,), (1,)), ((), ())), preferred_element_type=jnp.float32
                )
                * inv_root
            )

        scores = [
            jnp.where(far_pos < limits[p], against(keys_v[p, :, lanes]), -1e30) for p in range(2)
        ]
        own_scores = jnp.where(own_seen, against(new_keys), -1e30)
        peak = jnp.maximum(
            jnp.maximum(
                jnp.max(scores[0], axis=1, keepdims=True), jnp.max(scores[1], axis=1, keepdims=True)
            ),
            jnp.max(own_scores, axis=1, keepdims=True),
        )
        weights = [jnp.exp(s - peak) for s in scores]
        own_weights = jnp.exp(own_scores - peak)
        total = (
            jnp.sum(weights[0], axis=1, keepdims=True)
            + jnp.sum(weights[1], axis=1, keepdims=True)
            + jnp.sum(own_weights, axis=1, keepdims=True)
        )
        scale = 1.0 / total
        attended = jnp.dot(
            (own_weights * scale).astype(jnp.bfloat16),
            new_values,
            preferred_element_type=jnp.float32,
        )
        for p in range(2):
            attended = attended + jnp.dot(
                (weights[p] * scale).astype(jnp.bfloat16),
                values_v[p, :, lanes],
                preferred_element_type=jnp.float32,
            )
        attended = attended.astype(jnp.bfloat16)
        for g in range(group_size):
            attended_v[k, :, g * HD : (g + 1) * HD] = attended[g * ROWS : (g + 1) * ROWS, :]

    second = Gather(gather_o, 1, 1)
    attend(1 - half)
    second.cross(attended_v.at[1 - half])
    attend(half)
    second.begin(attended_v.at[half])
    block(gather_o, node)[...] = attended_v[half]
    gates_start()
    heads.sent()

    def w_pass(q, core):
        rows = w_cols.at[pl.ds(pl.multiple_of((2 * q + core) * 128, 128), 128), :]
        return rdma(rows, rows, twin_send.at[5], twin_recv.at[5], twin)

    def w_pass_all():
        return rdma(w_cols.at[0:512, :], w_cols.at[0:512, :], twin_send.at[5], twin_recv.at[5], twin)

    local[7].wait()
    w_pass(quad, c).start()
    w_all().wait_recv()
    for m in mates:
        w_pass(m % QUADS, c).start()
    second.forward()
    w_pass_all().wait_recv()

    def out_project(group):
        cols[group_rows(group), :] = jnp.dot(
            gather_o[group_rows(group), :], w_cols[...], preferred_element_type=jnp.float32
        )

    second.near_ready()
    out_project(half)
    columns = Scatter(cols, own_cols, 1)
    columns.start(mates)
    block(own_cols, node)[...] = block(cols, node)[...]
    second.far_ready()
    out_project(1 - half)
    columns.start(across)
    second.finish()
    w_all().wait_send()
    w_pass_all().wait_send()
    columns.arrived()
    for q in range(QUADS):
        lanes = slice(q * wide, (q + 1) * wide)
        hidden[:, lanes] = states[:, lanes] + (
            own_cols[q * ROWS : (q + 1) * ROWS, :]
            + own_cols[(q + QUADS) * ROWS : (q + QUADS + 1) * ROWS, :]
        )
    block(gather_m, node)[...] = norm_rows(hidden[...], moe_gain[...]).astype(jnp.bfloat16)

    third = Gather(gather_m, 2, 2)
    third.cross(block(gather_m, node))
    third.begin(block(gather_m, node))
    columns.sent()
    gates_wait()
    for i in (3, 4):
        local[i].wait()
        shared[i].wait_recv()

    def code_of(largest):
        return jnp.ceil(jnp.log2(jnp.maximum(largest, 1e-30)) * CODE_STEPS)

    def encode(values, ref):
        code = code_of(jnp.max(jnp.abs(values), axis=1, keepdims=True))
        factor = jnp.exp2(CODE_TOP - code * (1.0 / CODE_STEPS))
        ref[:, 0:wide] = jnp.round(values * factor).astype(jnp.int32).astype(jnp.int16)
        ref[:, wide : wide + 128] = jnp.broadcast_to(
            code.astype(jnp.int32), (values.shape[0], 128)
        ).astype(jnp.int16)

    def decode(ref):
        values = ref[...]
        code = values[:, wide : wide + 1].astype(jnp.int32).astype(jnp.float32)
        factor = jnp.exp2(code * (1.0 / CODE_STEPS) - CODE_TOP)
        return values[:, :wide].astype(jnp.int32).astype(jnp.float32) * factor

    all_rows = NODES * ROWS
    all_lane = lax.broadcasted_iota(jnp.int32, (all_rows, 128), 1)

    def gate_up():
        for e in range(2):

            @pl.loop(0, ff // 256)
            def _(t):
                at = pl.multiple_of(t * 256, 256)
                inputs = gather_m[...]
                g = jnp.dot(
                    inputs, gate_up_v[e, :, pl.ds(at, 256)], preferred_element_type=jnp.float32
                )
                u = jnp.dot(
                    inputs,
                    gate_up_v[e, :, pl.ds(pl.multiple_of(ff + t * 256, 256), 256)],
                    preferred_element_type=jnp.float32,
                )
                act[e, :, pl.ds(at, 256)] = (g / (1.0 + jnp.exp(-g)) * u).astype(jnp.bfloat16)

    def part_lanes(part):
        return slice(part * wide, (part + 1) * wide)

    def down(part):
        total = jnp.zeros((all_rows, wide), jnp.float32)
        for e in range(2):
            got = jnp.dot(
                act[e], down_v[e, :, part_lanes(part)], preferred_element_type=jnp.float32
            )
            got = got.astype(jnp.bfloat16).astype(jnp.float32)
            total = total + jnp.where(share[e] > 0.0, share[e] * got, 0.0)
        mix[:, part_lanes(part)] = total

    def encode_rows(part, group):
        for q in range(QUADS):
            rows = pl.ds(pl.multiple_of((group * QUADS + q) * ROWS, ROWS), ROWS)
            encode(mix[rows, part_lanes(part)], coded.at[part, rows, :])

    class Return:
        def __init__(self, dst, send, recv, shift):
            self.dst, self.send, self.recv, self.shift = dst, ret_sem.at[send], recv, shift

        def start(self, part):
            for m in mates:
                rdma(
                    block(coded.at[part], (m + self.shift) % NODES),
                    self.dst.at[part, quad],
                    self.send,
                    ret_sem.at[self.recv + part],
                    device(m),
                ).start()

        def arrived(self, part):
            ref = self.dst.at[part, 0:3]
            rdma(ref, ref, self.send, ret_sem.at[self.recv + part], device(mirror)).wait_recv()

        def sent(self):
            ref = self.dst.at[:, 0:3]
            rdma(ref, ref, self.send, self.send, device(mirror)).wait_send()

    third.forward()
    third.near_ready()
    gates = gates_all[...]
    share = [
        jnp.sum(jnp.where(all_lane == 2 * node + e, gates, 0.0), axis=1, keepdims=True)
        for e in range(2)
    ]
    third.far_ready()
    gate_up()
    home = Return(near_in, 0, 3, 0)
    relay = Return(relay_in, 1, 7, QUADS)
    for part in range(QUADS):
        down(part)
        encode_rows(part, 1 - half)
        relay.start(part)
    for part in range(QUADS):
        encode_rows(part, half)
        if part < 2:
            home.start(part)
    third.finish()

    def last(part):
        return rdma(
            mirror_out.at[part],
            mirror_in.at[part],
            ret_sem.at[2],
            ret_sem.at[11 + part],
            device(mirror),
        )

    for part in range(QUADS):
        relay.arrived(part)
        total = block(mix, mirror)[:, part_lanes(part)]
        for m in mates:
            total = total + decode(relay_in.at[part, m % QUADS])
        encode(total, mirror_out.at[part])
        last(part).start()
        if part < 2:
            home.start(2 + part)
    for part in range(QUADS):
        lanes = part_lanes(part)
        home.arrived(part)
        total = hidden[:, lanes] + block(mix, node)[:, lanes]
        for m in mates:
            total = total + decode(near_in.at[part, m % QUADS])
        hidden[:, lanes] = total
    home.sent()
    relay.sent()
    for copy in shared:
        copy.wait_send()
    for part in range(QUADS):
        last(part).wait_recv()
        lanes = part_lanes(part)
        out[:, lanes] = hidden[:, lanes] + decode(mirror_in.at[part])
    rdma(mirror_out, mirror_in, ret_sem.at[2], ret_sem.at[2], device(mirror)).wait_send()


def tuned(
    states,
    attn_gain,
    moe_gain,
    w_query,
    w_key,
    w_value,
    w_output,
    w_gate_up,
    w_down,
    key_cache,
    value_cache,
    cache_lengths,
    prefix_slot,
    routes,
    gate_weights,
):
    step_count, row_count, width = states.shape
    rows = step_count * row_count
    prefix_count, span, kv_width = key_cache.shape
    ff = w_down.shape[1]
    rates = np.tile(THETA ** (-(np.arange(HD // 2) * 2.0 / HD)), 2)
    rates = jnp.asarray(rates.astype(np.float32).reshape(1, HD))
    in_hbm = pl.BlockSpec(memory_space=pl.ANY)
    everyone = NODES * rows
    coded_width = width // QUADS + 128
    bf16, f32, i16 = jnp.bfloat16, jnp.float32, jnp.int16
    out, appended = pl.pallas_call(
        layer_kernel,
        out_shape=(
            pltpu.VMEM((rows, width), f32),
            pltpu.VMEM((rows, 2 * kv_width), bf16),
        ),
        in_specs=[in_hbm] * 16,
        scratch_shapes=[
            pltpu.VMEM((rows, width), f32),
            pltpu.VMEM((1, width), f32),
            pltpu.VMEM((1, width), f32),
            pltpu.VMEM((1, HD), f32),
            pltpu.SMEM(cache_lengths.shape, jnp.int32),
            pltpu.SMEM(prefix_slot.shape, jnp.int32),
            pltpu.VMEM(routes.shape, jnp.int32),
            pltpu.VMEM(gate_weights.shape, f32),
            pltpu.VMEM((width, 256), bf16),
            pltpu.VMEM((64, width), bf16),
            pltpu.VMEM((everyone, 128), f32),
            pltpu.VMEM((everyone, width), bf16),
            pltpu.VMEM((everyone, width // 2), bf16),
            pltpu.VMEM((everyone, width), bf16),
            pltpu.VMEM((2, rows, width // 2), bf16),
            pltpu.VMEM((NODES, 2 * rows + 8, 128), f32),
            pltpu.VMEM((NODES, 2 * rows + 8, 128), f32),
            pltpu.VMEM((width // 2, width // QUADS), bf16),
            pltpu.VMEM((everyone, width // QUADS), f32),
            pltpu.VMEM((everyone, width // QUADS), f32),
            pltpu.VMEM((rows, width), f32),
            pltpu.VMEM((2, everyone, ff), bf16),
            pltpu.VMEM((everyone, width), f32),
            pltpu.VMEM((QUADS, everyone, coded_width), i16),
            pltpu.VMEM((QUADS, QUADS, rows, coded_width), i16),
            pltpu.VMEM((QUADS, QUADS, rows, coded_width), i16),
            pltpu.VMEM((QUADS, rows, coded_width), i16),
            pltpu.VMEM((QUADS, rows, coded_width), i16),
            pltpu.VMEM((rows, kv_width), f32),
            pltpu.VMEM((rows, kv_width), f32),
            pltpu.VMEM((HQ * rows, HD), bf16),
            pltpu.VMEM((2, width, 2 * ff), bf16),
            pltpu.VMEM((2, ff, width), bf16),
            pltpu.VMEM((prefix_count, span, kv_width), bf16),
            pltpu.VMEM((prefix_count, span, kv_width), bf16),
            pltpu.SemaphoreType.DMA((8,)),
            pltpu.SemaphoreType.DMA((8,)),
            pltpu.SemaphoreType.DMA((6,)),
            pltpu.SemaphoreType.DMA((6,)),
            pltpu.SemaphoreType.DMA((18,)),
            pltpu.SemaphoreType.DMA((8,)),
            pltpu.SemaphoreType.DMA((15,)),
        ],
        compiler_params=pltpu.CompilerParams(
            collective_id=0, has_side_effects=True, vmem_limit_bytes=56 * 1024 * 1024
        ),
    )(
        states.reshape(rows, width),
        attn_gain.reshape(1, width),
        moe_gain.reshape(1, width),
        rates,
        cache_lengths,
        prefix_slot,
        routes,
        gate_weights,
        w_query,
        w_key.T,
        w_value.T,
        w_output,
        w_gate_up[0],
        w_down[0],
        key_cache,
        value_cache,
    )
    return (
        out.reshape(step_count, row_count, width),
        appended.reshape(step_count, row_count, 2 * kv_width),
    )


def solution(mesh):
    return jax.shard_map(
        tuned if mesh.shape["ep"] == TUNED_DEVICES else shards,
        mesh=mesh,
        in_specs=(
            P(None, ("groups", "ep"), None),
            P(),
            P(),
            P(None, "ep"),
            P(None, "ep"),
            P(None, "ep"),
            P("ep", None),
            P("ep", None, None),
            P("ep", None, None),
            P(("groups", "ep"), None, None),
            P(("groups", "ep"), None, None),
            P(("groups", "ep")),
            P(("groups", "ep")),
            P(("groups", "ep"), None, None),
            P(None, ("groups", "ep"), None),
        ),
        out_specs=(P(None, ("groups", "ep"), None), P(None, ("groups", "ep"), None)),
        check_vma=False,
    )
```

```python
import math

import jax
import jax.numpy as jnp
import numpy as np
from jax import lax
from jax.experimental import pallas as pl
from jax.experimental.pallas import tpu as pltpu
from jax.sharding import PartitionSpec as P

HQ = 16
KVH = 2
HD = 128
TOPK = 8


EPS = 1e-06
THETA = 1000000.0


def rms_scale(values, gain):
    squares = jnp.mean(values * values, axis=-1, keepdims=True)
    return values * lax.rsqrt(squares + EPS) * gain


def rotate(vectors, positions):
    head_size = vectors.shape[-1]
    half_size = head_size // 2
    inverse_rate = THETA ** (-(jnp.arange(half_size).astype(jnp.float32) * 2.0 / head_size))
    phases = positions[..., None, None] * inverse_rate
    cosine = jnp.cos(phases)
    sine_part = jnp.sin(phases)
    first_half = vectors[..., :half_size]
    second_half = vectors[..., half_size:]
    return jnp.concatenate(
        [
            first_half * cosine - second_half * sine_part,
            second_half * cosine + first_half * sine_part,
        ],
        axis=-1,
    )


def attend_block(queries, new_keys, new_values, key_block, value_block, lengths, slots):
    step_count, row_count, head_count, head_size = queries.shape
    prefix_count, cache_span, kv_heads, _ = key_block.shape
    group_size = head_count // kv_heads
    grouped = queries.reshape(step_count, row_count, kv_heads, group_size, head_size)
    inv_root = 1.0 / math.sqrt(head_size)
    far_scores = (
        jnp.einsum("srkgd,pckd->srkgpc", grouped, key_block, preferred_element_type=jnp.float32)
        * inv_root
    )
    visible = (jnp.arange(cache_span)[None, None, :] < lengths[None, :, None]) & (
        slots[:, None, None] == jnp.arange(prefix_count)[None, :, None]
    )
    far_scores = jnp.where(visible[None, :, None, None], far_scores, -1e30)
    own_scores = (
        jnp.einsum("srkgd,trkd->srkgt", grouped, new_keys, preferred_element_type=jnp.float32)
        * inv_root
    )
    causal = jnp.arange(step_count)[None, :] <= jnp.arange(step_count)[:, None]
    own_scores = jnp.where(causal[:, None, None, None, :], own_scores, -1e30)
    peak = jnp.maximum(jnp.max(far_scores, axis=(-2, -1)), jnp.max(own_scores, axis=-1))
    far_weights = jnp.exp(far_scores - peak[..., None, None])
    own_weights = jnp.exp(own_scores - peak[..., None])
    normalizer = jnp.sum(far_weights, axis=(-2, -1)) + jnp.sum(own_weights, axis=-1)
    far_probs = (far_weights / normalizer[..., None, None]).astype(jnp.bfloat16)
    own_probs = (own_weights / normalizer[..., None]).astype(jnp.bfloat16)
    attended = jnp.einsum(
        "srkgpc,pckd->srkgd", far_probs, value_block, preferred_element_type=jnp.float32
    )
    attended = attended + jnp.einsum(
        "srkgt,trkd->srkgd", own_probs, new_values, preferred_element_type=jnp.float32
    )
    return attended.reshape(step_count, row_count, head_count * head_size).astype(jnp.bfloat16)


def shards(
    states,
    attn_gain,
    moe_gain,
    w_query,
    w_key,
    w_value,
    w_output,
    w_gate_up,
    w_down,
    key_cache,
    value_cache,
    cache_lengths,
    prefix_slot,
    routes,
    gate_weights,
):
    devices = lax.axis_size("ep")
    step_count, row_count, model_width = states.shape
    query_cols = w_query.shape[1]
    kv_cols = w_key.shape[1]
    normed = rms_scale(states, attn_gain).astype(jnp.bfloat16)
    joined = jnp.concatenate([w_query, w_key, w_value], axis=1)
    head_parts = jnp.einsum(
        "srd,dc->src",
        lax.all_gather(normed, "ep", axis=1, tiled=True),
        joined,
        preferred_element_type=jnp.float32,
    )
    own_cols = lax.all_to_all(head_parts, "ep", split_axis=1, concat_axis=2, tiled=True)
    own_cols = own_cols.reshape(step_count, row_count, devices, query_cols + 2 * kv_cols)
    queries = own_cols[..., :query_cols].reshape(step_count, row_count, HQ, HD)
    new_keys = own_cols[..., query_cols : query_cols + kv_cols].reshape(
        step_count, row_count, KVH, HD
    )
    new_values = (
        own_cols[..., query_cols + kv_cols :]
        .reshape(step_count, row_count, KVH, HD)
        .astype(jnp.bfloat16)
    )
    prefix_count, cache_span, _ = key_cache.shape
    lengths_here = jnp.sum(
        jnp.where(
            prefix_slot[:, None] == jnp.arange(prefix_count)[None, :], cache_lengths[None, :], 0
        ),
        axis=1,
    )
    positions = (
        lengths_here.astype(jnp.float32)[None, :]
        + jnp.arange(step_count).astype(jnp.float32)[:, None]
    )
    queries = rotate(queries, positions).astype(jnp.bfloat16)
    new_keys = rotate(new_keys, positions).astype(jnp.bfloat16)
    attended = attend_block(
        queries,
        new_keys,
        new_values,
        key_cache.reshape(prefix_count, cache_span, KVH, HD),
        value_cache.reshape(prefix_count, cache_span, KVH, HD),
        cache_lengths,
        prefix_slot,
    )
    w_columns = lax.all_to_all(w_output, "ep", split_axis=1, concat_axis=0, tiled=True)
    column_part = jnp.einsum(
        "srf,fc->src",
        lax.all_gather(attended, "ep", axis=1, tiled=True),
        w_columns,
        preferred_element_type=jnp.float32,
    )
    projected = lax.all_to_all(column_part, "ep", split_axis=1, concat_axis=2, tiled=True)
    hidden = states + projected
    moe_input = (
        rms_scale(hidden, moe_gain)
        .astype(jnp.bfloat16)
        .reshape(step_count * row_count, model_width)
    )
    expert_count = w_gate_up.shape[0] * devices
    capacity = max(2, 4 * row_count * TOPK // expert_count)
    flat_routes = jnp.swapaxes(routes, 0, 1).reshape(-1)
    order = jnp.arange(flat_routes.shape[0])
    earlier = (flat_routes[:, None] == flat_routes[None, :]) & (order[None, :] < order[:, None])
    within = jnp.sum(earlier.astype(jnp.int32), axis=1)
    slot_index = flat_routes * capacity + within
    dispatch = (jnp.arange(expert_count * capacity)[:, None] == slot_index[None, :]).astype(
        jnp.bfloat16
    )
    repeated = jnp.repeat(moe_input, TOPK, axis=0)
    outgoing = jnp.dot(dispatch, repeated, preferred_element_type=jnp.float32).astype(jnp.bfloat16)
    outgoing = outgoing.reshape(expert_count, capacity, model_width)
    both = jnp.einsum(
        "nsd,df->nsf",
        lax.all_to_all(outgoing, "ep", split_axis=0, concat_axis=0, tiled=True),
        w_gate_up[0],
        preferred_element_type=jnp.float32,
    )
    half_cols = both.shape[-1] // 2
    activation = (jax.nn.silu(both[..., :half_cols]) * both[..., half_cols:]).astype(jnp.bfloat16)
    expert_done = jnp.einsum(
        "nsf,fd->nsd", activation, w_down[0], preferred_element_type=jnp.float32
    ).astype(jnp.bfloat16)
    returned = lax.all_to_all(expert_done, "ep", split_axis=0, concat_axis=0, tiled=True)
    picked = returned.reshape(expert_count * capacity, model_width)[slot_index]
    picked = picked.astype(jnp.float32).reshape(step_count, row_count, TOPK, model_width)
    mixture = jnp.sum(gate_weights[..., None] * picked, axis=2)
    appended = jnp.concatenate(
        [
            new_keys.reshape(step_count, row_count, KVH * HD),
            new_values.reshape(step_count, row_count, KVH * HD),
        ],
        axis=-1,
    )
    return (hidden + mixture, appended)


TUNED_DEVICES = 16
ROWS = 16
NODES = 8
QUADS = 4
CODE_TOP = 14.99
CODE_STEPS = 256.0


def norm_rows(values, gain):
    squares = jnp.mean(values * values, axis=-1, keepdims=True)
    return values * lax.rsqrt(squares + EPS) * gain


def layer_kernel(
    states_in,
    attn_gain_in,
    moe_gain_in,
    rates_in,
    lengths_in,
    slots_in,
    routes_in,
    gate_weights_in,
    w_query,
    w_key,
    w_value,
    w_output,
    w_gate_up,
    w_down,
    key_cache,
    value_cache,
    out,
    appended,
    states,
    attn_gain,
    moe_gain,
    rates,
    lengths,
    slots,
    routes,
    gate_weights,
    w_query_v,
    w_kv_v,
    gates_all,
    gather_q,
    gather_o,
    gather_m,
    attended_v,
    parts,
    parts_m,
    own_parts,
    w_cols,
    cols,
    cols_far,
    cols_out,
    cols_in,
    own_cols,
    hidden,
    act,
    mix,
    near_out,
    far_out,
    near_in,
    relay_in,
    mirror_out,
    mirror_in,
    fresh_k,
    fresh_v,
    queries,
    gate_up_v,
    down_v,
    keys_v,
    values_v,
    small_sem,
    load_sem,
    twin_send,
    twin_recv,
    ag_sem,
    a2a_sem,
    w_sem,
    ret_sem,
):
    me = lax.axis_index("ep")
    c = me % 2
    node = me // 2
    half = node // QUADS
    quad = node % QUADS
    twin = me + 1 - 2 * c
    group = lax.axis_index("groups")
    twin_group = {"groups": 1 - group, "ep": me}
    width = states.shape[1]
    wide = width // QUADS
    deep = width // 2
    ff = down_v.shape[1]

    def device(m):
        return m * 2 + c

    mates = [half * QUADS + (quad + i) % QUADS for i in range(1, QUADS)]
    mirror = (node + QUADS) % NODES
    across = [(1 - half) * QUADS + (quad + i) % QUADS for i in range(QUADS)]

    def block(ref, m):
        return ref.at[pl.ds(pl.multiple_of(m * ROWS, ROWS), ROWS), :]

    def rdma(src, dst, send, recv, target):
        return pltpu.make_async_remote_copy(
            src_ref=src,
            dst_ref=dst,
            send_sem=send,
            recv_sem=recv,
            device_id=target if isinstance(target, dict) else {"ep": target},
            device_id_type=pl.DeviceIdType.MESH,
        )

    barrier = pltpu.get_barrier_semaphore()
    partners = [{"ep": device((node + i) % NODES)} for i in range(1, NODES)]
    for target in partners + [{"ep": twin}, twin_group]:
        pl.semaphore_signal(
            barrier,
            inc=1,
            device_id=target,
            device_id_type=pl.DeviceIdType.MESH,
        )

    small = [
        pltpu.make_async_copy(s, d, small_sem.at[i])
        for i, (s, d) in enumerate(
            (
                (states_in, states),
                (attn_gain_in, attn_gain),
                (lengths_in, lengths),
                (slots_in, slots),
                (rates_in, rates),
                (routes_in, routes),
                (gate_weights_in, gate_weights),
                (moe_gain_in, moe_gain),
            )
        )
    ]
    for copy in small:
        copy.start()

    def lanes_of(index, size):
        return pl.ds(pl.multiple_of(index * size, size), size)

    def twin_pairs():
        return [
            (w_query, w_query_v.at[:, lanes_of(c, 128)]),
            (w_key, w_kv_v.at[pl.ds(pl.multiple_of(c * 16, 16), 16), :]),
            (w_value, w_kv_v.at[pl.ds(pl.multiple_of(32 + c * 16, 16), 16), :]),
            (w_gate_up, gate_up_v.at[c]),
            (w_down, down_v.at[c]),
        ]

    local = [pltpu.make_async_copy(s, d, load_sem.at[i]) for i, (s, d) in enumerate(twin_pairs())]
    shared = [
        rdma(s, d, twin_send.at[i], twin_recv.at[i], twin) for i, (s, d) in enumerate(twin_pairs())
    ]
    w_rows = pl.ds(pl.multiple_of((2 * quad + c) * 128, 128), 128)
    local += [
        pltpu.make_async_copy(key_cache, keys_v, load_sem.at[5]),
        pltpu.make_async_copy(value_cache, values_v, load_sem.at[6]),
        pltpu.make_async_copy(
            w_output.at[:, lanes_of(quad, wide)], w_cols.at[w_rows, :], load_sem.at[7]
        ),
    ]
    for i in (0, 1, 2, 5, 6, 7, 3, 4):
        local[i].start()

    class Gather:
        def __init__(self, buf, phase, chunks):
            self.buf, self.phase, self.chunks = buf, phase, chunks
            self.size = buf.shape[1] // chunks
            self.send = ag_sem.at[6 * phase]

        def lanes(self, part):
            if part == 0:
                return slice(None)
            return slice((part - 1) % 2 * self.size, ((part - 1) % 2 + 1) * self.size)

        def piece(self, m, part):
            return self.buf.at[pl.ds(pl.multiple_of(m * ROWS, ROWS), ROWS), self.lanes(part)]

        def push(self, src, m, part, target):
            landed = ag_sem.at[6 * self.phase + 1 + part]
            rdma(src, self.piece(m, part), self.send, landed, device(target)).start()

        def arrived(self, part, count):
            ref = self.buf.at[0 : count * ROWS, self.lanes(part)]
            landed = ag_sem.at[6 * self.phase + 1 + part]
            rdma(ref, ref, self.send, landed, device(mirror)).wait_recv()

        def cross(self, source):
            for part in range(1, 1 + self.chunks):
                self.push(source.at[:, self.lanes(part)], node, part, mirror)

        def begin(self, source):
            for m in mates:
                self.push(source, node, 0, m)

        def forward(self):
            for part in range(1, 1 + self.chunks):
                self.arrived(part, 1)
                for m in mates:
                    self.push(self.piece(mirror, part), mirror, part + 2, m)

        def near_ready(self):
            self.arrived(0, QUADS - 1)

        def far_ready(self):
            for part in range(3, 3 + self.chunks):
                self.arrived(part, QUADS - 1)

        def finish(self):
            ref = self.buf.at[0 : 7 * ROWS, :]
            rdma(ref, ref, self.send, self.send, device(mirror)).wait_send()

    class Scatter:
        def __init__(self, src, mirror_src, dst, phase):
            self.src, self.mirror_src, self.dst = src, mirror_src, dst
            self.send = a2a_sem.at[3 * phase]
            self.near, self.far = a2a_sem.at[3 * phase + 1], a2a_sem.at[3 * phase + 2]

        def pick(self, ref, m):
            return ref.at[m] if len(ref.shape) == 3 else block(ref, m)

        def push(self, src, m, recv):
            rdma(src, self.pick(self.dst, node), self.send, recv, device(m)).start()

        def to_mates(self):
            for m in mates:
                self.push(self.pick(self.src, m), m, self.near)

        def to_mirror(self):
            self.push(self.mirror_src, mirror, self.far)

        def to_far(self):
            for m in across[1:]:
                self.push(self.pick(self.src, m), m, self.far)

        def some(self, ref, count):
            return ref.at[0 : count if len(ref.shape) == 3 else count * ROWS]

        def near_ready(self):
            dst = self.some(self.dst, 3)
            rdma(dst, dst, self.send, self.near, device(mirror)).wait_recv()

        def far_ready(self):
            dst = self.some(self.dst, 4)
            rdma(dst, dst, self.send, self.far, device(mirror)).wait_recv()

        def sent(self):
            src = self.some(self.src, 7)
            rdma(src, src, self.send, self.far, device(mirror)).wait_send()

    others = mates + across

    small[0].wait()
    small[1].wait()
    block(gather_q, node)[...] = norm_rows(states[...], attn_gain[...]).astype(jnp.bfloat16)
    pl.semaphore_wait(barrier, NODES + 1)

    first = Gather(gather_q, 0, 2)
    first.cross(block(gather_q, node))
    first.begin(block(gather_q, node))
    for i in (0, 1, 2, 3):
        shared[i].start()

    def group_rows(group):
        return pl.ds(pl.multiple_of(group * 64, 64), 64)

    def project(rows, count):
        inputs = gather_q[rows, :]
        q = jnp.dot(inputs, w_query_v[...], preferred_element_type=jnp.float32)
        kv = lax.dot_general(
            inputs, w_kv_v[...], (((1,), (1,)), ((), ())), preferred_element_type=jnp.float32
        )
        kv = kv.reshape(count, ROWS, 64)
        kv = jnp.concatenate([kv[:, 0:8, :], kv[:, 8:16, :]], axis=-1)
        q = [q[:, 128 * i : 128 * i + 128].reshape(count, ROWS, 128) for i in range(2)]
        return jnp.concatenate(q + [kv], axis=1)

    def project_group(group):
        parts[pl.ds(group * QUADS, QUADS)] = project(group_rows(group), QUADS)

    mirror_rows = pl.ds(pl.multiple_of(mirror * ROWS, ROWS), ROWS)

    slim = wide // 2

    def w_piece(q, core, part):
        rows = pl.ds(pl.multiple_of((2 * q + core) * 128, 128), 128)
        return w_cols.at[rows, lanes_of(part, slim)]

    def w_start():
        for m in mates:
            at = pl.multiple_of(m % QUADS * wide + group * slim, slim)
            rdma(
                w_output.at[:, pl.ds(at, slim)],
                w_piece(quad, c, group),
                w_sem.at[0],
                w_sem.at[1 + quad],
                device(m),
            ).start()

    def w_arrived(m):
        piece = w_piece(m % QUADS, c, group)
        rdma(piece, piece, w_sem.at[0], w_sem.at[1 + m % QUADS], device(m)).wait_recv()

    def w_over(m):
        piece = w_piece(m % QUADS, c, group)
        rdma(piece, piece, w_sem.at[5], w_sem.at[6], twin_group).start()

    def w_three(send, recv):
        ref = w_cols.at[0:384, 0:slim]
        return rdma(ref, ref, w_sem.at[send], w_sem.at[recv], twin_group)

    def w_pass(m, part):
        piece = w_piece(m % QUADS, c, part)
        rdma(piece, piece, w_sem.at[7], w_sem.at[8], twin).start()

    def w_pass_all():
        ref = w_cols.at[0:512, :]
        return rdma(ref, ref, w_sem.at[7], w_sem.at[8], twin)

    def gates_start():
        mine = block(gates_all, node)
        for m in others:
            rdma(mine, mine, a2a_sem.at[6], a2a_sem.at[7], device(m)).start()

    def gates_wait():
        ref = gates_all.at[0 : 7 * ROWS, :]
        rdma(ref, ref, a2a_sem.at[6], a2a_sem.at[7], device(mirror)).wait()

    first.forward()
    for i in (0, 1, 2):
        local[i].wait()
        shared[i].wait_recv()
    first.near_ready()
    project_group(half)
    heads = Scatter(parts, parts_m.at[0], own_parts, 0)
    heads.to_mates()
    own_parts[node] = parts[node]
    parts_m[...] = project(mirror_rows, 1)
    heads.to_mirror()

    for copy in small[2:]:
        copy.wait()
    row_id = lax.broadcasted_iota(jnp.int32, (ROWS, 128), 0)
    lane_id = lax.broadcasted_iota(jnp.int32, (ROWS, 128), 1)
    chosen = jnp.concatenate([routes[:, 0, :], routes[:, 1, :]], axis=0)
    shares = jnp.concatenate([gate_weights[0], gate_weights[1]], axis=0)
    weighed = jnp.zeros((ROWS, 128), jnp.float32)
    for k in range(TOPK):
        weighed = jnp.where(lane_id == chosen[:, k : k + 1], shares[:, k : k + 1], weighed)
    block(gates_all, node)[...] = weighed
    slot_of = jnp.zeros((ROWS, 128), jnp.int32)
    for b in range(8):
        slot_of = jnp.where(row_id % 8 == b, slots[b], slot_of)
    limits = [jnp.where(slot_of == p, lengths[p], 0) for p in range(2)]
    phases = (limits[0] + limits[1] + row_id // 8).astype(jnp.float32) * rates[...]
    cosine = jnp.cos(phases)
    sine = jnp.sin(phases)
    sine = jnp.where(lane_id < 64, -sine, sine)

    first.far_ready()
    project_group(1 - half)
    heads.to_far()
    w_start()
    first.finish()

    def turned(vectors):
        return vectors * cosine + pltpu.roll(vectors, 64, 1) * sine

    def unpack(k):
        for q in range(QUADS):
            j = k * QUADS + q
            for i in range(2):
                at = (2 * q + i) * ROWS
                queries[k, at : at + ROWS, :] = turned(
                    own_parts[j, i * ROWS : (i + 1) * ROWS, :]
                ).astype(jnp.bfloat16)
            packed = own_parts[j, 2 * ROWS : 2 * ROWS + 8, :]
            unpacked = jnp.concatenate([packed[:, 0:64], packed[:, 64:128]], axis=0)
            fresh_k[k, :, q * 32 : (q + 1) * 32] = unpacked[:, 0:32]
            fresh_v[k, :, q * 32 : (q + 1) * 32] = unpacked[:, 32:64]

    local[5].wait()
    local[6].wait()
    inv_root = 1.0 / math.sqrt(HD)
    group_size = HQ // KVH
    q_rows = group_size * ROWS
    span = keys_v.shape[1]
    far_pos = lax.broadcasted_iota(jnp.int32, (q_rows, span), 1)
    row_at = lax.broadcasted_iota(jnp.int32, (q_rows, ROWS), 0) % ROWS
    col_at = lax.broadcasted_iota(jnp.int32, (q_rows, ROWS), 1)
    own_seen = (row_at % 8 == col_at % 8) & (col_at // 8 <= row_at // 8)
    limits = [jnp.concatenate([m[:, 0:1]] * group_size, axis=0) for m in limits]

    def attend(k):
        lanes = lanes_of(k, HD)
        new_keys = turned(fresh_k[k]).astype(jnp.bfloat16)
        new_values = fresh_v[k].astype(jnp.bfloat16)
        appended[:, lanes] = new_keys
        appended[:, lanes_of(KVH + k, HD)] = new_values
        q = queries[k]

        def against(rows):
            return (
                lax.dot_general(
                    q, rows, (((1,), (1,)), ((), ())), preferred_element_type=jnp.float32
                )
                * inv_root
            )

        scores = [
            jnp.where(far_pos < limits[p], against(keys_v[p, :, lanes]), -1e30) for p in range(2)
        ]
        own_scores = jnp.where(own_seen, against(new_keys), -1e30)
        peak = jnp.maximum(
            jnp.maximum(
                jnp.max(scores[0], axis=1, keepdims=True), jnp.max(scores[1], axis=1, keepdims=True)
            ),
            jnp.max(own_scores, axis=1, keepdims=True),
        )
        weights = [jnp.exp(s - peak) for s in scores]
        own_weights = jnp.exp(own_scores - peak)
        total = (
            jnp.sum(weights[0], axis=1, keepdims=True)
            + jnp.sum(weights[1], axis=1, keepdims=True)
            + jnp.sum(own_weights, axis=1, keepdims=True)
        )
        scale = 1.0 / total
        attended = jnp.dot(
            (own_weights * scale).astype(jnp.bfloat16),
            new_values,
            preferred_element_type=jnp.float32,
        )
        for p in range(2):
            attended = attended + jnp.dot(
                (weights[p] * scale).astype(jnp.bfloat16),
                values_v[p, :, lanes],
                preferred_element_type=jnp.float32,
            )
        attended = attended.astype(jnp.bfloat16)
        for g in range(group_size):
            attended_v[k, :, g * HD : (g + 1) * HD] = attended[g * ROWS : (g + 1) * ROWS, :]

    second = Gather(gather_o, 1, 1)
    heads.near_ready()
    unpack(half)
    attend(half)
    second.begin(attended_v.at[half])
    block(gather_o, node)[...] = attended_v[half]
    heads.far_ready()
    unpack(1 - half)
    attend(1 - half)
    second.cross(attended_v.at[1 - half])
    heads.sent()

    for m in mates:
        w_arrived(m)
        w_over(m)
        w_pass(m, group)
    local[7].wait()
    w_pass(node, 0)
    w_pass(node, 1)
    second.forward()
    w_three(5, 6).wait_recv()
    for m in mates:
        w_pass(m, 1 - group)
    w_pass_all().wait_recv()
    shared[4].start()

    def code_of(largest):
        return jnp.ceil(jnp.log2(jnp.maximum(largest, 1e-30)) * CODE_STEPS)

    def encode(values, ref):
        size = values.shape[1]
        code = code_of(jnp.max(jnp.abs(values), axis=1, keepdims=True))
        factor = jnp.exp2(CODE_TOP - code * (1.0 / CODE_STEPS))
        ref[:, 0:size] = jnp.round(values * factor).astype(jnp.int32).astype(jnp.int16)
        ref[:, size : size + 128] = jnp.broadcast_to(
            code.astype(jnp.int32), (values.shape[0], 128)
        ).astype(jnp.int16)

    def decode(ref):
        values = ref[...]
        size = values.shape[1] - 128
        code = values[:, size : size + 1].astype(jnp.int32).astype(jnp.float32)
        factor = jnp.exp2(code * (1.0 / CODE_STEPS) - CODE_TOP)
        return values[:, :size].astype(jnp.int32).astype(jnp.float32) * factor

    def out_project(rows):
        return jnp.dot(gather_o[rows, :], w_cols[...], preferred_element_type=jnp.float32)

    second.near_ready()
    def near_block(ref, m):
        return ref.at[pl.ds(pl.multiple_of(m % QUADS * ROWS, ROWS), ROWS), :]

    def columns_to(m):
        rdma(
            near_block(cols, m),
            near_block(own_cols, node),
            a2a_sem.at[3],
            a2a_sem.at[4],
            device(m),
        ).start()

    def columns_over(m):
        rdma(
            cols_out.at[m % QUADS],
            cols_in.at[quad],
            a2a_sem.at[5],
            a2a_sem.at[8],
            device(m),
        ).start()

    cols[...] = out_project(group_rows(half))
    for m in mates:
        columns_to(m)
    near_block(own_cols, node)[...] = near_block(cols, node)[...]
    encode(out_project(mirror_rows), cols_out.at[quad])
    columns_over(mirror)
    second.far_ready()
    cols_far[...] = out_project(group_rows(1 - half))
    for m in across[1:]:
        encode(near_block(cols_far, m)[...], cols_out.at[m % QUADS])
        columns_over(m)
    gates_start()
    second.finish()
    w_three(0, 0).wait_send()
    w_three(5, 6).wait_send()
    w_pass_all().wait_send()
    ref = own_cols.at[0 : 3 * ROWS, :]
    rdma(ref, ref, a2a_sem.at[3], a2a_sem.at[4], device(mirror)).wait()
    rdma(cols_out, cols_in, a2a_sem.at[5], a2a_sem.at[8], device(mirror)).wait()
    for q in range(QUADS):
        lanes = slice(q * wide, (q + 1) * wide)
        hidden[:, lanes] = states[:, lanes] + (
            own_cols[q * ROWS : (q + 1) * ROWS, :] + decode(cols_in.at[q])
        )
    block(gather_m, node)[...] = norm_rows(hidden[...], moe_gain[...]).astype(jnp.bfloat16)

    third = Gather(gather_m, 2, 2)
    third.cross(block(gather_m, node))
    third.begin(block(gather_m, node))
    gates_wait()

    all_rows = NODES * ROWS
    all_lane = lax.broadcasted_iota(jnp.int32, (all_rows, 128), 1)

    def gate_up():
        for e in range(2):

            @pl.loop(0, ff // 256)
            def _(t):
                at = pl.multiple_of(t * 256, 256)
                inputs = gather_m[...]
                g = jnp.dot(
                    inputs, gate_up_v[e, :, pl.ds(at, 256)], preferred_element_type=jnp.float32
                )
                u = jnp.dot(
                    inputs,
                    gate_up_v[e, :, pl.ds(pl.multiple_of(ff + t * 256, 256), 256)],
                    preferred_element_type=jnp.float32,
                )
                act[e, :, pl.ds(at, 256)] = (g / (1.0 + jnp.exp(-g)) * u).astype(jnp.bfloat16)

    def part_lanes(part):
        return slice(part * wide, (part + 1) * wide)

    def down(part):
        total = jnp.zeros((all_rows, wide), jnp.float32)
        for e in range(2):
            got = jnp.dot(
                act[e], down_v[e, :, part_lanes(part)], preferred_element_type=jnp.float32
            )
            got = got.astype(jnp.bfloat16).astype(jnp.float32)
            total = total + jnp.where(share[e] > 0.0, share[e] * got, 0.0)
        mix[:, part_lanes(part)] = total

    def encode_far(part):
        for q in range(QUADS):
            rows = pl.ds(pl.multiple_of(((1 - half) * QUADS + q) * ROWS, ROWS), ROWS)
            encode(mix[rows, part_lanes(part)], far_out.at[part, q])

    def encode_near():
        for q in range(QUADS):
            rows = pl.ds(pl.multiple_of((half * QUADS + q) * ROWS, ROWS), ROWS)
            encode(mix[rows, :], near_out.at[q])

    def relay_start(part):
        for m in mates:
            rdma(
                far_out.at[part, m % QUADS],
                relay_in.at[part, quad],
                ret_sem.at[0],
                ret_sem.at[1 + part],
                device(m),
            ).start()

    def relay_wait(part):
        ref = relay_in.at[part, 0:3]
        rdma(ref, ref, ret_sem.at[0], ret_sem.at[1 + part], device(mirror)).wait_recv()

    def home_start():
        for m in mates:
            rdma(
                near_out.at[m % QUADS],
                near_in.at[quad],
                ret_sem.at[5],
                ret_sem.at[6],
                device(m),
            ).start()

    third.forward()
    third.near_ready()
    gates = gates_all[...]
    share = [
        jnp.sum(jnp.where(all_lane == 2 * node + e, gates, 0.0), axis=1, keepdims=True)
        for e in range(2)
    ]
    third.far_ready()
    for i in (3, 4):
        local[i].wait()
        shared[i].wait_recv()
    gate_up()
    for part in range(QUADS):
        down(part)
        encode_far(part)
        relay_start(part)
    encode_near()
    home_start()
    third.finish()

    def last(part):
        return rdma(
            mirror_out.at[part],
            mirror_in.at[part],
            ret_sem.at[7],
            ret_sem.at[8 + part],
            device(mirror),
        )

    for part in range(QUADS):
        relay_wait(part)
        total = block(mix, mirror)[:, part_lanes(part)]
        for m in mates:
            total = total + decode(relay_in.at[part, m % QUADS])
        encode(total, mirror_out.at[part])
        last(part).start()
    ref = near_in.at[0:3]
    rdma(ref, ref, ret_sem.at[5], ret_sem.at[6], device(mirror)).wait()
    total = hidden[...] + block(mix, node)[...]
    for m in mates:
        total = total + decode(near_in.at[m % QUADS])
    hidden[...] = total
    ref = relay_in.at[:, 0:3]
    rdma(ref, ref, ret_sem.at[0], ret_sem.at[0], device(mirror)).wait_send()
    for copy in shared:
        copy.wait_send()
    for part in range(QUADS):
        last(part).wait_recv()
        lanes = part_lanes(part)
        out[:, lanes] = hidden[:, lanes] + decode(mirror_in.at[part])
    rdma(mirror_out, mirror_in, ret_sem.at[7], ret_sem.at[7], device(mirror)).wait_send()


def tuned(
    states,
    attn_gain,
    moe_gain,
    w_query,
    w_key,
    w_value,
    w_output,
    w_gate_up,
    w_down,
    key_cache,
    value_cache,
    cache_lengths,
    prefix_slot,
    routes,
    gate_weights,
):
    step_count, row_count, width = states.shape
    rows = step_count * row_count
    prefix_count, span, kv_width = key_cache.shape
    ff = w_down.shape[1]
    rates = np.tile(THETA ** (-(np.arange(HD // 2) * 2.0 / HD)), 2)
    rates = jnp.asarray(rates.astype(np.float32).reshape(1, HD))
    in_hbm = pl.BlockSpec(memory_space=pl.ANY)
    everyone = NODES * rows
    coded_width = width // QUADS + 128
    bf16, f32, i16 = jnp.bfloat16, jnp.float32, jnp.int16
    out, appended = pl.pallas_call(
        layer_kernel,
        out_shape=(
            pltpu.VMEM((rows, width), f32),
            pltpu.VMEM((rows, 2 * kv_width), bf16),
        ),
        in_specs=[in_hbm] * 16,
        scratch_shapes=[
            pltpu.VMEM((rows, width), f32),
            pltpu.VMEM((1, width), f32),
            pltpu.VMEM((1, width), f32),
            pltpu.VMEM((1, HD), f32),
            pltpu.SMEM(cache_lengths.shape, jnp.int32),
            pltpu.SMEM(prefix_slot.shape, jnp.int32),
            pltpu.VMEM(routes.shape, jnp.int32),
            pltpu.VMEM(gate_weights.shape, f32),
            pltpu.VMEM((width, 256), bf16),
            pltpu.VMEM((64, width), bf16),
            pltpu.VMEM((everyone, 128), f32),
            pltpu.VMEM((everyone, width), bf16),
            pltpu.VMEM((everyone, width // 2), bf16),
            pltpu.VMEM((everyone, width), bf16),
            pltpu.VMEM((2, rows, width // 2), bf16),
            pltpu.VMEM((NODES, 2 * rows + 8, 128), f32),
            pltpu.VMEM((1, 2 * rows + 8, 128), f32),
            pltpu.VMEM((NODES, 2 * rows + 8, 128), f32),
            pltpu.VMEM((width // 2, width // QUADS), bf16),
            pltpu.VMEM((QUADS * rows, width // QUADS), f32),
            pltpu.VMEM((QUADS * rows, width // QUADS), f32),
            pltpu.VMEM((QUADS, rows, coded_width), i16),
            pltpu.VMEM((QUADS, rows, coded_width), i16),
            pltpu.VMEM((QUADS * rows, width // QUADS), f32),
            pltpu.VMEM((rows, width), f32),
            pltpu.VMEM((2, everyone, ff), bf16),
            pltpu.VMEM((everyone, width), f32),
            pltpu.VMEM((QUADS, rows, width + 128), i16),
            pltpu.VMEM((QUADS, QUADS, rows, coded_width), i16),
            pltpu.VMEM((QUADS, rows, width + 128), i16),
            pltpu.VMEM((QUADS, QUADS, rows, coded_width), i16),
            pltpu.VMEM((QUADS, rows, coded_width), i16),
            pltpu.VMEM((QUADS, rows, coded_width), i16),
            pltpu.VMEM((2, rows, HD), f32),
            pltpu.VMEM((2, rows, HD), f32),
            pltpu.VMEM((2, HQ // 2 * rows, HD), bf16),
            pltpu.VMEM((2, width, 2 * ff), bf16),
            pltpu.VMEM((2, ff, width), bf16),
            pltpu.VMEM((prefix_count, span, kv_width), bf16),
            pltpu.VMEM((prefix_count, span, kv_width), bf16),
            pltpu.SemaphoreType.DMA((8,)),
            pltpu.SemaphoreType.DMA((8,)),
            pltpu.SemaphoreType.DMA((5,)),
            pltpu.SemaphoreType.DMA((5,)),
            pltpu.SemaphoreType.DMA((18,)),
            pltpu.SemaphoreType.DMA((9,)),
            pltpu.SemaphoreType.DMA((9,)),
            pltpu.SemaphoreType.DMA((12,)),
        ],
        compiler_params=pltpu.CompilerParams(
            collective_id=0, has_side_effects=True, vmem_limit_bytes=56 * 1024 * 1024
        ),
    )(
        states.reshape(rows, width),
        attn_gain.reshape(1, width),
        moe_gain.reshape(1, width),
        rates,
        cache_lengths,
        prefix_slot,
        routes,
        gate_weights,
        w_query,
        w_key.T,
        w_value.T,
        w_output,
        w_gate_up[0],
        w_down[0],
        key_cache,
        value_cache,
    )
    return (
        out.reshape(step_count, row_count, width),
        appended.reshape(step_count, row_count, 2 * kv_width),
    )


def solution(mesh):
    return jax.shard_map(
        tuned if mesh.shape["ep"] == TUNED_DEVICES else shards,
        mesh=mesh,
        in_specs=(
            P(None, ("groups", "ep"), None),
            P(),
            P(),
            P(None, "ep"),
            P(None, "ep"),
            P(None, "ep"),
            P("ep", None),
            P("ep", None, None),
            P("ep", None, None),
            P(("groups", "ep"), None, None),
            P(("groups", "ep"), None, None),
            P(("groups", "ep")),
            P(("groups", "ep")),
            P(("groups", "ep"), None, None),
            P(None, ("groups", "ep"), None),
        ),
        out_specs=(P(None, ("groups", "ep"), None), P(None, ("groups", "ep"), None)),
        check_vma=False,
    )
```

```python
import math

import jax
import jax.numpy as jnp
import numpy as np
from jax import lax
from jax.experimental import pallas as pl
from jax.experimental.pallas import tpu as pltpu
from jax.sharding import PartitionSpec as P

HQ = 16
KVH = 2
HD = 128
TOPK = 8


EPS = 1e-06
THETA = 1000000.0


def rms_scale(values, gain):
    squares = jnp.mean(values * values, axis=-1, keepdims=True)
    return values * lax.rsqrt(squares + EPS) * gain


def rotate(vectors, positions):
    head_size = vectors.shape[-1]
    half_size = head_size // 2
    inverse_rate = THETA ** (-(jnp.arange(half_size).astype(jnp.float32) * 2.0 / head_size))
    phases = positions[..., None, None] * inverse_rate
    cosine = jnp.cos(phases)
    sine_part = jnp.sin(phases)
    first_half = vectors[..., :half_size]
    second_half = vectors[..., half_size:]
    return jnp.concatenate(
        [
            first_half * cosine - second_half * sine_part,
            second_half * cosine + first_half * sine_part,
        ],
        axis=-1,
    )


def attend_block(queries, new_keys, new_values, key_block, value_block, lengths, slots):
    step_count, row_count, head_count, head_size = queries.shape
    prefix_count, cache_span, kv_heads, _ = key_block.shape
    group_size = head_count // kv_heads
    grouped = queries.reshape(step_count, row_count, kv_heads, group_size, head_size)
    inv_root = 1.0 / math.sqrt(head_size)
    far_scores = (
        jnp.einsum("srkgd,pckd->srkgpc", grouped, key_block, preferred_element_type=jnp.float32)
        * inv_root
    )
    visible = (jnp.arange(cache_span)[None, None, :] < lengths[None, :, None]) & (
        slots[:, None, None] == jnp.arange(prefix_count)[None, :, None]
    )
    far_scores = jnp.where(visible[None, :, None, None], far_scores, -1e30)
    own_scores = (
        jnp.einsum("srkgd,trkd->srkgt", grouped, new_keys, preferred_element_type=jnp.float32)
        * inv_root
    )
    causal = jnp.arange(step_count)[None, :] <= jnp.arange(step_count)[:, None]
    own_scores = jnp.where(causal[:, None, None, None, :], own_scores, -1e30)
    peak = jnp.maximum(jnp.max(far_scores, axis=(-2, -1)), jnp.max(own_scores, axis=-1))
    far_weights = jnp.exp(far_scores - peak[..., None, None])
    own_weights = jnp.exp(own_scores - peak[..., None])
    normalizer = jnp.sum(far_weights, axis=(-2, -1)) + jnp.sum(own_weights, axis=-1)
    far_probs = (far_weights / normalizer[..., None, None]).astype(jnp.bfloat16)
    own_probs = (own_weights / normalizer[..., None]).astype(jnp.bfloat16)
    attended = jnp.einsum(
        "srkgpc,pckd->srkgd", far_probs, value_block, preferred_element_type=jnp.float32
    )
    attended = attended + jnp.einsum(
        "srkgt,trkd->srkgd", own_probs, new_values, preferred_element_type=jnp.float32
    )
    return attended.reshape(step_count, row_count, head_count * head_size).astype(jnp.bfloat16)


def shards(
    states,
    attn_gain,
    moe_gain,
    w_query,
    w_key,
    w_value,
    w_output,
    w_gate_up,
    w_down,
    key_cache,
    value_cache,
    cache_lengths,
    prefix_slot,
    routes,
    gate_weights,
):
    devices = lax.axis_size("ep")
    step_count, row_count, model_width = states.shape
    query_cols = w_query.shape[1]
    kv_cols = w_key.shape[1]
    normed = rms_scale(states, attn_gain).astype(jnp.bfloat16)
    joined = jnp.concatenate([w_query, w_key, w_value], axis=1)
    head_parts = jnp.einsum(
        "srd,dc->src",
        lax.all_gather(normed, "ep", axis=1, tiled=True),
        joined,
        preferred_element_type=jnp.float32,
    )
    own_cols = lax.all_to_all(head_parts, "ep", split_axis=1, concat_axis=2, tiled=True)
    own_cols = own_cols.reshape(step_count, row_count, devices, query_cols + 2 * kv_cols)
    queries = own_cols[..., :query_cols].reshape(step_count, row_count, HQ, HD)
    new_keys = own_cols[..., query_cols : query_cols + kv_cols].reshape(
        step_count, row_count, KVH, HD
    )
    new_values = (
        own_cols[..., query_cols + kv_cols :]
        .reshape(step_count, row_count, KVH, HD)
        .astype(jnp.bfloat16)
    )
    prefix_count, cache_span, _ = key_cache.shape
    lengths_here = jnp.sum(
        jnp.where(
            prefix_slot[:, None] == jnp.arange(prefix_count)[None, :], cache_lengths[None, :], 0
        ),
        axis=1,
    )
    positions = (
        lengths_here.astype(jnp.float32)[None, :]
        + jnp.arange(step_count).astype(jnp.float32)[:, None]
    )
    queries = rotate(queries, positions).astype(jnp.bfloat16)
    new_keys = rotate(new_keys, positions).astype(jnp.bfloat16)
    attended = attend_block(
        queries,
        new_keys,
        new_values,
        key_cache.reshape(prefix_count, cache_span, KVH, HD),
        value_cache.reshape(prefix_count, cache_span, KVH, HD),
        cache_lengths,
        prefix_slot,
    )
    w_columns = lax.all_to_all(w_output, "ep", split_axis=1, concat_axis=0, tiled=True)
    column_part = jnp.einsum(
        "srf,fc->src",
        lax.all_gather(attended, "ep", axis=1, tiled=True),
        w_columns,
        preferred_element_type=jnp.float32,
    )
    projected = lax.all_to_all(column_part, "ep", split_axis=1, concat_axis=2, tiled=True)
    hidden = states + projected
    moe_input = (
        rms_scale(hidden, moe_gain)
        .astype(jnp.bfloat16)
        .reshape(step_count * row_count, model_width)
    )
    expert_count = w_gate_up.shape[0] * devices
    capacity = max(2, 4 * row_count * TOPK // expert_count)
    flat_routes = jnp.swapaxes(routes, 0, 1).reshape(-1)
    order = jnp.arange(flat_routes.shape[0])
    earlier = (flat_routes[:, None] == flat_routes[None, :]) & (order[None, :] < order[:, None])
    within = jnp.sum(earlier.astype(jnp.int32), axis=1)
    slot_index = flat_routes * capacity + within
    dispatch = (jnp.arange(expert_count * capacity)[:, None] == slot_index[None, :]).astype(
        jnp.bfloat16
    )
    repeated = jnp.repeat(moe_input, TOPK, axis=0)
    outgoing = jnp.dot(dispatch, repeated, preferred_element_type=jnp.float32).astype(jnp.bfloat16)
    outgoing = outgoing.reshape(expert_count, capacity, model_width)
    both = jnp.einsum(
        "nsd,df->nsf",
        lax.all_to_all(outgoing, "ep", split_axis=0, concat_axis=0, tiled=True),
        w_gate_up[0],
        preferred_element_type=jnp.float32,
    )
    half_cols = both.shape[-1] // 2
    activation = (jax.nn.silu(both[..., :half_cols]) * both[..., half_cols:]).astype(jnp.bfloat16)
    expert_done = jnp.einsum(
        "nsf,fd->nsd", activation, w_down[0], preferred_element_type=jnp.float32
    ).astype(jnp.bfloat16)
    returned = lax.all_to_all(expert_done, "ep", split_axis=0, concat_axis=0, tiled=True)
    picked = returned.reshape(expert_count * capacity, model_width)[slot_index]
    picked = picked.astype(jnp.float32).reshape(step_count, row_count, TOPK, model_width)
    mixture = jnp.sum(gate_weights[..., None] * picked, axis=2)
    appended = jnp.concatenate(
        [
            new_keys.reshape(step_count, row_count, KVH * HD),
            new_values.reshape(step_count, row_count, KVH * HD),
        ],
        axis=-1,
    )
    return (hidden + mixture, appended)


TUNED_DEVICES = 16
ROWS = 16
NODES = 8
QUADS = 4
CODE_TOP = 14.99
CODE_STEPS = 256.0


def norm_rows(values, gain):
    squares = jnp.mean(values * values, axis=-1, keepdims=True)
    return values * lax.rsqrt(squares + EPS) * gain


def layer_kernel(
    states_in,
    attn_gain_in,
    moe_gain_in,
    rates_in,
    lengths_in,
    slots_in,
    routes_in,
    gate_weights_in,
    w_query,
    w_key,
    w_value,
    w_output,
    w_gate_up,
    w_down,
    key_cache,
    value_cache,
    out,
    appended,
    states,
    attn_gain,
    moe_gain,
    rates,
    lengths,
    slots,
    routes,
    gate_weights,
    w_query_v,
    w_kv_v,
    gates_all,
    gather_q,
    gather_o,
    gather_m,
    attended_v,
    parts,
    parts_m,
    own_parts,
    w_cols,
    cols,
    cols_far,
    cols_out,
    cols_in,
    own_cols,
    hidden,
    act,
    mix,
    near_out,
    far_out,
    near_in,
    relay_in,
    mirror_out,
    mirror_in,
    fresh_k,
    fresh_v,
    queries,
    gate_up_v,
    down_v,
    keys_v,
    values_v,
    small_sem,
    load_sem,
    twin_send,
    twin_recv,
    ag_sem,
    a2a_sem,
    w_sem,
    ret_sem,
):
    me = lax.axis_index("ep")
    c = me % 2
    node = me // 2
    half = node // QUADS
    quad = node % QUADS
    twin = me + 1 - 2 * c
    group = lax.axis_index("groups")
    twin_group = {"groups": 1 - group, "ep": me}
    width = states.shape[1]
    wide = width // QUADS
    deep = width // 2
    ff = down_v.shape[1]

    def device(m):
        return m * 2 + c

    mate_y = node + 1 - 2 * (node % 2)
    mate_z = node + 2 - 4 * (quad // 2)
    mate_yz = mate_z + mate_y - node
    mates = [mate_y, mate_yz, mate_z]
    mirror = (node + QUADS) % NODES
    across = [mirror] + [(m + QUADS) % NODES for m in mates]

    def block(ref, m):
        return ref.at[pl.ds(pl.multiple_of(m * ROWS, ROWS), ROWS), :]

    def rdma(src, dst, send, recv, target):
        return pltpu.make_async_remote_copy(
            src_ref=src,
            dst_ref=dst,
            send_sem=send,
            recv_sem=recv,
            device_id=target if isinstance(target, dict) else {"ep": target},
            device_id_type=pl.DeviceIdType.MESH,
        )

    barrier = pltpu.get_barrier_semaphore()
    partners = [{"ep": device((node + i) % NODES)} for i in range(1, NODES)]
    for target in partners + [{"ep": twin}, twin_group]:
        pl.semaphore_signal(
            barrier,
            inc=1,
            device_id=target,
            device_id_type=pl.DeviceIdType.MESH,
        )

    small = [
        pltpu.make_async_copy(s, d, small_sem.at[i])
        for i, (s, d) in enumerate(
            (
                (states_in, states),
                (attn_gain_in, attn_gain),
                (lengths_in, lengths),
                (slots_in, slots),
                (rates_in, rates),
                (routes_in, routes),
                (gate_weights_in, gate_weights),
                (moe_gain_in, moe_gain),
            )
        )
    ]
    for copy in small:
        copy.start()

    def lanes_of(index, size):
        return pl.ds(pl.multiple_of(index * size, size), size)

    def twin_pairs():
        return [
            (w_query, w_query_v.at[:, lanes_of(c, 128)]),
            (w_key, w_kv_v.at[pl.ds(pl.multiple_of(c * 16, 16), 16), :]),
            (w_value, w_kv_v.at[pl.ds(pl.multiple_of(32 + c * 16, 16), 16), :]),
            (w_gate_up, gate_up_v.at[c]),
            (w_down, down_v.at[c]),
        ]

    local = [pltpu.make_async_copy(s, d, load_sem.at[i]) for i, (s, d) in enumerate(twin_pairs())]
    shared = [
        rdma(s, d, twin_send.at[i], twin_recv.at[i], twin) for i, (s, d) in enumerate(twin_pairs())
    ]
    w_rows = pl.ds(pl.multiple_of((2 * quad + c) * 128, 128), 128)
    local += [
        pltpu.make_async_copy(key_cache, keys_v, load_sem.at[5]),
        pltpu.make_async_copy(value_cache, values_v, load_sem.at[6]),
        pltpu.make_async_copy(
            w_output.at[:, lanes_of(quad, wide)], w_cols.at[w_rows, :], load_sem.at[7]
        ),
    ]
    for i in (0, 1, 2, 5, 6, 7, 3, 4):
        local[i].start()

    class Gather:
        def __init__(self, buf, phase, chunks):
            self.buf, self.phase, self.chunks = buf, phase, chunks
            self.size = buf.shape[1] // chunks
            self.send = ag_sem.at[6 * phase]

        def lanes(self, part):
            if part == 0:
                return slice(None)
            return slice((part - 1) % 2 * self.size, ((part - 1) % 2 + 1) * self.size)

        def piece(self, m, part):
            return self.buf.at[pl.ds(pl.multiple_of(m * ROWS, ROWS), ROWS), self.lanes(part)]

        def push(self, src, m, part, target):
            landed = ag_sem.at[6 * self.phase + 1 + part]
            rdma(src, self.piece(m, part), self.send, landed, device(target)).start()

        def arrived(self, part, count):
            ref = self.buf.at[0 : count * ROWS, self.lanes(part)]
            landed = ag_sem.at[6 * self.phase + 1 + part]
            rdma(ref, ref, self.send, landed, device(mirror)).wait_recv()

        def cross(self, source):
            for part in range(1, 1 + self.chunks):
                self.push(source.at[:, self.lanes(part)], node, part, mirror)

        def begin(self, source):
            for m in mates:
                self.push(source, node, 0, m)

        def forward(self):
            for part in range(1, 1 + self.chunks):
                self.arrived(part, 1)
                for m in mates:
                    self.push(self.piece(mirror, part), mirror, part + 2, m)

        def near_ready(self):
            self.arrived(0, QUADS - 1)

        def far_ready(self):
            for part in range(3, 3 + self.chunks):
                self.arrived(part, QUADS - 1)

        def finish(self):
            ref = self.buf.at[0 : 7 * ROWS, :]
            rdma(ref, ref, self.send, self.send, device(mirror)).wait_send()

    class Scatter:
        def __init__(self, src, mirror_src, dst, phase):
            self.src, self.mirror_src, self.dst = src, mirror_src, dst
            self.send = a2a_sem.at[3 * phase]
            self.near, self.far = a2a_sem.at[3 * phase + 1], a2a_sem.at[3 * phase + 2]

        def pick(self, ref, m):
            return ref.at[m] if len(ref.shape) == 3 else block(ref, m)

        def push(self, src, m, recv):
            rdma(src, self.pick(self.dst, node), self.send, recv, device(m)).start()

        def to_mates(self):
            for m in mates:
                self.push(self.pick(self.src, m), m, self.near)

        def to_mirror(self):
            self.push(self.mirror_src, mirror, self.far)

        def to_far(self):
            for m in across[1:]:
                self.push(self.pick(self.src, m), m, self.far)

        def some(self, ref, count):
            return ref.at[0 : count if len(ref.shape) == 3 else count * ROWS]

        def near_ready(self):
            dst = self.some(self.dst, 3)
            rdma(dst, dst, self.send, self.near, device(mirror)).wait_recv()

        def far_ready(self):
            dst = self.some(self.dst, 4)
            rdma(dst, dst, self.send, self.far, device(mirror)).wait_recv()

        def sent(self):
            src = self.some(self.src, 7)
            rdma(src, src, self.send, self.far, device(mirror)).wait_send()

    others = mates + across

    small[0].wait()
    small[1].wait()
    block(gather_q, node)[...] = norm_rows(states[...], attn_gain[...]).astype(jnp.bfloat16)
    pl.semaphore_wait(barrier, NODES + 1)

    first = Gather(gather_q, 0, 2)
    first.cross(block(gather_q, node))
    first.begin(block(gather_q, node))
    for i in (0, 1, 2, 3):
        shared[i].start()

    def group_rows(group):
        return pl.ds(pl.multiple_of(group * 64, 64), 64)

    def project(rows, count):
        inputs = gather_q[rows, :]
        q = jnp.dot(inputs, w_query_v[...], preferred_element_type=jnp.float32)
        kv = lax.dot_general(
            inputs, w_kv_v[...], (((1,), (1,)), ((), ())), preferred_element_type=jnp.float32
        )
        kv = kv.reshape(count, ROWS, 64)
        kv = jnp.concatenate([kv[:, 0:8, :], kv[:, 8:16, :]], axis=-1)
        q = [q[:, 128 * i : 128 * i + 128].reshape(count, ROWS, 128) for i in range(2)]
        return jnp.concatenate(q + [kv], axis=1)

    def project_group(group):
        parts[pl.ds(group * QUADS, QUADS)] = project(group_rows(group), QUADS)

    mirror_rows = pl.ds(pl.multiple_of(mirror * ROWS, ROWS), ROWS)

    slim = wide // 2

    def w_piece(q, core, part):
        rows = pl.ds(pl.multiple_of((2 * q + core) * 128, 128), 128)
        return w_cols.at[rows, lanes_of(part, slim)]

    def w_start():
        for m in mates:
            at = pl.multiple_of(m % QUADS * wide + group * slim, slim)
            rdma(
                w_output.at[:, pl.ds(at, slim)],
                w_piece(quad, c, group),
                w_sem.at[0],
                w_sem.at[1 + quad],
                device(m),
            ).start()

    def w_arrived(m):
        piece = w_piece(m % QUADS, c, group)
        rdma(piece, piece, w_sem.at[0], w_sem.at[1 + m % QUADS], device(m)).wait_recv()

    def w_over(m):
        piece = w_piece(m % QUADS, c, group)
        rdma(piece, piece, w_sem.at[5], w_sem.at[6], twin_group).start()

    def w_three(send, recv):
        ref = w_cols.at[0:384, 0:slim]
        return rdma(ref, ref, w_sem.at[send], w_sem.at[recv], twin_group)

    def w_pass(m, part):
        piece = w_piece(m % QUADS, c, part)
        rdma(piece, piece, w_sem.at[7], w_sem.at[8], twin).start()

    def w_pass_all():
        ref = w_cols.at[0:512, :]
        return rdma(ref, ref, w_sem.at[7], w_sem.at[8], twin)

    def gates_start():
        mine = block(gates_all, node)
        for m in others:
            rdma(mine, mine, a2a_sem.at[6], a2a_sem.at[7], device(m)).start()

    def gates_wait():
        ref = gates_all.at[0 : 7 * ROWS, :]
        rdma(ref, ref, a2a_sem.at[6], a2a_sem.at[7], device(mirror)).wait()

    first.forward()
    for i in (0, 1, 2):
        local[i].wait()
        shared[i].wait_recv()
    first.near_ready()
    project_group(half)
    heads = Scatter(parts, parts_m.at[0], own_parts, 0)
    heads.to_mates()
    own_parts[node] = parts[node]
    parts_m[...] = project(mirror_rows, 1)
    heads.to_mirror()

    for copy in small[2:]:
        copy.wait()
    row_id = lax.broadcasted_iota(jnp.int32, (ROWS, 128), 0)
    lane_id = lax.broadcasted_iota(jnp.int32, (ROWS, 128), 1)
    chosen = jnp.concatenate([routes[:, 0, :], routes[:, 1, :]], axis=0)
    shares = jnp.concatenate([gate_weights[0], gate_weights[1]], axis=0)
    weighed = jnp.zeros((ROWS, 128), jnp.float32)
    for k in range(TOPK):
        weighed = jnp.where(lane_id == chosen[:, k : k + 1], shares[:, k : k + 1], weighed)
    block(gates_all, node)[...] = weighed
    slot_of = jnp.zeros((ROWS, 128), jnp.int32)
    for b in range(8):
        slot_of = jnp.where(row_id % 8 == b, slots[b], slot_of)
    limits = [jnp.where(slot_of == p, lengths[p], 0) for p in range(2)]
    phases = (limits[0] + limits[1] + row_id // 8).astype(jnp.float32) * rates[...]
    cosine = jnp.cos(phases)
    sine = jnp.sin(phases)
    sine = jnp.where(lane_id < 64, -sine, sine)

    first.far_ready()
    project_group(1 - half)
    heads.to_far()
    w_start()
    first.finish()

    def turned(vectors):
        return vectors * cosine + pltpu.roll(vectors, 64, 1) * sine

    def unpack(k):
        for q in range(QUADS):
            j = k * QUADS + q
            for i in range(2):
                at = (2 * q + i) * ROWS
                queries[k, at : at + ROWS, :] = turned(
                    own_parts[j, i * ROWS : (i + 1) * ROWS, :]
                ).astype(jnp.bfloat16)
            packed = own_parts[j, 2 * ROWS : 2 * ROWS + 8, :]
            unpacked = jnp.concatenate([packed[:, 0:64], packed[:, 64:128]], axis=0)
            fresh_k[k, :, q * 32 : (q + 1) * 32] = unpacked[:, 0:32]
            fresh_v[k, :, q * 32 : (q + 1) * 32] = unpacked[:, 32:64]

    local[5].wait()
    local[6].wait()
    inv_root = 1.0 / math.sqrt(HD)
    group_size = HQ // KVH
    q_rows = group_size * ROWS
    span = keys_v.shape[1]
    far_pos = lax.broadcasted_iota(jnp.int32, (q_rows, span), 1)
    row_at = lax.broadcasted_iota(jnp.int32, (q_rows, ROWS), 0) % ROWS
    col_at = lax.broadcasted_iota(jnp.int32, (q_rows, ROWS), 1)
    own_seen = (row_at % 8 == col_at % 8) & (col_at // 8 <= row_at // 8)
    limits = [jnp.concatenate([m[:, 0:1]] * group_size, axis=0) for m in limits]

    def attend(k):
        lanes = lanes_of(k, HD)
        new_keys = turned(fresh_k[k]).astype(jnp.bfloat16)
        new_values = fresh_v[k].astype(jnp.bfloat16)
        appended[:, lanes] = new_keys
        appended[:, lanes_of(KVH + k, HD)] = new_values
        q = queries[k]

        def against(rows):
            return (
                lax.dot_general(
                    q, rows, (((1,), (1,)), ((), ())), preferred_element_type=jnp.float32
                )
                * inv_root
            )

        scores = [
            jnp.where(far_pos < limits[p], against(keys_v[p, :, lanes]), -1e30) for p in range(2)
        ]
        own_scores = jnp.where(own_seen, against(new_keys), -1e30)
        peak = jnp.maximum(
            jnp.maximum(
                jnp.max(scores[0], axis=1, keepdims=True), jnp.max(scores[1], axis=1, keepdims=True)
            ),
            jnp.max(own_scores, axis=1, keepdims=True),
        )
        weights = [jnp.exp(s - peak) for s in scores]
        own_weights = jnp.exp(own_scores - peak)
        total = (
            jnp.sum(weights[0], axis=1, keepdims=True)
            + jnp.sum(weights[1], axis=1, keepdims=True)
            + jnp.sum(own_weights, axis=1, keepdims=True)
        )
        scale = 1.0 / total
        attended = jnp.dot(
            (own_weights * scale).astype(jnp.bfloat16),
            new_values,
            preferred_element_type=jnp.float32,
        )
        for p in range(2):
            attended = attended + jnp.dot(
                (weights[p] * scale).astype(jnp.bfloat16),
                values_v[p, :, lanes],
                preferred_element_type=jnp.float32,
            )
        attended = attended.astype(jnp.bfloat16)
        for g in range(group_size):
            attended_v[k, :, g * HD : (g + 1) * HD] = attended[g * ROWS : (g + 1) * ROWS, :]

    second = Gather(gather_o, 1, 1)
    heads.near_ready()
    unpack(half)
    attend(half)
    second.begin(attended_v.at[half])
    block(gather_o, node)[...] = attended_v[half]
    heads.far_ready()
    unpack(1 - half)
    attend(1 - half)
    second.cross(attended_v.at[1 - half])
    heads.sent()

    for m in mates:
        w_arrived(m)
        w_over(m)
        w_pass(m, group)
    local[7].wait()
    w_pass(node, 0)
    w_pass(node, 1)
    second.forward()
    w_three(5, 6).wait_recv()
    for m in mates:
        w_pass(m, 1 - group)
    w_pass_all().wait_recv()
    shared[4].start()

    def code_of(largest):
        return jnp.ceil(jnp.log2(jnp.maximum(largest, 1e-30)) * CODE_STEPS)

    def encode(values, ref):
        size = values.shape[1]
        code = code_of(jnp.max(jnp.abs(values), axis=1, keepdims=True))
        factor = jnp.exp2(CODE_TOP - code * (1.0 / CODE_STEPS))
        ref[:, 0:size] = jnp.round(values * factor).astype(jnp.int32).astype(jnp.int16)
        ref[:, size : size + 128] = jnp.broadcast_to(
            code.astype(jnp.int32), (values.shape[0], 128)
        ).astype(jnp.int16)

    def decode(ref):
        values = ref[...]
        size = values.shape[1] - 128
        code = values[:, size : size + 1].astype(jnp.int32).astype(jnp.float32)
        factor = jnp.exp2(code * (1.0 / CODE_STEPS) - CODE_TOP)
        return values[:, :size].astype(jnp.int32).astype(jnp.float32) * factor

    def out_project(rows):
        return jnp.dot(gather_o[rows, :], w_cols[...], preferred_element_type=jnp.float32)

    second.near_ready()
    def near_block(ref, m):
        return ref.at[pl.ds(pl.multiple_of(m % QUADS * ROWS, ROWS), ROWS), :]

    def columns_to(m):
        rdma(
            near_block(cols, m),
            near_block(own_cols, node),
            a2a_sem.at[3],
            a2a_sem.at[4],
            device(m),
        ).start()

    def columns_over(m):
        rdma(
            cols_out.at[m % QUADS],
            cols_in.at[quad],
            a2a_sem.at[5],
            a2a_sem.at[8],
            device(m),
        ).start()

    cols[...] = out_project(group_rows(half))
    for m in mates:
        columns_to(m)
    near_block(own_cols, node)[...] = near_block(cols, node)[...]
    encode(out_project(mirror_rows), cols_out.at[quad])
    columns_over(mirror)
    second.far_ready()
    cols_far[...] = out_project(group_rows(1 - half))
    for m in across[1:]:
        encode(near_block(cols_far, m)[...], cols_out.at[m % QUADS])
        columns_over(m)
    gates_start()
    second.finish()
    w_three(0, 0).wait_send()
    w_three(5, 6).wait_send()
    w_pass_all().wait_send()
    ref = own_cols.at[0 : 3 * ROWS, :]
    rdma(ref, ref, a2a_sem.at[3], a2a_sem.at[4], device(mirror)).wait()
    rdma(cols_out, cols_in, a2a_sem.at[5], a2a_sem.at[8], device(mirror)).wait()
    for q in range(QUADS):
        lanes = slice(q * wide, (q + 1) * wide)
        hidden[:, lanes] = states[:, lanes] + (
            own_cols[q * ROWS : (q + 1) * ROWS, :] + decode(cols_in.at[q])
        )
    block(gather_m, node)[...] = norm_rows(hidden[...], moe_gain[...]).astype(jnp.bfloat16)

    third = Gather(gather_m, 2, 2)
    third.cross(block(gather_m, node))
    third.begin(block(gather_m, node))
    gates_wait()

    all_rows = NODES * ROWS
    all_lane = lax.broadcasted_iota(jnp.int32, (all_rows, 128), 1)

    def gate_up():
        for e in range(2):

            @pl.loop(0, ff // 256)
            def _(t):
                at = pl.multiple_of(t * 256, 256)
                inputs = gather_m[...]
                g = jnp.dot(
                    inputs, gate_up_v[e, :, pl.ds(at, 256)], preferred_element_type=jnp.float32
                )
                u = jnp.dot(
                    inputs,
                    gate_up_v[e, :, pl.ds(pl.multiple_of(ff + t * 256, 256), 256)],
                    preferred_element_type=jnp.float32,
                )
                act[e, :, pl.ds(at, 256)] = (g / (1.0 + jnp.exp(-g)) * u).astype(jnp.bfloat16)

    def part_lanes(part):
        return slice(part * deep, (part + 1) * deep)

    def down(part):
        for t in range(2):
            lanes = slice((2 * part + t) * wide, (2 * part + t + 1) * wide)
            total = jnp.zeros((all_rows, wide), jnp.float32)
            for e in range(2):
                got = jnp.dot(act[e], down_v[e, :, lanes], preferred_element_type=jnp.float32)
                got = got.astype(jnp.bfloat16).astype(jnp.float32)
                total = total + jnp.where(share[e] > 0.0, share[e] * got, 0.0)
            mix[:, lanes] = total

    def encode_far(part):
        for q in range(QUADS):
            rows = pl.ds(pl.multiple_of(((1 - half) * QUADS + q) * ROWS, ROWS), ROWS)
            encode(mix[rows, part_lanes(part)], far_out.at[part, q])

    def encode_near():
        for q in range(QUADS):
            rows = pl.ds(pl.multiple_of((half * QUADS + q) * ROWS, ROWS), ROWS)
            encode(mix[rows, :], near_out.at[q])

    def relay_start(part):
        for m in mates:
            rdma(
                far_out.at[part, m % QUADS],
                relay_in.at[part, quad],
                ret_sem.at[0],
                ret_sem.at[1 + part],
                device(m),
            ).start()

    def relay_wait(part):
        ref = relay_in.at[part, 0:3]
        rdma(ref, ref, ret_sem.at[0], ret_sem.at[1 + part], device(mirror)).wait_recv()

    def home_start():
        for m in mates:
            rdma(
                near_out.at[m % QUADS],
                near_in.at[quad],
                ret_sem.at[5],
                ret_sem.at[6],
                device(m),
            ).start()

    third.forward()
    third.near_ready()
    gates = gates_all[...]
    share = [
        jnp.sum(jnp.where(all_lane == 2 * node + e, gates, 0.0), axis=1, keepdims=True)
        for e in range(2)
    ]
    third.far_ready()
    for i in (3, 4):
        local[i].wait()
        shared[i].wait_recv()
    gate_up()
    for part in range(2):
        down(part)
        encode_far(part)
        relay_start(part)
    encode_near()
    third.finish()

    def last(part):
        return rdma(
            mirror_out.at[part],
            mirror_in.at[part],
            ret_sem.at[7],
            ret_sem.at[8 + part],
            device(mirror),
        )

    for part in range(2):
        relay_wait(part)
        total = block(mix, mirror)[:, part_lanes(part)]
        for m in mates:
            total = total + decode(relay_in.at[part, m % QUADS])
        encode(total, mirror_out.at[part])
        last(part).start()
        if part == 0:
            home_start()
    ref = near_in.at[0:3]
    rdma(ref, ref, ret_sem.at[5], ret_sem.at[6], device(mirror)).wait()
    total = hidden[...] + block(mix, node)[...]
    for m in mates:
        total = total + decode(near_in.at[m % QUADS])
    hidden[...] = total
    ref = relay_in.at[:, 0:3]
    rdma(ref, ref, ret_sem.at[0], ret_sem.at[0], device(mirror)).wait_send()
    for copy in shared:
        copy.wait_send()
    for part in range(2):
        last(part).wait_recv()
        lanes = part_lanes(part)
        out[:, lanes] = hidden[:, lanes] + decode(mirror_in.at[part])
    rdma(mirror_out, mirror_in, ret_sem.at[7], ret_sem.at[7], device(mirror)).wait_send()


def tuned(
    states,
    attn_gain,
    moe_gain,
    w_query,
    w_key,
    w_value,
    w_output,
    w_gate_up,
    w_down,
    key_cache,
    value_cache,
    cache_lengths,
    prefix_slot,
    routes,
    gate_weights,
):
    step_count, row_count, width = states.shape
    rows = step_count * row_count
    prefix_count, span, kv_width = key_cache.shape
    ff = w_down.shape[1]
    rates = np.tile(THETA ** (-(np.arange(HD // 2) * 2.0 / HD)), 2)
    rates = jnp.asarray(rates.astype(np.float32).reshape(1, HD))
    in_hbm = pl.BlockSpec(memory_space=pl.ANY)
    everyone = NODES * rows
    coded_width = width // QUADS + 128
    bf16, f32, i16 = jnp.bfloat16, jnp.float32, jnp.int16
    out, appended = pl.pallas_call(
        layer_kernel,
        out_shape=(
            pltpu.VMEM((rows, width), f32),
            pltpu.VMEM((rows, 2 * kv_width), bf16),
        ),
        in_specs=[in_hbm] * 16,
        scratch_shapes=[
            pltpu.VMEM((rows, width), f32),
            pltpu.VMEM((1, width), f32),
            pltpu.VMEM((1, width), f32),
            pltpu.VMEM((1, HD), f32),
            pltpu.SMEM(cache_lengths.shape, jnp.int32),
            pltpu.SMEM(prefix_slot.shape, jnp.int32),
            pltpu.VMEM(routes.shape, jnp.int32),
            pltpu.VMEM(gate_weights.shape, f32),
            pltpu.VMEM((width, 256), bf16),
            pltpu.VMEM((64, width), bf16),
            pltpu.VMEM((everyone, 128), f32),
            pltpu.VMEM((everyone, width), bf16),
            pltpu.VMEM((everyone, width // 2), bf16),
            pltpu.VMEM((everyone, width), bf16),
            pltpu.VMEM((2, rows, width // 2), bf16),
            pltpu.VMEM((NODES, 2 * rows + 8, 128), f32),
            pltpu.VMEM((1, 2 * rows + 8, 128), f32),
            pltpu.VMEM((NODES, 2 * rows + 8, 128), f32),
            pltpu.VMEM((width // 2, width // QUADS), bf16),
            pltpu.VMEM((QUADS * rows, width // QUADS), f32),
            pltpu.VMEM((QUADS * rows, width // QUADS), f32),
            pltpu.VMEM((QUADS, rows, coded_width), i16),
            pltpu.VMEM((QUADS, rows, coded_width), i16),
            pltpu.VMEM((QUADS * rows, width // QUADS), f32),
            pltpu.VMEM((rows, width), f32),
            pltpu.VMEM((2, everyone, ff), bf16),
            pltpu.VMEM((everyone, width), f32),
            pltpu.VMEM((QUADS, rows, width + 128), i16),
            pltpu.VMEM((2, QUADS, rows, width // 2 + 128), i16),
            pltpu.VMEM((QUADS, rows, width + 128), i16),
            pltpu.VMEM((2, QUADS, rows, width // 2 + 128), i16),
            pltpu.VMEM((2, rows, width // 2 + 128), i16),
            pltpu.VMEM((2, rows, width // 2 + 128), i16),
            pltpu.VMEM((2, rows, HD), f32),
            pltpu.VMEM((2, rows, HD), f32),
            pltpu.VMEM((2, HQ // 2 * rows, HD), bf16),
            pltpu.VMEM((2, width, 2 * ff), bf16),
            pltpu.VMEM((2, ff, width), bf16),
            pltpu.VMEM((prefix_count, span, kv_width), bf16),
            pltpu.VMEM((prefix_count, span, kv_width), bf16),
            pltpu.SemaphoreType.DMA((8,)),
            pltpu.SemaphoreType.DMA((8,)),
            pltpu.SemaphoreType.DMA((5,)),
            pltpu.SemaphoreType.DMA((5,)),
            pltpu.SemaphoreType.DMA((18,)),
            pltpu.SemaphoreType.DMA((9,)),
            pltpu.SemaphoreType.DMA((9,)),
            pltpu.SemaphoreType.DMA((12,)),
        ],
        compiler_params=pltpu.CompilerParams(
            collective_id=0, has_side_effects=True, vmem_limit_bytes=56 * 1024 * 1024
        ),
    )(
        states.reshape(rows, width),
        attn_gain.reshape(1, width),
        moe_gain.reshape(1, width),
        rates,
        cache_lengths,
        prefix_slot,
        routes,
        gate_weights,
        w_query,
        w_key.T,
        w_value.T,
        w_output,
        w_gate_up[0],
        w_down[0],
        key_cache,
        value_cache,
    )
    return (
        out.reshape(step_count, row_count, width),
        appended.reshape(step_count, row_count, 2 * kv_width),
    )


def solution(mesh):
    return jax.shard_map(
        tuned if mesh.shape["ep"] == TUNED_DEVICES else shards,
        mesh=mesh,
        in_specs=(
            P(None, ("groups", "ep"), None),
            P(),
            P(),
            P(None, "ep"),
            P(None, "ep"),
            P(None, "ep"),
            P("ep", None),
            P("ep", None, None),
            P("ep", None, None),
            P(("groups", "ep"), None, None),
            P(("groups", "ep"), None, None),
            P(("groups", "ep")),
            P(("groups", "ep")),
            P(("groups", "ep"), None, None),
            P(None, ("groups", "ep"), None),
        ),
        out_specs=(P(None, ("groups", "ep"), None), P(None, ("groups", "ep"), None)),
        check_vma=False,
    )
```

```python
import math

import jax
import jax.numpy as jnp
import numpy as np
from jax import lax
from jax.experimental import pallas as pl
from jax.experimental.pallas import tpu as pltpu
from jax.sharding import PartitionSpec as P

HQ = 16
KVH = 2
HD = 128
TOPK = 8


EPS = 1e-06
THETA = 1000000.0


def rms_scale(values, gain):
    squares = jnp.mean(values * values, axis=-1, keepdims=True)
    return values * lax.rsqrt(squares + EPS) * gain


def rotate(vectors, positions):
    head_size = vectors.shape[-1]
    half_size = head_size // 2
    inverse_rate = THETA ** (-(jnp.arange(half_size).astype(jnp.float32) * 2.0 / head_size))
    phases = positions[..., None, None] * inverse_rate
    cosine = jnp.cos(phases)
    sine_part = jnp.sin(phases)
    first_half = vectors[..., :half_size]
    second_half = vectors[..., half_size:]
    return jnp.concatenate(
        [
            first_half * cosine - second_half * sine_part,
            second_half * cosine + first_half * sine_part,
        ],
        axis=-1,
    )


def attend_block(queries, new_keys, new_values, key_block, value_block, lengths, slots):
    step_count, row_count, head_count, head_size = queries.shape
    prefix_count, cache_span, kv_heads, _ = key_block.shape
    group_size = head_count // kv_heads
    grouped = queries.reshape(step_count, row_count, kv_heads, group_size, head_size)
    inv_root = 1.0 / math.sqrt(head_size)
    far_scores = (
        jnp.einsum("srkgd,pckd->srkgpc", grouped, key_block, preferred_element_type=jnp.float32)
        * inv_root
    )
    visible = (jnp.arange(cache_span)[None, None, :] < lengths[None, :, None]) & (
        slots[:, None, None] == jnp.arange(prefix_count)[None, :, None]
    )
    far_scores = jnp.where(visible[None, :, None, None], far_scores, -1e30)
    own_scores = (
        jnp.einsum("srkgd,trkd->srkgt", grouped, new_keys, preferred_element_type=jnp.float32)
        * inv_root
    )
    causal = jnp.arange(step_count)[None, :] <= jnp.arange(step_count)[:, None]
    own_scores = jnp.where(causal[:, None, None, None, :], own_scores, -1e30)
    peak = jnp.maximum(jnp.max(far_scores, axis=(-2, -1)), jnp.max(own_scores, axis=-1))
    far_weights = jnp.exp(far_scores - peak[..., None, None])
    own_weights = jnp.exp(own_scores - peak[..., None])
    normalizer = jnp.sum(far_weights, axis=(-2, -1)) + jnp.sum(own_weights, axis=-1)
    far_probs = (far_weights / normalizer[..., None, None]).astype(jnp.bfloat16)
    own_probs = (own_weights / normalizer[..., None]).astype(jnp.bfloat16)
    attended = jnp.einsum(
        "srkgpc,pckd->srkgd", far_probs, value_block, preferred_element_type=jnp.float32
    )
    attended = attended + jnp.einsum(
        "srkgt,trkd->srkgd", own_probs, new_values, preferred_element_type=jnp.float32
    )
    return attended.reshape(step_count, row_count, head_count * head_size).astype(jnp.bfloat16)


def shards(
    states,
    attn_gain,
    moe_gain,
    w_query,
    w_key,
    w_value,
    w_output,
    w_gate_up,
    w_down,
    key_cache,
    value_cache,
    cache_lengths,
    prefix_slot,
    routes,
    gate_weights,
):
    devices = lax.axis_size("ep")
    step_count, row_count, model_width = states.shape
    query_cols = w_query.shape[1]
    kv_cols = w_key.shape[1]
    normed = rms_scale(states, attn_gain).astype(jnp.bfloat16)
    joined = jnp.concatenate([w_query, w_key, w_value], axis=1)
    head_parts = jnp.einsum(
        "srd,dc->src",
        lax.all_gather(normed, "ep", axis=1, tiled=True),
        joined,
        preferred_element_type=jnp.float32,
    )
    own_cols = lax.all_to_all(head_parts, "ep", split_axis=1, concat_axis=2, tiled=True)
    own_cols = own_cols.reshape(step_count, row_count, devices, query_cols + 2 * kv_cols)
    queries = own_cols[..., :query_cols].reshape(step_count, row_count, HQ, HD)
    new_keys = own_cols[..., query_cols : query_cols + kv_cols].reshape(
        step_count, row_count, KVH, HD
    )
    new_values = (
        own_cols[..., query_cols + kv_cols :]
        .reshape(step_count, row_count, KVH, HD)
        .astype(jnp.bfloat16)
    )
    prefix_count, cache_span, _ = key_cache.shape
    lengths_here = jnp.sum(
        jnp.where(
            prefix_slot[:, None] == jnp.arange(prefix_count)[None, :], cache_lengths[None, :], 0
        ),
        axis=1,
    )
    positions = (
        lengths_here.astype(jnp.float32)[None, :]
        + jnp.arange(step_count).astype(jnp.float32)[:, None]
    )
    queries = rotate(queries, positions).astype(jnp.bfloat16)
    new_keys = rotate(new_keys, positions).astype(jnp.bfloat16)
    attended = attend_block(
        queries,
        new_keys,
        new_values,
        key_cache.reshape(prefix_count, cache_span, KVH, HD),
        value_cache.reshape(prefix_count, cache_span, KVH, HD),
        cache_lengths,
        prefix_slot,
    )
    w_columns = lax.all_to_all(w_output, "ep", split_axis=1, concat_axis=0, tiled=True)
    column_part = jnp.einsum(
        "srf,fc->src",
        lax.all_gather(attended, "ep", axis=1, tiled=True),
        w_columns,
        preferred_element_type=jnp.float32,
    )
    projected = lax.all_to_all(column_part, "ep", split_axis=1, concat_axis=2, tiled=True)
    hidden = states + projected
    moe_input = (
        rms_scale(hidden, moe_gain)
        .astype(jnp.bfloat16)
        .reshape(step_count * row_count, model_width)
    )
    expert_count = w_gate_up.shape[0] * devices
    capacity = max(2, 4 * row_count * TOPK // expert_count)
    flat_routes = jnp.swapaxes(routes, 0, 1).reshape(-1)
    order = jnp.arange(flat_routes.shape[0])
    earlier = (flat_routes[:, None] == flat_routes[None, :]) & (order[None, :] < order[:, None])
    within = jnp.sum(earlier.astype(jnp.int32), axis=1)
    slot_index = flat_routes * capacity + within
    dispatch = (jnp.arange(expert_count * capacity)[:, None] == slot_index[None, :]).astype(
        jnp.bfloat16
    )
    repeated = jnp.repeat(moe_input, TOPK, axis=0)
    outgoing = jnp.dot(dispatch, repeated, preferred_element_type=jnp.float32).astype(jnp.bfloat16)
    outgoing = outgoing.reshape(expert_count, capacity, model_width)
    both = jnp.einsum(
        "nsd,df->nsf",
        lax.all_to_all(outgoing, "ep", split_axis=0, concat_axis=0, tiled=True),
        w_gate_up[0],
        preferred_element_type=jnp.float32,
    )
    half_cols = both.shape[-1] // 2
    activation = (jax.nn.silu(both[..., :half_cols]) * both[..., half_cols:]).astype(jnp.bfloat16)
    expert_done = jnp.einsum(
        "nsf,fd->nsd", activation, w_down[0], preferred_element_type=jnp.float32
    ).astype(jnp.bfloat16)
    returned = lax.all_to_all(expert_done, "ep", split_axis=0, concat_axis=0, tiled=True)
    picked = returned.reshape(expert_count * capacity, model_width)[slot_index]
    picked = picked.astype(jnp.float32).reshape(step_count, row_count, TOPK, model_width)
    mixture = jnp.sum(gate_weights[..., None] * picked, axis=2)
    appended = jnp.concatenate(
        [
            new_keys.reshape(step_count, row_count, KVH * HD),
            new_values.reshape(step_count, row_count, KVH * HD),
        ],
        axis=-1,
    )
    return (hidden + mixture, appended)


TUNED_DEVICES = 16
ROWS = 16
NODES = 8
QUADS = 4
CODE_TOP = 14.99
CODE_STEPS = 256.0


def norm_rows(values, gain):
    squares = jnp.mean(values * values, axis=-1, keepdims=True)
    return values * lax.rsqrt(squares + EPS) * gain


def layer_kernel(
    states_in,
    attn_gain_in,
    moe_gain_in,
    rates_in,
    lengths_in,
    slots_in,
    routes_in,
    gate_weights_in,
    w_query,
    w_key,
    w_value,
    w_output,
    w_gate_up,
    w_down,
    key_cache,
    value_cache,
    out,
    appended,
    states,
    attn_gain,
    moe_gain,
    rates,
    lengths,
    slots,
    routes,
    gate_weights,
    w_query_v,
    w_kv_v,
    gates_all,
    gather_q,
    gather_o,
    gather_m,
    attended_v,
    parts,
    parts_m,
    own_parts,
    w_cols,
    cols,
    cols_far,
    cols_out,
    cols_in,
    own_cols,
    hidden,
    act,
    mix,
    near_out,
    far_out,
    near_in,
    relay_in,
    mirror_out,
    mirror_in,
    fresh_k,
    fresh_v,
    queries,
    gate_up_v,
    down_v,
    keys_v,
    values_v,
    small_sem,
    load_sem,
    twin_send,
    twin_recv,
    ag_sem,
    a2a_sem,
    w_sem,
    ret_sem,
):
    me = lax.axis_index("ep")
    c = me % 2
    node = me // 2
    half = node // QUADS
    quad = node % QUADS
    twin = me + 1 - 2 * c
    group = lax.axis_index("groups")
    twin_group = {"groups": 1 - group, "ep": me}
    width = states.shape[1]
    wide = width // QUADS
    deep = width // 2
    ff = down_v.shape[1]

    def device(m):
        return m * 2 + c

    mate_y = node + 1 - 2 * (node % 2)
    mate_z = node + 2 - 4 * (quad // 2)
    mate_yz = mate_z + mate_y - node
    mates = [mate_y, mate_yz, mate_z]
    mirror = (node + QUADS) % NODES
    across = [mirror] + [(m + QUADS) % NODES for m in mates]

    def block(ref, m):
        return ref.at[pl.ds(pl.multiple_of(m * ROWS, ROWS), ROWS), :]

    def rdma(src, dst, send, recv, target):
        return pltpu.make_async_remote_copy(
            src_ref=src,
            dst_ref=dst,
            send_sem=send,
            recv_sem=recv,
            device_id=target if isinstance(target, dict) else {"ep": target},
            device_id_type=pl.DeviceIdType.MESH,
        )

    barrier = pltpu.get_barrier_semaphore()
    partners = [{"ep": device((node + i) % NODES)} for i in range(1, NODES)]
    for target in partners + [{"ep": twin}, twin_group]:
        pl.semaphore_signal(
            barrier,
            inc=1,
            device_id=target,
            device_id_type=pl.DeviceIdType.MESH,
        )

    small = [
        pltpu.make_async_copy(s, d, small_sem.at[i])
        for i, (s, d) in enumerate(
            (
                (states_in, states),
                (attn_gain_in, attn_gain),
                (lengths_in, lengths),
                (slots_in, slots),
                (rates_in, rates),
                (routes_in, routes),
                (gate_weights_in, gate_weights),
                (moe_gain_in, moe_gain),
            )
        )
    ]
    for copy in small:
        copy.start()

    def lanes_of(index, size):
        return pl.ds(pl.multiple_of(index * size, size), size)

    def twin_pairs():
        return [
            (w_query, w_query_v.at[:, lanes_of(c, 128)]),
            (w_key, w_kv_v.at[pl.ds(pl.multiple_of(c * 16, 16), 16), :]),
            (w_value, w_kv_v.at[pl.ds(pl.multiple_of(32 + c * 16, 16), 16), :]),
            (w_gate_up, gate_up_v.at[c]),
            (w_down, down_v.at[c]),
        ]

    local = [pltpu.make_async_copy(s, d, load_sem.at[i]) for i, (s, d) in enumerate(twin_pairs())]
    shared = [
        rdma(s, d, twin_send.at[i], twin_recv.at[i], twin) for i, (s, d) in enumerate(twin_pairs())
    ]
    w_rows = pl.ds(pl.multiple_of((2 * quad + c) * 128, 128), 128)
    local += [
        pltpu.make_async_copy(key_cache, keys_v, load_sem.at[5]),
        pltpu.make_async_copy(value_cache, values_v, load_sem.at[6]),
        pltpu.make_async_copy(
            w_output.at[:, lanes_of(quad, wide)], w_cols.at[w_rows, :], load_sem.at[7]
        ),
    ]
    for i in (0, 1, 2, 5, 6, 7, 3, 4):
        local[i].start()

    class Gather:
        def __init__(self, buf, phase, chunks):
            self.buf, self.phase, self.chunks = buf, phase, chunks
            self.size = buf.shape[1] // chunks
            self.send = ag_sem.at[6 * phase]

        def lanes(self, part):
            if part == 0:
                return slice(None)
            return slice((part - 1) % 2 * self.size, ((part - 1) % 2 + 1) * self.size)

        def piece(self, m, part):
            return self.buf.at[pl.ds(pl.multiple_of(m * ROWS, ROWS), ROWS), self.lanes(part)]

        def push(self, src, m, part, target):
            landed = ag_sem.at[6 * self.phase + 1 + part]
            rdma(src, self.piece(m, part), self.send, landed, device(target)).start()

        def arrived(self, part, count):
            ref = self.buf.at[0 : count * ROWS, self.lanes(part)]
            landed = ag_sem.at[6 * self.phase + 1 + part]
            rdma(ref, ref, self.send, landed, device(mirror)).wait_recv()

        def cross(self, source):
            for part in range(1, 1 + self.chunks):
                self.push(source.at[:, self.lanes(part)], node, part, mirror)

        def begin(self, source):
            for m in (mate_y, mate_yz, mate_z):
                self.push(source, node, 0, m)

        def forward(self):
            for part in range(1, 1 + self.chunks):
                self.arrived(part, 1)
                for m in (mate_y, mate_yz, mate_z):
                    self.push(self.piece(mirror, part), mirror, part + 2, m)

        def near_ready(self):
            self.arrived(0, QUADS - 1)

        def far_ready(self):
            for part in range(3, 3 + self.chunks):
                self.arrived(part, QUADS - 1)

        def finish(self):
            ref = self.buf.at[0 : 7 * ROWS, :]
            rdma(ref, ref, self.send, self.send, device(mirror)).wait_send()

    class Scatter:
        def __init__(self, src, mirror_src, dst, phase):
            self.src, self.mirror_src, self.dst = src, mirror_src, dst
            self.send = a2a_sem.at[3 * phase]
            self.near, self.far = a2a_sem.at[3 * phase + 1], a2a_sem.at[3 * phase + 2]

        def pick(self, ref, m):
            return ref.at[m] if len(ref.shape) == 3 else block(ref, m)

        def push(self, src, m, recv):
            rdma(src, self.pick(self.dst, node), self.send, recv, device(m)).start()

        def to_mates(self):
            for m in (mate_y, mate_yz, mate_z):
                self.push(self.pick(self.src, m), m, self.near)

        def to_mirror(self):
            self.push(self.mirror_src, mirror, self.far)

        def to_far(self):
            for m in ((mate_y + QUADS) % NODES, (mate_yz + QUADS) % NODES, (mate_z + QUADS) % NODES):
                self.push(self.pick(self.src, m), m, self.far)

        def some(self, ref, count):
            return ref.at[0 : count if len(ref.shape) == 3 else count * ROWS]

        def near_ready(self):
            dst = self.some(self.dst, 3)
            rdma(dst, dst, self.send, self.near, device(mirror)).wait_recv()

        def far_ready(self):
            dst = self.some(self.dst, 4)
            rdma(dst, dst, self.send, self.far, device(mirror)).wait_recv()

        def sent(self):
            src = self.some(self.src, 7)
            rdma(src, src, self.send, self.far, device(mirror)).wait_send()

    others = mates + across

    small[0].wait()
    small[1].wait()
    block(gather_q, node)[...] = norm_rows(states[...], attn_gain[...]).astype(jnp.bfloat16)
    pl.semaphore_wait(barrier, NODES + 1)

    first = Gather(gather_q, 0, 2)
    first.cross(block(gather_q, node))
    first.begin(block(gather_q, node))
    for i in (0, 1, 2, 3):
        shared[i].start()

    def group_rows(group):
        return pl.ds(pl.multiple_of(group * 64, 64), 64)

    def project(rows, count):
        inputs = gather_q[rows, :]
        q = jnp.dot(inputs, w_query_v[...], preferred_element_type=jnp.float32)
        kv = lax.dot_general(
            inputs, w_kv_v[...], (((1,), (1,)), ((), ())), preferred_element_type=jnp.float32
        )
        kv = kv.reshape(count, ROWS, 64)
        kv = jnp.concatenate([kv[:, 0:8, :], kv[:, 8:16, :]], axis=-1)
        q = [q[:, 128 * i : 128 * i + 128].reshape(count, ROWS, 128) for i in range(2)]
        return jnp.concatenate(q + [kv], axis=1)

    def project_group(group):
        parts[pl.ds(group * QUADS, QUADS)] = project(group_rows(group), QUADS)

    mirror_rows = pl.ds(pl.multiple_of(mirror * ROWS, ROWS), ROWS)

    slim = wide // 2

    def w_piece(q, core, part):
        rows = pl.ds(pl.multiple_of((2 * q + core) * 128, 128), 128)
        return w_cols.at[rows, lanes_of(part, slim)]

    def w_start():
        for m in (mate_y, mate_z, mate_yz):
            at = pl.multiple_of(m % QUADS * wide + group * slim, slim)
            rdma(
                w_output.at[:, pl.ds(at, slim)],
                w_piece(quad, c, group),
                w_sem.at[0],
                w_sem.at[1 + quad],
                device(m),
            ).start()

    def w_arrived(m):
        piece = w_piece(m % QUADS, c, group)
        rdma(piece, piece, w_sem.at[0], w_sem.at[1 + m % QUADS], device(m)).wait_recv()

    def w_over(m):
        piece = w_piece(m % QUADS, c, group)
        rdma(piece, piece, w_sem.at[5], w_sem.at[6], twin_group).start()

    def w_three(send, recv):
        ref = w_cols.at[0:384, 0:slim]
        return rdma(ref, ref, w_sem.at[send], w_sem.at[recv], twin_group)

    def w_pass(m, part):
        piece = w_piece(m % QUADS, c, part)
        rdma(piece, piece, w_sem.at[7], w_sem.at[8], twin).start()

    def w_pass_all():
        ref = w_cols.at[0:512, :]
        return rdma(ref, ref, w_sem.at[7], w_sem.at[8], twin)

    def gates_start():
        mine = block(gates_all, node)
        for m in others:
            rdma(mine, mine, a2a_sem.at[6], a2a_sem.at[7], device(m)).start()

    def gates_wait():
        ref = gates_all.at[0 : 7 * ROWS, :]
        rdma(ref, ref, a2a_sem.at[6], a2a_sem.at[7], device(mirror)).wait()

    first.forward()
    for i in (0, 1, 2):
        local[i].wait()
        shared[i].wait_recv()
    first.near_ready()
    project_group(half)
    heads = Scatter(parts, parts_m.at[0], own_parts, 0)
    heads.to_mates()
    own_parts[node] = parts[node]
    parts_m[...] = project(mirror_rows, 1)
    heads.to_mirror()

    for copy in small[2:]:
        copy.wait()
    row_id = lax.broadcasted_iota(jnp.int32, (ROWS, 128), 0)
    lane_id = lax.broadcasted_iota(jnp.int32, (ROWS, 128), 1)
    chosen = jnp.concatenate([routes[:, 0, :], routes[:, 1, :]], axis=0)
    shares = jnp.concatenate([gate_weights[0], gate_weights[1]], axis=0)
    weighed = jnp.zeros((ROWS, 128), jnp.float32)
    for k in range(TOPK):
        weighed = jnp.where(lane_id == chosen[:, k : k + 1], shares[:, k : k + 1], weighed)
    block(gates_all, node)[...] = weighed
    slot_of = jnp.zeros((ROWS, 128), jnp.int32)
    for b in range(8):
        slot_of = jnp.where(row_id % 8 == b, slots[b], slot_of)
    limits = [jnp.where(slot_of == p, lengths[p], 0) for p in range(2)]
    phases = (limits[0] + limits[1] + row_id // 8).astype(jnp.float32) * rates[...]
    cosine = jnp.cos(phases)
    sine = jnp.sin(phases)
    sine = jnp.where(lane_id < 64, -sine, sine)

    first.far_ready()
    project_group(1 - half)
    heads.to_far()
    w_start()
    first.finish()

    def turned(vectors):
        return vectors * cosine + pltpu.roll(vectors, 64, 1) * sine

    def unpack(k):
        for q in range(QUADS):
            j = k * QUADS + q
            for i in range(2):
                at = (2 * q + i) * ROWS
                queries[k, at : at + ROWS, :] = turned(
                    own_parts[j, i * ROWS : (i + 1) * ROWS, :]
                ).astype(jnp.bfloat16)
            packed = own_parts[j, 2 * ROWS : 2 * ROWS + 8, :]
            unpacked = jnp.concatenate([packed[:, 0:64], packed[:, 64:128]], axis=0)
            fresh_k[k, :, q * 32 : (q + 1) * 32] = unpacked[:, 0:32]
            fresh_v[k, :, q * 32 : (q + 1) * 32] = unpacked[:, 32:64]

    local[5].wait()
    local[6].wait()
    inv_root = 1.0 / math.sqrt(HD)
    group_size = HQ // KVH
    q_rows = group_size * ROWS
    span = keys_v.shape[1]
    far_pos = lax.broadcasted_iota(jnp.int32, (q_rows, span), 1)
    row_at = lax.broadcasted_iota(jnp.int32, (q_rows, ROWS), 0) % ROWS
    col_at = lax.broadcasted_iota(jnp.int32, (q_rows, ROWS), 1)
    own_seen = (row_at % 8 == col_at % 8) & (col_at // 8 <= row_at // 8)
    limits = [jnp.concatenate([m[:, 0:1]] * group_size, axis=0) for m in limits]

    def attend(k):
        lanes = lanes_of(k, HD)
        new_keys = turned(fresh_k[k]).astype(jnp.bfloat16)
        new_values = fresh_v[k].astype(jnp.bfloat16)
        appended[:, lanes] = new_keys
        appended[:, lanes_of(KVH + k, HD)] = new_values
        q = queries[k]

        def against(rows):
            return (
                lax.dot_general(
                    q, rows, (((1,), (1,)), ((), ())), preferred_element_type=jnp.float32
                )
                * inv_root
            )

        scores = [
            jnp.where(far_pos < limits[p], against(keys_v[p, :, lanes]), -1e30) for p in range(2)
        ]
        own_scores = jnp.where(own_seen, against(new_keys), -1e30)
        peak = jnp.maximum(
            jnp.maximum(
                jnp.max(scores[0], axis=1, keepdims=True), jnp.max(scores[1], axis=1, keepdims=True)
            ),
            jnp.max(own_scores, axis=1, keepdims=True),
        )
        weights = [jnp.exp(s - peak) for s in scores]
        own_weights = jnp.exp(own_scores - peak)
        total = (
            jnp.sum(weights[0], axis=1, keepdims=True)
            + jnp.sum(weights[1], axis=1, keepdims=True)
            + jnp.sum(own_weights, axis=1, keepdims=True)
        )
        scale = 1.0 / total
        attended = jnp.dot(
            (own_weights * scale).astype(jnp.bfloat16),
            new_values,
            preferred_element_type=jnp.float32,
        )
        for p in range(2):
            attended = attended + jnp.dot(
                (weights[p] * scale).astype(jnp.bfloat16),
                values_v[p, :, lanes],
                preferred_element_type=jnp.float32,
            )
        attended = attended.astype(jnp.bfloat16)
        for g in range(group_size):
            attended_v[k, :, g * HD : (g + 1) * HD] = attended[g * ROWS : (g + 1) * ROWS, :]

    second = Gather(gather_o, 1, 1)
    heads.near_ready()
    unpack(half)
    attend(half)
    block(gather_o, node)[...] = attended_v[half]
    heads.far_ready()
    unpack(1 - half)
    attend(1 - half)
    second.cross(attended_v.at[1 - half])
    second.begin(attended_v.at[half])
    heads.sent()

    for m in (mate_y, mate_yz, mate_z):
        w_arrived(m)
        w_over(m)
        w_pass(m, group)
    local[7].wait()
    w_pass(node, 0)
    w_pass(node, 1)
    second.forward()
    w_three(5, 6).wait_recv()
    for m in (mate_y, mate_yz, mate_z):
        w_pass(m, 1 - group)
    w_pass_all().wait_recv()
    shared[4].start()

    def code_of(largest):
        return jnp.ceil(jnp.log2(jnp.maximum(largest, 1e-30)) * CODE_STEPS)

    def encode(values, ref):
        size = values.shape[1]
        code = code_of(jnp.max(jnp.abs(values), axis=1, keepdims=True))
        factor = jnp.exp2(CODE_TOP - code * (1.0 / CODE_STEPS))
        ref[:, 0:size] = jnp.round(values * factor).astype(jnp.int32).astype(jnp.int16)
        ref[:, size : size + 128] = jnp.broadcast_to(
            code.astype(jnp.int32), (values.shape[0], 128)
        ).astype(jnp.int16)

    def decode(ref):
        values = ref[...]
        size = values.shape[1] - 128
        code = values[:, size : size + 1].astype(jnp.int32).astype(jnp.float32)
        factor = jnp.exp2(code * (1.0 / CODE_STEPS) - CODE_TOP)
        return values[:, :size].astype(jnp.int32).astype(jnp.float32) * factor

    def out_project(rows):
        return jnp.dot(gather_o[rows, :], w_cols[...], preferred_element_type=jnp.float32)

    second.near_ready()
    def near_block(ref, m):
        return ref.at[pl.ds(pl.multiple_of(m % QUADS * ROWS, ROWS), ROWS), :]

    def columns_to(m):
        rdma(
            near_block(cols, m),
            near_block(own_cols, node),
            a2a_sem.at[3],
            a2a_sem.at[4],
            device(m),
        ).start()

    def columns_over(m):
        rdma(
            cols_out.at[m % QUADS],
            cols_in.at[quad],
            a2a_sem.at[5],
            a2a_sem.at[8],
            device(m),
        ).start()

    cols[...] = out_project(group_rows(half))
    for m in (mate_y, mate_z, mate_yz):
        columns_to(m)
    near_block(own_cols, node)[...] = near_block(cols, node)[...]
    encode(out_project(mirror_rows), cols_out.at[quad])
    columns_over(mirror)
    second.far_ready()
    cols_far[...] = out_project(group_rows(1 - half))
    for m in ((mate_y + QUADS) % NODES, (mate_yz + QUADS) % NODES, (mate_z + QUADS) % NODES):
        encode(near_block(cols_far, m)[...], cols_out.at[m % QUADS])
        columns_over(m)
    gates_start()
    second.finish()
    w_three(0, 0).wait_send()
    w_three(5, 6).wait_send()
    w_pass_all().wait_send()
    ref = own_cols.at[0 : 3 * ROWS, :]
    rdma(ref, ref, a2a_sem.at[3], a2a_sem.at[4], device(mirror)).wait()
    rdma(cols_out, cols_in, a2a_sem.at[5], a2a_sem.at[8], device(mirror)).wait()
    for q in range(QUADS):
        lanes = slice(q * wide, (q + 1) * wide)
        hidden[:, lanes] = states[:, lanes] + (
            own_cols[q * ROWS : (q + 1) * ROWS, :] + decode(cols_in.at[q])
        )
    block(gather_m, node)[...] = norm_rows(hidden[...], moe_gain[...]).astype(jnp.bfloat16)

    third = Gather(gather_m, 2, 2)
    third.cross(block(gather_m, node))
    third.begin(block(gather_m, node))
    gates_wait()

    all_rows = NODES * ROWS
    all_lane = lax.broadcasted_iota(jnp.int32, (all_rows, 128), 1)

    def gate_up():
        for e in range(2):

            @pl.loop(0, ff // 256)
            def _(t):
                at = pl.multiple_of(t * 256, 256)
                inputs = gather_m[...]
                g = jnp.dot(
                    inputs, gate_up_v[e, :, pl.ds(at, 256)], preferred_element_type=jnp.float32
                )
                u = jnp.dot(
                    inputs,
                    gate_up_v[e, :, pl.ds(pl.multiple_of(ff + t * 256, 256), 256)],
                    preferred_element_type=jnp.float32,
                )
                act[e, :, pl.ds(at, 256)] = (g / (1.0 + jnp.exp(-g)) * u).astype(jnp.bfloat16)

    def part_lanes(part):
        return slice(part * deep, (part + 1) * deep)

    def down(part):
        for t in range(2):
            lanes = slice((2 * part + t) * wide, (2 * part + t + 1) * wide)
            total = jnp.zeros((all_rows, wide), jnp.float32)
            for e in range(2):
                got = jnp.dot(act[e], down_v[e, :, lanes], preferred_element_type=jnp.float32)
                got = got.astype(jnp.bfloat16).astype(jnp.float32)
                total = total + jnp.where(share[e] > 0.0, share[e] * got, 0.0)
            mix[:, lanes] = total

    def encode_far(part):
        for q in range(QUADS):
            rows = pl.ds(pl.multiple_of(((1 - half) * QUADS + q) * ROWS, ROWS), ROWS)
            encode(mix[rows, part_lanes(part)], far_out.at[part, q])

    def encode_near():
        for q in range(QUADS):
            rows = pl.ds(pl.multiple_of((half * QUADS + q) * ROWS, ROWS), ROWS)
            encode(mix[rows, :], near_out.at[q])

    def relay_start(part):
        for m in (mate_y, mate_yz, mate_z):
            rdma(
                far_out.at[part, m % QUADS],
                relay_in.at[part, quad],
                ret_sem.at[0],
                ret_sem.at[1 + part],
                device(m),
            ).start()

    def relay_wait(part):
        ref = relay_in.at[part, 0:3]
        rdma(ref, ref, ret_sem.at[0], ret_sem.at[1 + part], device(mirror)).wait_recv()

    def home_start():
        for m in (mate_y, mate_yz, mate_z):
            rdma(
                near_out.at[m % QUADS],
                near_in.at[quad],
                ret_sem.at[5],
                ret_sem.at[6],
                device(m),
            ).start()

    third.forward()
    third.near_ready()
    gates = gates_all[...]
    share = [
        jnp.sum(jnp.where(all_lane == 2 * node + e, gates, 0.0), axis=1, keepdims=True)
        for e in range(2)
    ]
    third.far_ready()
    for i in (3, 4):
        local[i].wait()
        shared[i].wait_recv()
    gate_up()
    for part in range(2):
        down(part)
        encode_far(part)
        relay_start(part)
    encode_near()
    third.finish()

    def last(part):
        return rdma(
            mirror_out.at[part],
            mirror_in.at[part],
            ret_sem.at[7],
            ret_sem.at[8 + part],
            device(mirror),
        )

    for part in range(2):
        relay_wait(part)
        total = block(mix, mirror)[:, part_lanes(part)]
        for m in mates:
            total = total + decode(relay_in.at[part, m % QUADS])
        encode(total, mirror_out.at[part])
        last(part).start()
        if part == 0:
            home_start()
    ref = near_in.at[0:3]
    rdma(ref, ref, ret_sem.at[5], ret_sem.at[6], device(mirror)).wait()
    total = hidden[...] + block(mix, node)[...]
    for m in mates:
        total = total + decode(near_in.at[m % QUADS])
    hidden[...] = total
    ref = relay_in.at[:, 0:3]
    rdma(ref, ref, ret_sem.at[0], ret_sem.at[0], device(mirror)).wait_send()
    for copy in shared:
        copy.wait_send()
    for part in range(2):
        last(part).wait_recv()
        lanes = part_lanes(part)
        out[:, lanes] = hidden[:, lanes] + decode(mirror_in.at[part])
    rdma(mirror_out, mirror_in, ret_sem.at[7], ret_sem.at[7], device(mirror)).wait_send()


def tuned(
    states,
    attn_gain,
    moe_gain,
    w_query,
    w_key,
    w_value,
    w_output,
    w_gate_up,
    w_down,
    key_cache,
    value_cache,
    cache_lengths,
    prefix_slot,
    routes,
    gate_weights,
):
    step_count, row_count, width = states.shape
    rows = step_count * row_count
    prefix_count, span, kv_width = key_cache.shape
    ff = w_down.shape[1]
    rates = np.tile(THETA ** (-(np.arange(HD // 2) * 2.0 / HD)), 2)
    rates = jnp.asarray(rates.astype(np.float32).reshape(1, HD))
    in_hbm = pl.BlockSpec(memory_space=pl.ANY)
    everyone = NODES * rows
    coded_width = width // QUADS + 128
    bf16, f32, i16 = jnp.bfloat16, jnp.float32, jnp.int16
    out, appended = pl.pallas_call(
        layer_kernel,
        out_shape=(
            pltpu.VMEM((rows, width), f32),
            pltpu.VMEM((rows, 2 * kv_width), bf16),
        ),
        in_specs=[in_hbm] * 16,
        scratch_shapes=[
            pltpu.VMEM((rows, width), f32),
            pltpu.VMEM((1, width), f32),
            pltpu.VMEM((1, width), f32),
            pltpu.VMEM((1, HD), f32),
            pltpu.SMEM(cache_lengths.shape, jnp.int32),
            pltpu.SMEM(prefix_slot.shape, jnp.int32),
            pltpu.VMEM(routes.shape, jnp.int32),
            pltpu.VMEM(gate_weights.shape, f32),
            pltpu.VMEM((width, 256), bf16),
            pltpu.VMEM((64, width), bf16),
            pltpu.VMEM((everyone, 128), f32),
            pltpu.VMEM((everyone, width), bf16),
            pltpu.VMEM((everyone, width // 2), bf16),
            pltpu.VMEM((everyone, width), bf16),
            pltpu.VMEM((2, rows, width // 2), bf16),
            pltpu.VMEM((NODES, 2 * rows + 8, 128), f32),
            pltpu.VMEM((1, 2 * rows + 8, 128), f32),
            pltpu.VMEM((NODES, 2 * rows + 8, 128), f32),
            pltpu.VMEM((width // 2, width // QUADS), bf16),
            pltpu.VMEM((QUADS * rows, width // QUADS), f32),
            pltpu.VMEM((QUADS * rows, width // QUADS), f32),
            pltpu.VMEM((QUADS, rows, coded_width), i16),
            pltpu.VMEM((QUADS, rows, coded_width), i16),
            pltpu.VMEM((QUADS * rows, width // QUADS), f32),
            pltpu.VMEM((rows, width), f32),
            pltpu.VMEM((2, everyone, ff), bf16),
            pltpu.VMEM((everyone, width), f32),
            pltpu.VMEM((QUADS, rows, width + 128), i16),
            pltpu.VMEM((2, QUADS, rows, width // 2 + 128), i16),
            pltpu.VMEM((QUADS, rows, width + 128), i16),
            pltpu.VMEM((2, QUADS, rows, width // 2 + 128), i16),
            pltpu.VMEM((2, rows, width // 2 + 128), i16),
            pltpu.VMEM((2, rows, width // 2 + 128), i16),
            pltpu.VMEM((2, rows, HD), f32),
            pltpu.VMEM((2, rows, HD), f32),
            pltpu.VMEM((2, HQ // 2 * rows, HD), bf16),
            pltpu.VMEM((2, width, 2 * ff), bf16),
            pltpu.VMEM((2, ff, width), bf16),
            pltpu.VMEM((prefix_count, span, kv_width), bf16),
            pltpu.VMEM((prefix_count, span, kv_width), bf16),
            pltpu.SemaphoreType.DMA((8,)),
            pltpu.SemaphoreType.DMA((8,)),
            pltpu.SemaphoreType.DMA((5,)),
            pltpu.SemaphoreType.DMA((5,)),
            pltpu.SemaphoreType.DMA((18,)),
            pltpu.SemaphoreType.DMA((9,)),
            pltpu.SemaphoreType.DMA((9,)),
            pltpu.SemaphoreType.DMA((12,)),
        ],
        compiler_params=pltpu.CompilerParams(
            collective_id=0, has_side_effects=True, vmem_limit_bytes=56 * 1024 * 1024
        ),
    )(
        states.reshape(rows, width),
        attn_gain.reshape(1, width),
        moe_gain.reshape(1, width),
        rates,
        cache_lengths,
        prefix_slot,
        routes,
        gate_weights,
        w_query,
        w_key.T,
        w_value.T,
        w_output,
        w_gate_up[0],
        w_down[0],
        key_cache,
        value_cache,
    )
    return (
        out.reshape(step_count, row_count, width),
        appended.reshape(step_count, row_count, 2 * kv_width),
    )


def solution(mesh):
    return jax.shard_map(
        tuned if mesh.shape["ep"] == TUNED_DEVICES else shards,
        mesh=mesh,
        in_specs=(
            P(None, ("groups", "ep"), None),
            P(),
            P(),
            P(None, "ep"),
            P(None, "ep"),
            P(None, "ep"),
            P("ep", None),
            P("ep", None, None),
            P("ep", None, None),
            P(("groups", "ep"), None, None),
            P(("groups", "ep"), None, None),
            P(("groups", "ep")),
            P(("groups", "ep")),
            P(("groups", "ep"), None, None),
            P(None, ("groups", "ep"), None),
        ),
        out_specs=(P(None, ("groups", "ep"), None), P(None, ("groups", "ep"), None)),
        check_vma=False,
    )
```

```python
import math

import jax
import jax.numpy as jnp
import numpy as np
from jax import lax
from jax.experimental import pallas as pl
from jax.experimental.pallas import tpu as pltpu
from jax.sharding import PartitionSpec as P

HQ = 16
KVH = 2
HD = 128
TOPK = 8


EPS = 1e-06
THETA = 1000000.0


def rms_scale(values, gain):
    squares = jnp.mean(values * values, axis=-1, keepdims=True)
    return values * lax.rsqrt(squares + EPS) * gain


def rotate(vectors, positions):
    head_size = vectors.shape[-1]
    half_size = head_size // 2
    inverse_rate = THETA ** (-(jnp.arange(half_size).astype(jnp.float32) * 2.0 / head_size))
    phases = positions[..., None, None] * inverse_rate
    cosine = jnp.cos(phases)
    sine_part = jnp.sin(phases)
    first_half = vectors[..., :half_size]
    second_half = vectors[..., half_size:]
    return jnp.concatenate(
        [
            first_half * cosine - second_half * sine_part,
            second_half * cosine + first_half * sine_part,
        ],
        axis=-1,
    )


def attend_block(queries, new_keys, new_values, key_block, value_block, lengths, slots):
    step_count, row_count, head_count, head_size = queries.shape
    prefix_count, cache_span, kv_heads, _ = key_block.shape
    group_size = head_count // kv_heads
    grouped = queries.reshape(step_count, row_count, kv_heads, group_size, head_size)
    inv_root = 1.0 / math.sqrt(head_size)
    far_scores = (
        jnp.einsum("srkgd,pckd->srkgpc", grouped, key_block, preferred_element_type=jnp.float32)
        * inv_root
    )
    visible = (jnp.arange(cache_span)[None, None, :] < lengths[None, :, None]) & (
        slots[:, None, None] == jnp.arange(prefix_count)[None, :, None]
    )
    far_scores = jnp.where(visible[None, :, None, None], far_scores, -1e30)
    own_scores = (
        jnp.einsum("srkgd,trkd->srkgt", grouped, new_keys, preferred_element_type=jnp.float32)
        * inv_root
    )
    causal = jnp.arange(step_count)[None, :] <= jnp.arange(step_count)[:, None]
    own_scores = jnp.where(causal[:, None, None, None, :], own_scores, -1e30)
    peak = jnp.maximum(jnp.max(far_scores, axis=(-2, -1)), jnp.max(own_scores, axis=-1))
    far_weights = jnp.exp(far_scores - peak[..., None, None])
    own_weights = jnp.exp(own_scores - peak[..., None])
    normalizer = jnp.sum(far_weights, axis=(-2, -1)) + jnp.sum(own_weights, axis=-1)
    far_probs = (far_weights / normalizer[..., None, None]).astype(jnp.bfloat16)
    own_probs = (own_weights / normalizer[..., None]).astype(jnp.bfloat16)
    attended = jnp.einsum(
        "srkgpc,pckd->srkgd", far_probs, value_block, preferred_element_type=jnp.float32
    )
    attended = attended + jnp.einsum(
        "srkgt,trkd->srkgd", own_probs, new_values, preferred_element_type=jnp.float32
    )
    return attended.reshape(step_count, row_count, head_count * head_size).astype(jnp.bfloat16)


def shards(
    states,
    attn_gain,
    moe_gain,
    w_query,
    w_key,
    w_value,
    w_output,
    w_gate_up,
    w_down,
    key_cache,
    value_cache,
    cache_lengths,
    prefix_slot,
    routes,
    gate_weights,
):
    devices = lax.axis_size("ep")
    step_count, row_count, model_width = states.shape
    query_cols = w_query.shape[1]
    kv_cols = w_key.shape[1]
    normed = rms_scale(states, attn_gain).astype(jnp.bfloat16)
    joined = jnp.concatenate([w_query, w_key, w_value], axis=1)
    head_parts = jnp.einsum(
        "srd,dc->src",
        lax.all_gather(normed, "ep", axis=1, tiled=True),
        joined,
        preferred_element_type=jnp.float32,
    )
    own_cols = lax.all_to_all(head_parts, "ep", split_axis=1, concat_axis=2, tiled=True)
    own_cols = own_cols.reshape(step_count, row_count, devices, query_cols + 2 * kv_cols)
    queries = own_cols[..., :query_cols].reshape(step_count, row_count, HQ, HD)
    new_keys = own_cols[..., query_cols : query_cols + kv_cols].reshape(
        step_count, row_count, KVH, HD
    )
    new_values = (
        own_cols[..., query_cols + kv_cols :]
        .reshape(step_count, row_count, KVH, HD)
        .astype(jnp.bfloat16)
    )
    prefix_count, cache_span, _ = key_cache.shape
    lengths_here = jnp.sum(
        jnp.where(
            prefix_slot[:, None] == jnp.arange(prefix_count)[None, :], cache_lengths[None, :], 0
        ),
        axis=1,
    )
    positions = (
        lengths_here.astype(jnp.float32)[None, :]
        + jnp.arange(step_count).astype(jnp.float32)[:, None]
    )
    queries = rotate(queries, positions).astype(jnp.bfloat16)
    new_keys = rotate(new_keys, positions).astype(jnp.bfloat16)
    attended = attend_block(
        queries,
        new_keys,
        new_values,
        key_cache.reshape(prefix_count, cache_span, KVH, HD),
        value_cache.reshape(prefix_count, cache_span, KVH, HD),
        cache_lengths,
        prefix_slot,
    )
    w_columns = lax.all_to_all(w_output, "ep", split_axis=1, concat_axis=0, tiled=True)
    column_part = jnp.einsum(
        "srf,fc->src",
        lax.all_gather(attended, "ep", axis=1, tiled=True),
        w_columns,
        preferred_element_type=jnp.float32,
    )
    projected = lax.all_to_all(column_part, "ep", split_axis=1, concat_axis=2, tiled=True)
    hidden = states + projected
    moe_input = (
        rms_scale(hidden, moe_gain)
        .astype(jnp.bfloat16)
        .reshape(step_count * row_count, model_width)
    )
    expert_count = w_gate_up.shape[0] * devices
    capacity = max(2, 4 * row_count * TOPK // expert_count)
    flat_routes = jnp.swapaxes(routes, 0, 1).reshape(-1)
    order = jnp.arange(flat_routes.shape[0])
    earlier = (flat_routes[:, None] == flat_routes[None, :]) & (order[None, :] < order[:, None])
    within = jnp.sum(earlier.astype(jnp.int32), axis=1)
    slot_index = flat_routes * capacity + within
    dispatch = (jnp.arange(expert_count * capacity)[:, None] == slot_index[None, :]).astype(
        jnp.bfloat16
    )
    repeated = jnp.repeat(moe_input, TOPK, axis=0)
    outgoing = jnp.dot(dispatch, repeated, preferred_element_type=jnp.float32).astype(jnp.bfloat16)
    outgoing = outgoing.reshape(expert_count, capacity, model_width)
    both = jnp.einsum(
        "nsd,df->nsf",
        lax.all_to_all(outgoing, "ep", split_axis=0, concat_axis=0, tiled=True),
        w_gate_up[0],
        preferred_element_type=jnp.float32,
    )
    half_cols = both.shape[-1] // 2
    activation = (jax.nn.silu(both[..., :half_cols]) * both[..., half_cols:]).astype(jnp.bfloat16)
    expert_done = jnp.einsum(
        "nsf,fd->nsd", activation, w_down[0], preferred_element_type=jnp.float32
    ).astype(jnp.bfloat16)
    returned = lax.all_to_all(expert_done, "ep", split_axis=0, concat_axis=0, tiled=True)
    picked = returned.reshape(expert_count * capacity, model_width)[slot_index]
    picked = picked.astype(jnp.float32).reshape(step_count, row_count, TOPK, model_width)
    mixture = jnp.sum(gate_weights[..., None] * picked, axis=2)
    appended = jnp.concatenate(
        [
            new_keys.reshape(step_count, row_count, KVH * HD),
            new_values.reshape(step_count, row_count, KVH * HD),
        ],
        axis=-1,
    )
    return (hidden + mixture, appended)


TUNED_DEVICES = 16
ROWS = 16
NODES = 8
QUADS = 4
CODE_TOP = 14.99
CODE_STEPS = 256.0


def norm_rows(values, gain):
    squares = jnp.mean(values * values, axis=-1, keepdims=True)
    return values * lax.rsqrt(squares + EPS) * gain


def layer_kernel(
    states_in,
    attn_gain_in,
    moe_gain_in,
    rates_in,
    lengths_in,
    slots_in,
    routes_in,
    gate_weights_in,
    w_query,
    w_key,
    w_value,
    w_output,
    w_gate_up,
    w_down,
    key_cache,
    value_cache,
    out,
    appended,
    states,
    attn_gain,
    moe_gain,
    rates,
    lengths,
    slots,
    routes,
    gate_weights,
    w_query_v,
    w_kv_v,
    gates_all,
    gather_q,
    gather_o,
    gather_m,
    attended_v,
    parts,
    parts_m,
    own_parts,
    w_cols,
    cols,
    cols_far,
    cols_out,
    cols_in,
    own_cols,
    hidden,
    act,
    mix,
    near_out,
    far_out,
    near_in,
    relay_in,
    mirror_out,
    mirror_in,
    fresh_k,
    fresh_v,
    queries,
    gate_up_v,
    down_v,
    keys_v,
    values_v,
    small_sem,
    load_sem,
    twin_send,
    twin_recv,
    ag_sem,
    a2a_sem,
    w_sem,
    ret_sem,
):
    me = lax.axis_index("ep")
    c = me % 2
    node = me // 2
    half = node // QUADS
    quad = node % QUADS
    twin = me + 1 - 2 * c
    group = lax.axis_index("groups")
    twin_group = {"groups": 1 - group, "ep": me}
    width = states.shape[1]
    wide = width // QUADS
    deep = width // 2
    ff = down_v.shape[1]

    def device(m):
        return m * 2 + c

    mate_y = node + 1 - 2 * (node % 2)
    mate_z = node + 2 - 4 * (quad // 2)
    mate_yz = mate_z + mate_y - node
    mates = [mate_y, mate_yz, mate_z]
    mirror = (node + QUADS) % NODES
    across = [mirror] + [(m + QUADS) % NODES for m in mates]

    def block(ref, m):
        return ref.at[pl.ds(pl.multiple_of(m * ROWS, ROWS), ROWS), :]

    def rdma(src, dst, send, recv, target):
        return pltpu.make_async_remote_copy(
            src_ref=src,
            dst_ref=dst,
            send_sem=send,
            recv_sem=recv,
            device_id=target if isinstance(target, dict) else {"ep": target},
            device_id_type=pl.DeviceIdType.MESH,
        )

    barrier = pltpu.get_barrier_semaphore()
    partners = [{"ep": device((node + i) % NODES)} for i in range(1, NODES)]
    for target in partners + [{"ep": twin}, twin_group]:
        pl.semaphore_signal(
            barrier,
            inc=1,
            device_id=target,
            device_id_type=pl.DeviceIdType.MESH,
        )

    small = [
        pltpu.make_async_copy(s, d, small_sem.at[i])
        for i, (s, d) in enumerate(
            (
                (states_in, states),
                (attn_gain_in, attn_gain),
                (lengths_in, lengths),
                (slots_in, slots),
                (rates_in, rates),
                (routes_in, routes),
                (gate_weights_in, gate_weights),
                (moe_gain_in, moe_gain),
            )
        )
    ]
    for copy in small:
        copy.start()

    def lanes_of(index, size):
        return pl.ds(pl.multiple_of(index * size, size), size)

    def twin_pairs():
        return [
            (w_query, w_query_v.at[:, lanes_of(c, 128)]),
            (w_key, w_kv_v.at[pl.ds(pl.multiple_of(c * 16, 16), 16), :]),
            (w_value, w_kv_v.at[pl.ds(pl.multiple_of(32 + c * 16, 16), 16), :]),
            (w_gate_up, gate_up_v.at[c]),
            (w_down, down_v.at[c]),
        ]

    local = [pltpu.make_async_copy(s, d, load_sem.at[i]) for i, (s, d) in enumerate(twin_pairs())]
    shared = [
        rdma(s, d, twin_send.at[i], twin_recv.at[i], twin) for i, (s, d) in enumerate(twin_pairs())
    ]
    w_rows = pl.ds(pl.multiple_of((2 * quad + c) * 128, 128), 128)
    local += [
        pltpu.make_async_copy(key_cache, keys_v, load_sem.at[5]),
        pltpu.make_async_copy(value_cache, values_v, load_sem.at[6]),
        pltpu.make_async_copy(
            w_output.at[:, lanes_of(quad, wide)], w_cols.at[w_rows, :], load_sem.at[7]
        ),
    ]
    for i in (0, 1, 2, 5, 6, 7, 3, 4):
        local[i].start()

    class Gather:
        def __init__(self, buf, phase, chunks):
            self.buf, self.phase, self.chunks = buf, phase, chunks
            self.size = buf.shape[1] // chunks
            self.send = ag_sem.at[6 * phase]

        def lanes(self, part):
            if part == 0:
                return slice(None)
            return slice((part - 1) % 2 * self.size, ((part - 1) % 2 + 1) * self.size)

        def piece(self, m, part):
            return self.buf.at[pl.ds(pl.multiple_of(m * ROWS, ROWS), ROWS), self.lanes(part)]

        def push(self, src, m, part, target):
            landed = ag_sem.at[6 * self.phase + 1 + part]
            rdma(src, self.piece(m, part), self.send, landed, device(target)).start()

        def arrived(self, part, count):
            ref = self.buf.at[0 : count * ROWS, self.lanes(part)]
            landed = ag_sem.at[6 * self.phase + 1 + part]
            rdma(ref, ref, self.send, landed, device(mirror)).wait_recv()

        def cross(self, source):
            for part in range(1, 1 + self.chunks):
                self.push(source.at[:, self.lanes(part)], node, part, mirror)

        def begin(self, source):
            for m in (mate_y, mate_yz, mate_z):
                self.push(source, node, 0, m)

        def forward(self):
            for part in range(1, 1 + self.chunks):
                self.arrived(part, 1)
                for m in (mate_y, mate_yz, mate_z):
                    self.push(self.piece(mirror, part), mirror, part + 2, m)

        def near_ready(self):
            self.arrived(0, QUADS - 1)

        def far_ready(self):
            for part in range(3, 3 + self.chunks):
                self.arrived(part, QUADS - 1)

        def finish(self):
            ref = self.buf.at[0 : 7 * ROWS, :]
            rdma(ref, ref, self.send, self.send, device(mirror)).wait_send()

    class Scatter:
        def __init__(self, src, mirror_src, dst, phase):
            self.src, self.mirror_src, self.dst = src, mirror_src, dst
            self.send = a2a_sem.at[3 * phase]
            self.near, self.far = a2a_sem.at[3 * phase + 1], a2a_sem.at[3 * phase + 2]

        def pick(self, ref, m):
            return ref.at[m] if len(ref.shape) == 3 else block(ref, m)

        def push(self, src, m, recv):
            rdma(src, self.pick(self.dst, node), self.send, recv, device(m)).start()

        def to_mates(self):
            for m in (mate_yz, mate_y, mate_z):
                self.push(self.pick(self.src, m), m, self.near)

        def to_mirror(self):
            self.push(self.mirror_src, mirror, self.far)

        def to_far(self):
            for m in ((mate_y + QUADS) % NODES, (mate_yz + QUADS) % NODES, (mate_z + QUADS) % NODES):
                self.push(self.pick(self.src, m), m, self.far)

        def some(self, ref, count):
            return ref.at[0 : count if len(ref.shape) == 3 else count * ROWS]

        def near_ready(self):
            dst = self.some(self.dst, 3)
            rdma(dst, dst, self.send, self.near, device(mirror)).wait_recv()

        def far_ready(self):
            dst = self.some(self.dst, 4)
            rdma(dst, dst, self.send, self.far, device(mirror)).wait_recv()

        def sent(self):
            src = self.some(self.src, 7)
            rdma(src, src, self.send, self.far, device(mirror)).wait_send()

    others = mates + across

    small[0].wait()
    small[1].wait()
    block(gather_q, node)[...] = norm_rows(states[...], attn_gain[...]).astype(jnp.bfloat16)
    pl.semaphore_wait(barrier, NODES + 1)

    first = Gather(gather_q, 0, 2)
    first.cross(block(gather_q, node))
    first.begin(block(gather_q, node))
    for i in (0, 1, 2, 3):
        shared[i].start()

    def group_rows(group):
        return pl.ds(pl.multiple_of(group * 64, 64), 64)

    def project(rows, count):
        inputs = gather_q[rows, :]
        q = jnp.dot(inputs, w_query_v[...], preferred_element_type=jnp.float32)
        kv = lax.dot_general(
            inputs, w_kv_v[...], (((1,), (1,)), ((), ())), preferred_element_type=jnp.float32
        )
        kv = kv.reshape(count, ROWS, 64)
        kv = jnp.concatenate([kv[:, 0:8, :], kv[:, 8:16, :]], axis=-1)
        q = [q[:, 128 * i : 128 * i + 128].reshape(count, ROWS, 128) for i in range(2)]
        return jnp.concatenate(q + [kv], axis=1)

    def project_group(group):
        parts[pl.ds(group * QUADS, QUADS)] = project(group_rows(group), QUADS)

    mirror_rows = pl.ds(pl.multiple_of(mirror * ROWS, ROWS), ROWS)

    slim = wide // 2

    def w_piece(q, core, part):
        rows = pl.ds(pl.multiple_of((2 * q + core) * 128, 128), 128)
        return w_cols.at[rows, lanes_of(part, slim)]

    def w_start():
        for m in (mate_y, mate_z, mate_yz):
            at = pl.multiple_of(m % QUADS * wide + group * slim, slim)
            rdma(
                w_output.at[:, pl.ds(at, slim)],
                w_piece(quad, c, group),
                w_sem.at[0],
                w_sem.at[1 + quad],
                device(m),
            ).start()

    def w_arrived(m):
        piece = w_piece(m % QUADS, c, group)
        rdma(piece, piece, w_sem.at[0], w_sem.at[1 + m % QUADS], device(m)).wait_recv()

    def w_over(m):
        piece = w_piece(m % QUADS, c, group)
        rdma(piece, piece, w_sem.at[5], w_sem.at[6], twin_group).start()

    def w_three(send, recv):
        ref = w_cols.at[0:384, 0:slim]
        return rdma(ref, ref, w_sem.at[send], w_sem.at[recv], twin_group)

    def w_pass(m, part):
        piece = w_piece(m % QUADS, c, part)
        rdma(piece, piece, w_sem.at[7], w_sem.at[8], twin).start()

    def w_pass_all():
        ref = w_cols.at[0:512, :]
        return rdma(ref, ref, w_sem.at[7], w_sem.at[8], twin)

    def gates_start():
        mine = block(gates_all, node)
        for m in others:
            rdma(mine, mine, a2a_sem.at[6], a2a_sem.at[7], device(m)).start()

    def gates_wait():
        ref = gates_all.at[0 : 7 * ROWS, :]
        rdma(ref, ref, a2a_sem.at[6], a2a_sem.at[7], device(mirror)).wait()

    first.forward()
    for i in (0, 1, 2):
        local[i].wait()
        shared[i].wait_recv()
    first.near_ready()
    project_group(half)
    heads = Scatter(parts, parts_m.at[0], own_parts, 0)
    heads.to_mates()
    own_parts[node] = parts[node]
    parts_m[...] = project(mirror_rows, 1)
    heads.to_mirror()

    for copy in small[2:]:
        copy.wait()
    row_id = lax.broadcasted_iota(jnp.int32, (ROWS, 128), 0)
    lane_id = lax.broadcasted_iota(jnp.int32, (ROWS, 128), 1)
    chosen = jnp.concatenate([routes[:, 0, :], routes[:, 1, :]], axis=0)
    shares = jnp.concatenate([gate_weights[0], gate_weights[1]], axis=0)
    weighed = jnp.zeros((ROWS, 128), jnp.float32)
    for k in range(TOPK):
        weighed = jnp.where(lane_id == chosen[:, k : k + 1], shares[:, k : k + 1], weighed)
    block(gates_all, node)[...] = weighed
    slot_of = jnp.zeros((ROWS, 128), jnp.int32)
    for b in range(8):
        slot_of = jnp.where(row_id % 8 == b, slots[b], slot_of)
    limits = [jnp.where(slot_of == p, lengths[p], 0) for p in range(2)]
    phases = (limits[0] + limits[1] + row_id // 8).astype(jnp.float32) * rates[...]
    cosine = jnp.cos(phases)
    sine = jnp.sin(phases)
    sine = jnp.where(lane_id < 64, -sine, sine)

    first.far_ready()
    project_group(1 - half)
    heads.to_far()
    w_start()
    first.finish()

    def turned(vectors):
        return vectors * cosine + pltpu.roll(vectors, 64, 1) * sine

    def unpack(k):
        for q in range(QUADS):
            j = k * QUADS + q
            for i in range(2):
                at = (2 * q + i) * ROWS
                queries[k, at : at + ROWS, :] = turned(
                    own_parts[j, i * ROWS : (i + 1) * ROWS, :]
                ).astype(jnp.bfloat16)
            packed = own_parts[j, 2 * ROWS : 2 * ROWS + 8, :]
            unpacked = jnp.concatenate([packed[:, 0:64], packed[:, 64:128]], axis=0)
            fresh_k[k, :, q * 32 : (q + 1) * 32] = unpacked[:, 0:32]
            fresh_v[k, :, q * 32 : (q + 1) * 32] = unpacked[:, 32:64]

    local[5].wait()
    local[6].wait()
    inv_root = 1.0 / math.sqrt(HD)
    group_size = HQ // KVH
    q_rows = group_size * ROWS
    span = keys_v.shape[1]
    far_pos = lax.broadcasted_iota(jnp.int32, (q_rows, span), 1)
    row_at = lax.broadcasted_iota(jnp.int32, (q_rows, ROWS), 0) % ROWS
    col_at = lax.broadcasted_iota(jnp.int32, (q_rows, ROWS), 1)
    own_seen = (row_at % 8 == col_at % 8) & (col_at // 8 <= row_at // 8)
    limits = [jnp.concatenate([m[:, 0:1]] * group_size, axis=0) for m in limits]

    def attend(k):
        lanes = lanes_of(k, HD)
        new_keys = turned(fresh_k[k]).astype(jnp.bfloat16)
        new_values = fresh_v[k].astype(jnp.bfloat16)
        appended[:, lanes] = new_keys
        appended[:, lanes_of(KVH + k, HD)] = new_values
        q = queries[k]

        def against(rows):
            return (
                lax.dot_general(
                    q, rows, (((1,), (1,)), ((), ())), preferred_element_type=jnp.float32
                )
                * inv_root
            )

        scores = [
            jnp.where(far_pos < limits[p], against(keys_v[p, :, lanes]), -1e30) for p in range(2)
        ]
        own_scores = jnp.where(own_seen, against(new_keys), -1e30)
        peak = jnp.maximum(
            jnp.maximum(
                jnp.max(scores[0], axis=1, keepdims=True), jnp.max(scores[1], axis=1, keepdims=True)
            ),
            jnp.max(own_scores, axis=1, keepdims=True),
        )
        weights = [jnp.exp(s - peak) for s in scores]
        own_weights = jnp.exp(own_scores - peak)
        total = (
            jnp.sum(weights[0], axis=1, keepdims=True)
            + jnp.sum(weights[1], axis=1, keepdims=True)
            + jnp.sum(own_weights, axis=1, keepdims=True)
        )
        scale = 1.0 / total
        attended = jnp.dot(
            (own_weights * scale).astype(jnp.bfloat16),
            new_values,
            preferred_element_type=jnp.float32,
        )
        for p in range(2):
            attended = attended + jnp.dot(
                (weights[p] * scale).astype(jnp.bfloat16),
                values_v[p, :, lanes],
                preferred_element_type=jnp.float32,
            )
        attended = attended.astype(jnp.bfloat16)
        for g in range(group_size):
            attended_v[k, :, g * HD : (g + 1) * HD] = attended[g * ROWS : (g + 1) * ROWS, :]

    second = Gather(gather_o, 1, 1)
    heads.near_ready()
    unpack(half)
    attend(half)
    block(gather_o, node)[...] = attended_v[half]
    heads.far_ready()
    unpack(1 - half)
    attend(1 - half)
    second.cross(attended_v.at[1 - half])
    second.begin(attended_v.at[half])
    heads.sent()

    for m in (mate_y, mate_yz, mate_z):
        w_arrived(m)
        w_over(m)
        w_pass(m, group)
    local[7].wait()
    w_pass(node, 0)
    w_pass(node, 1)
    second.forward()
    w_three(5, 6).wait_recv()
    for m in (mate_y, mate_yz, mate_z):
        w_pass(m, 1 - group)
    w_pass_all().wait_recv()
    shared[4].start()

    def code_of(largest):
        return jnp.ceil(jnp.log2(jnp.maximum(largest, 1e-30)) * CODE_STEPS)

    def encode(values, ref):
        size = values.shape[1]
        code = code_of(jnp.max(jnp.abs(values), axis=1, keepdims=True))
        factor = jnp.exp2(CODE_TOP - code * (1.0 / CODE_STEPS))
        ref[:, 0:size] = jnp.round(values * factor).astype(jnp.int32).astype(jnp.int16)
        ref[:, size : size + 128] = jnp.broadcast_to(
            code.astype(jnp.int32), (values.shape[0], 128)
        ).astype(jnp.int16)

    def decode(ref):
        values = ref[...]
        size = values.shape[1] - 128
        code = values[:, size : size + 1].astype(jnp.int32).astype(jnp.float32)
        factor = jnp.exp2(code * (1.0 / CODE_STEPS) - CODE_TOP)
        return values[:, :size].astype(jnp.int32).astype(jnp.float32) * factor

    def out_project(rows):
        return jnp.dot(gather_o[rows, :], w_cols[...], preferred_element_type=jnp.float32)

    second.near_ready()
    def near_block(ref, m):
        return ref.at[pl.ds(pl.multiple_of(m % QUADS * ROWS, ROWS), ROWS), :]

    def columns_to(m):
        rdma(
            near_block(cols, m),
            near_block(own_cols, node),
            a2a_sem.at[3],
            a2a_sem.at[4],
            device(m),
        ).start()

    def columns_over(m):
        rdma(
            cols_out.at[m % QUADS],
            cols_in.at[quad],
            a2a_sem.at[5],
            a2a_sem.at[8],
            device(m),
        ).start()

    cols[...] = out_project(group_rows(half))
    for m in (mate_y, mate_z, mate_yz):
        columns_to(m)
    near_block(own_cols, node)[...] = near_block(cols, node)[...]
    encode(out_project(mirror_rows), cols_out.at[quad])
    columns_over(mirror)
    second.far_ready()
    cols_far[...] = out_project(group_rows(1 - half))
    for m in ((mate_y + QUADS) % NODES, (mate_yz + QUADS) % NODES, (mate_z + QUADS) % NODES):
        encode(near_block(cols_far, m)[...], cols_out.at[m % QUADS])
        columns_over(m)
    gates_start()
    second.finish()
    w_three(0, 0).wait_send()
    w_three(5, 6).wait_send()
    w_pass_all().wait_send()
    ref = own_cols.at[0 : 3 * ROWS, :]
    rdma(ref, ref, a2a_sem.at[3], a2a_sem.at[4], device(mirror)).wait()
    rdma(cols_out, cols_in, a2a_sem.at[5], a2a_sem.at[8], device(mirror)).wait()
    for q in range(QUADS):
        lanes = slice(q * wide, (q + 1) * wide)
        hidden[:, lanes] = states[:, lanes] + (
            own_cols[q * ROWS : (q + 1) * ROWS, :] + decode(cols_in.at[q])
        )
    block(gather_m, node)[...] = norm_rows(hidden[...], moe_gain[...]).astype(jnp.bfloat16)

    third = Gather(gather_m, 2, 2)
    third.cross(block(gather_m, node))
    third.begin(block(gather_m, node))
    gates_wait()

    all_rows = NODES * ROWS
    all_lane = lax.broadcasted_iota(jnp.int32, (all_rows, 128), 1)

    def gate_up():
        for e in range(2):

            @pl.loop(0, ff // 256)
            def _(t):
                at = pl.multiple_of(t * 256, 256)
                inputs = gather_m[...]
                g = jnp.dot(
                    inputs, gate_up_v[e, :, pl.ds(at, 256)], preferred_element_type=jnp.float32
                )
                u = jnp.dot(
                    inputs,
                    gate_up_v[e, :, pl.ds(pl.multiple_of(ff + t * 256, 256), 256)],
                    preferred_element_type=jnp.float32,
                )
                act[e, :, pl.ds(at, 256)] = (g / (1.0 + jnp.exp(-g)) * u).astype(jnp.bfloat16)

    def part_lanes(part):
        return slice(part * deep, (part + 1) * deep)

    def down(part):
        for t in range(2):
            lanes = slice((2 * part + t) * wide, (2 * part + t + 1) * wide)
            total = jnp.zeros((all_rows, wide), jnp.float32)
            for e in range(2):
                got = jnp.dot(act[e], down_v[e, :, lanes], preferred_element_type=jnp.float32)
                got = got.astype(jnp.bfloat16).astype(jnp.float32)
                total = total + jnp.where(share[e] > 0.0, share[e] * got, 0.0)
            mix[:, lanes] = total

    def encode_far(part):
        for m in mates:
            far = block(mix, (m + QUADS) % NODES)
            encode(far[:, part_lanes(part)], far_out.at[part, m % QUADS])

    def encode_near():
        for m in mates:
            encode(block(mix, m)[...], near_out.at[m % QUADS])

    def relay_start(part):
        for m in (mate_y, mate_yz, mate_z):
            rdma(
                far_out.at[part, m % QUADS],
                relay_in.at[part, quad],
                ret_sem.at[0],
                ret_sem.at[1 + part],
                device(m),
            ).start()

    def relay_wait(part):
        ref = relay_in.at[part, 0:3]
        rdma(ref, ref, ret_sem.at[0], ret_sem.at[1 + part], device(mirror)).wait_recv()

    def home_start():
        for m in (mate_yz, mate_y, mate_z):
            rdma(
                near_out.at[m % QUADS],
                near_in.at[quad],
                ret_sem.at[5],
                ret_sem.at[6],
                device(m),
            ).start()

    third.forward()
    third.near_ready()
    gates = gates_all[...]
    share = [
        jnp.sum(jnp.where(all_lane == 2 * node + e, gates, 0.0), axis=1, keepdims=True)
        for e in range(2)
    ]
    third.far_ready()
    for i in (3, 4):
        local[i].wait()
        shared[i].wait_recv()
    gate_up()
    for part in range(2):
        down(part)
        encode_far(part)
        relay_start(part)
    encode_near()
    third.finish()

    def last(part):
        return rdma(
            mirror_out.at[part],
            mirror_in.at[part],
            ret_sem.at[7],
            ret_sem.at[8 + part],
            device(mirror),
        )

    for part in range(2):
        relay_wait(part)
        total = block(mix, mirror)[:, part_lanes(part)]
        for m in mates:
            total = total + decode(relay_in.at[part, m % QUADS])
        encode(total, mirror_out.at[part])
        last(part).start()
        if part == 0:
            home_start()
    ref = near_in.at[0:3]
    rdma(ref, ref, ret_sem.at[5], ret_sem.at[6], device(mirror)).wait()
    total = hidden[...] + block(mix, node)[...]
    for m in mates:
        total = total + decode(near_in.at[m % QUADS])
    hidden[...] = total
    ref = relay_in.at[:, 0:3]
    rdma(ref, ref, ret_sem.at[0], ret_sem.at[0], device(mirror)).wait_send()
    for copy in shared:
        copy.wait_send()
    for part in range(2):
        last(part).wait_recv()
        lanes = part_lanes(part)
        out[:, lanes] = hidden[:, lanes] + decode(mirror_in.at[part])
    rdma(mirror_out, mirror_in, ret_sem.at[7], ret_sem.at[7], device(mirror)).wait_send()


def tuned(
    states,
    attn_gain,
    moe_gain,
    w_query,
    w_key,
    w_value,
    w_output,
    w_gate_up,
    w_down,
    key_cache,
    value_cache,
    cache_lengths,
    prefix_slot,
    routes,
    gate_weights,
):
    step_count, row_count, width = states.shape
    rows = step_count * row_count
    prefix_count, span, kv_width = key_cache.shape
    ff = w_down.shape[1]
    rates = np.tile(THETA ** (-(np.arange(HD // 2) * 2.0 / HD)), 2)
    rates = jnp.asarray(rates.astype(np.float32).reshape(1, HD))
    in_hbm = pl.BlockSpec(memory_space=pl.ANY)
    everyone = NODES * rows
    coded_width = width // QUADS + 128
    bf16, f32, i16 = jnp.bfloat16, jnp.float32, jnp.int16
    out, appended = pl.pallas_call(
        layer_kernel,
        out_shape=(
            pltpu.VMEM((rows, width), f32),
            pltpu.VMEM((rows, 2 * kv_width), bf16),
        ),
        in_specs=[in_hbm] * 16,
        scratch_shapes=[
            pltpu.VMEM((rows, width), f32),
            pltpu.VMEM((1, width), f32),
            pltpu.VMEM((1, width), f32),
            pltpu.VMEM((1, HD), f32),
            pltpu.SMEM(cache_lengths.shape, jnp.int32),
            pltpu.SMEM(prefix_slot.shape, jnp.int32),
            pltpu.VMEM(routes.shape, jnp.int32),
            pltpu.VMEM(gate_weights.shape, f32),
            pltpu.VMEM((width, 256), bf16),
            pltpu.VMEM((64, width), bf16),
            pltpu.VMEM((everyone, 128), f32),
            pltpu.VMEM((everyone, width), bf16),
            pltpu.VMEM((everyone, width // 2), bf16),
            pltpu.VMEM((everyone, width), bf16),
            pltpu.VMEM((2, rows, width // 2), bf16),
            pltpu.VMEM((NODES, 2 * rows + 8, 128), f32),
            pltpu.VMEM((1, 2 * rows + 8, 128), f32),
            pltpu.VMEM((NODES, 2 * rows + 8, 128), f32),
            pltpu.VMEM((width // 2, width // QUADS), bf16),
            pltpu.VMEM((QUADS * rows, width // QUADS), f32),
            pltpu.VMEM((QUADS * rows, width // QUADS), f32),
            pltpu.VMEM((QUADS, rows, coded_width), i16),
            pltpu.VMEM((QUADS, rows, coded_width), i16),
            pltpu.VMEM((QUADS * rows, width // QUADS), f32),
            pltpu.VMEM((rows, width), f32),
            pltpu.VMEM((2, everyone, ff), bf16),
            pltpu.VMEM((everyone, width), f32),
            pltpu.VMEM((QUADS, rows, width + 128), i16),
            pltpu.VMEM((2, QUADS, rows, width // 2 + 128), i16),
            pltpu.VMEM((QUADS, rows, width + 128), i16),
            pltpu.VMEM((2, QUADS, rows, width // 2 + 128), i16),
            pltpu.VMEM((2, rows, width // 2 + 128), i16),
            pltpu.VMEM((2, rows, width // 2 + 128), i16),
            pltpu.VMEM((2, rows, HD), f32),
            pltpu.VMEM((2, rows, HD), f32),
            pltpu.VMEM((2, HQ // 2 * rows, HD), bf16),
            pltpu.VMEM((2, width, 2 * ff), bf16),
            pltpu.VMEM((2, ff, width), bf16),
            pltpu.VMEM((prefix_count, span, kv_width), bf16),
            pltpu.VMEM((prefix_count, span, kv_width), bf16),
            pltpu.SemaphoreType.DMA((8,)),
            pltpu.SemaphoreType.DMA((8,)),
            pltpu.SemaphoreType.DMA((5,)),
            pltpu.SemaphoreType.DMA((5,)),
            pltpu.SemaphoreType.DMA((18,)),
            pltpu.SemaphoreType.DMA((9,)),
            pltpu.SemaphoreType.DMA((9,)),
            pltpu.SemaphoreType.DMA((12,)),
        ],
        compiler_params=pltpu.CompilerParams(
            collective_id=0, has_side_effects=True, vmem_limit_bytes=56 * 1024 * 1024
        ),
    )(
        states.reshape(rows, width),
        attn_gain.reshape(1, width),
        moe_gain.reshape(1, width),
        rates,
        cache_lengths,
        prefix_slot,
        routes,
        gate_weights,
        w_query,
        w_key.T,
        w_value.T,
        w_output,
        w_gate_up[0],
        w_down[0],
        key_cache,
        value_cache,
    )
    return (
        out.reshape(step_count, row_count, width),
        appended.reshape(step_count, row_count, 2 * kv_width),
    )


def solution(mesh):
    return jax.shard_map(
        tuned if mesh.shape["ep"] == TUNED_DEVICES else shards,
        mesh=mesh,
        in_specs=(
            P(None, ("groups", "ep"), None),
            P(),
            P(),
            P(None, "ep"),
            P(None, "ep"),
            P(None, "ep"),
            P("ep", None),
            P("ep", None, None),
            P("ep", None, None),
            P(("groups", "ep"), None, None),
            P(("groups", "ep"), None, None),
            P(("groups", "ep")),
            P(("groups", "ep")),
            P(("groups", "ep"), None, None),
            P(None, ("groups", "ep"), None),
        ),
        out_specs=(P(None, ("groups", "ep"), None), P(None, ("groups", "ep"), None)),
        check_vma=False,
    )
```
